32 devices in a mesh: sections: 4 (over y, x), cache: 4 (over z), heads: 2 (over core).
Axes of the slice: x: 2, y: 2, z: 4, core: 2. Of those that a mesh axis runs over, the one named last changes fastest.
Arguments:
- hidden: bfloat16 [4, 1024, 2048], P('sections', 'cache'), may hold values from -6 to 6
- norm_gain: float32 [4, 2048], P('sections'), may hold values from 0.1 to 1.9
- w_query: bfloat16 [4, 2048, 4096], P('sections', None, 'heads'), may hold values from -0.125 to 0.125
- query_gain: float32 [4, 128], P('sections'), may hold values from 0.1 to 1.9
- w_output: bfloat16 [4, 4096, 2048], P('sections', 'heads'), may hold values from -0.09375 to 0.09375
- key_cache: bfloat16 [4, 128, 64, 512], P('sections', 'cache', None, 'heads'), may hold values from -6 to 6
- value_cache: bfloat16 [4, 128, 64, 512], P('sections', 'cache', None, 'heads'), may hold values from -6 to 6
- key_scale: float32 [4, 128, 4], P('sections', 'cache', 'heads'), may hold values from 0.5 to 120
- value_scale: float32 [4, 128, 4], P('sections', 'cache', 'heads'), may hold values from 0.5 to 2
- page_table: int32 [128], replicated, may hold values from 0 to 127, as said below
- page_tokens: int32 [128], replicated, may hold values from 1 to 64
- page_list: int32 [4, 8, 16], P('sections'), may hold values from 0 to 127, as said below
- list_len: int32 [4, 8], P('sections'), may hold values from 8 to 16, as said below
Outputs:
- mixed: bfloat16 [4, 1024, 2048], P('sections', 'cache', 'heads')
The draws below stay inside these ranges and needn't reach their ends.
Inputs may be any that keep to these rules, and one draw needn't show every extreme that they name: `page_table`: A permutation of the 128 slots; slot // 32 is the cache index that holds the page. `page_list`: the 16 entries of a block are distinct logical pages; among them at most 8 have their slot on any one cache index, and in every block some cache index holds exactly 8 of them. Entries of a list from list_len on are unused; some block uses all 16 entries.
All inputs are finite; a program needn't handle non-finite values.
Results may differ from the reference program's by a relative error of at most 0.008.
The reference program's roundings to bfloat16 on the way (of `normed`, `queries`, `scaled`, `attended` and `updated`) count: a program that leaves them out, or rounds other values in their place, can miss the bound.
Values may be sent and summed in bfloat16 or wider, within the bound.
A program may use at most 128 MiB of HBM per device.

```python
import math
import jax
import jax.numpy as jnp
from jax import lax

D = 2048
Q_HEADS = 32
KV_HEADS = 4
HEAD_DIM = 128
QBLOCK = 128
PAGE = 64
PAGES_DEV = 32
MOST = 8
LIST = 16
PAGES = 128
BLOCKS = 8
ROWS = 1024
N_SECTIONS = 4
N_CACHE = 4


def page_layout(key):
    slot_of_page = jax.random.permutation(jax.random.fold_in(key, 11), PAGES).astype(jnp.int32)
    page_of_slot = jnp.argsort(slot_of_page).astype(jnp.int32)
    remaining = LIST - MOST
    base_count = remaining // (N_CACHE - 1)
    leftover = remaining % (N_CACHE - 1)
    pair_count = (N_CACHE - 1) // 2
    headroom = base_count // 2
    shard_ids = jnp.arange(N_CACHE, dtype=jnp.int32)
    slot_ids = jnp.arange(PAGES, dtype=jnp.int32)
    slot_shard = slot_ids // PAGES_DEV

    def one_list(block_key):
        busy_shard = jax.random.randint(jax.random.fold_in(block_key, 1), (), 0, N_CACHE)
        spread = jax.random.permutation(jax.random.fold_in(block_key, 2), N_CACHE - 1).astype(jnp.int32)
        others = base_count + (spread < leftover).astype(jnp.int32)
        amounts = jax.random.randint(jax.random.fold_in(block_key, 3), (pair_count,), 0, headroom + 1).astype(jnp.int32)
        moves = jnp.zeros((N_CACHE - 1,), jnp.int32)
        moves = moves.at[0:2 * pair_count:2].add(amounts).at[1:2 * pair_count:2].add(-amounts)
        others = others + moves
        position = jnp.clip(shard_ids - (shard_ids > busy_shard).astype(jnp.int32), 0, N_CACHE - 2)
        quota = jnp.where(shard_ids == busy_shard, MOST, others[position])
        ranking = jax.random.permutation(jax.random.fold_in(block_key, 4), PAGES).astype(jnp.int32)
        sorted_order = jnp.argsort(slot_shard * PAGES + ranking)
        within = jnp.argsort(sorted_order).astype(jnp.int32) - slot_shard * PAGES_DEV
        chosen = (within < quota[slot_shard]).astype(jnp.int32)
        shuffle = jax.random.permutation(jax.random.fold_in(block_key, 5), PAGES).astype(jnp.int32)
        picked = jnp.argsort((1 - chosen) * PAGES + shuffle)[:LIST]
        return page_of_slot[picked]
    block_keys = jax.vmap(lambda index: jax.random.fold_in(key, index))(jnp.arange(N_SECTIONS * BLOCKS))
    lists = jax.vmap(one_list)(block_keys).reshape(N_SECTIONS, BLOCKS, LIST)
    return (slot_of_page, lists)


def draw_page_table(key, part):
    return page_layout(key)[0].astype(jnp.int32)


def draw_page_list(key, part):
    return page_layout(key)[1].astype(jnp.int32)


def draw_list_len(key, part):
    lengths = jax.random.randint(jax.random.fold_in(key, 21), (N_SECTIONS * BLOCKS,), LIST // 2, LIST + 1)
    full_block = jax.random.randint(jax.random.fold_in(key, 22), (), 0, N_SECTIONS * BLOCKS)
    flat = jnp.where(jnp.arange(N_SECTIONS * BLOCKS) == full_block, LIST, lengths)
    return flat.reshape(N_SECTIONS, BLOCKS).astype(jnp.int32)


def draw_key_scale(key, part):
    shape = (N_SECTIONS, PAGES, KV_HEADS)
    scales = jnp.exp(jax.random.uniform(jax.random.fold_in(key, 31), shape, jnp.float32, math.log(0.5), math.log(2.0)))
    return scales.astype(jnp.float32)


def place_ends(drawn, own_key, smallest, high):
    dims = drawn.shape
    spot = [jax.random.randint(jax.random.fold_in(own_key, axis), (), 0, dims[axis]) for axis in range(len(dims))]
    drawn = drawn.at[tuple(spot)].set(smallest)
    longest = dims.index(max(dims))
    spot[longest] = (spot[longest] + 1) % dims[longest]
    return drawn.at[tuple(spot)].set(high)


def block_scale(own_key, shape, shards, low, largest):
    loudness = 1.0
    for dim, shards_of in shards:
        steps = jax.random.uniform(jax.random.fold_in(jax.random.fold_in(own_key, 6), dim), (shards_of,), jnp.float32, low / len(shards), largest / len(shards))
        loudness = loudness * jnp.repeat(jnp.exp(steps), shape[dim] // shards_of).reshape((-1,) + (1,) * (len(shape) - 1 - dim))
    return loudness


def normal_values(stream_key, dims, width, reach, cuts=(), held_as=jnp.bfloat16):
    values = jax.random.normal(stream_key, dims, jnp.float32) * width
    if len(cuts) > 0:
        values = block_scale(stream_key, dims, cuts, -0.22, 0.18) * values
    return jnp.clip(values, min=-reach, max=reach).astype(held_as)


def setup_inputs(seed: int = 0) -> dict:
    streams_of = jax.random.split(jax.random.key(seed), 14)
    return {
        "hidden": normal_values(streams_of[0], (N_SECTIONS, ROWS, D), 1.0, 6.0, ((0, 4), (1, 4))),
        "norm_gain": jnp.clip(1.0 + 0.18 * jax.random.normal(streams_of[1], (N_SECTIONS, D), jnp.float32), 0.1, 1.9),
        "w_query": normal_values(streams_of[2], (N_SECTIONS, D, Q_HEADS * HEAD_DIM), D ** -0.5, 0.125, ((0, 4), (2, 2))),
        "query_gain": jnp.clip(1.0 + 0.18 * jax.random.normal(streams_of[3], (N_SECTIONS, HEAD_DIM), jnp.float32), 0.1, 1.9),
        "w_output": normal_values(streams_of[4], (N_SECTIONS, Q_HEADS * HEAD_DIM, D), (Q_HEADS * HEAD_DIM) ** -0.5, 0.09375, ((0, 4), (1, 2))),
        "key_cache": normal_values(streams_of[5], (N_SECTIONS, PAGES, PAGE, KV_HEADS * HEAD_DIM), 1.0, 6.0, ((0, 4), (1, 4), (3, 2))),
        "value_cache": normal_values(streams_of[6], (N_SECTIONS, PAGES, PAGE, KV_HEADS * HEAD_DIM), 1.0, 6.0, ((0, 4), (1, 4), (3, 2))),
        "key_scale": draw_key_scale(jax.random.fold_in(streams_of[13], 71), 0),
        "value_scale": jnp.clip(jnp.exp(math.log(2.0) - 1.3862944 * jax.random.uniform(streams_of[8], (N_SECTIONS, PAGES, KV_HEADS), jnp.float32) ** block_scale(streams_of[8], (N_SECTIONS, PAGES, KV_HEADS), ((0, 4), (1, 4), (2, 2)), -0.2, 0.2)), 0.5, 2.0),
        "page_table": draw_page_table(jax.random.fold_in(streams_of[13], 71), 0),
        "page_tokens": place_ends(jax.random.randint(streams_of[10], (PAGES,), 1, PAGE + 1), jax.random.fold_in(streams_of[10], 1), 1, PAGE).astype(jnp.int32),
        "page_list": draw_page_list(jax.random.fold_in(streams_of[13], 71), 0),
        "list_len": draw_list_len(jax.random.fold_in(streams_of[13], 71), 0),
    }


tiny_eps = 1e-06
masked_score = -1e+30

def one_section(hidden_rows, gain_row, query_weight, head_gain, output_weight, key_pages, value_pages, key_scales, value_scales, page_table, page_tokens, lists, lengths):
    inputs = hidden_rows.astype(jnp.float32)
    inverse = lax.rsqrt(lax.optimization_barrier(jnp.mean(inputs * inputs, axis=-1, keepdims=True)) + tiny_eps)
    normed = (inputs * inverse * gain_row).astype(jnp.bfloat16)
    projected = jnp.dot(normed, query_weight, preferred_element_type=jnp.float32).reshape(ROWS, Q_HEADS, HEAD_DIM)
    head_inverse = lax.rsqrt(lax.optimization_barrier(jnp.mean(projected * projected, axis=-1, keepdims=True)) + tiny_eps)
    queries = (projected * head_inverse * head_gain / math.sqrt(HEAD_DIM)).astype(jnp.bfloat16)
    group_size = Q_HEADS // KV_HEADS
    queries = queries.reshape(BLOCKS, QBLOCK, KV_HEADS, group_size, HEAD_DIM)

    def one_block(block_args):
        block_queries, entries, length = block_args
        slots = page_table[entries]
        counts = page_tokens[entries]
        key_rows = key_pages[slots].reshape(LIST * PAGE, KV_HEADS, HEAD_DIM).astype(jnp.float32)
        value_rows = value_pages[slots].reshape(LIST * PAGE, KV_HEADS, HEAD_DIM).astype(jnp.float32)
        key_factor = jnp.repeat(key_scales[slots], PAGE, axis=0).T
        value_factor = jnp.repeat(value_scales[slots], PAGE, axis=0).T
        entry_ids = jnp.arange(LIST, dtype=jnp.int32)
        token_ids = jnp.arange(PAGE, dtype=jnp.int32)
        live_mask = ((entry_ids[:, None] < length) & (token_ids[None, :] < counts[:, None])).reshape(LIST * PAGE)
        scores = jnp.einsum('rgjd,tgd->gjrt', block_queries.astype(jnp.float32), key_rows) * key_factor[:, None, None, :]
        scores = jnp.where(live_mask, scores, masked_score)
        top_score = lax.optimization_barrier(jnp.max(scores, axis=-1, keepdims=True))
        weights = jnp.where(live_mask, jnp.exp(scores - top_score), 0.0)
        totals = lax.optimization_barrier(jnp.sum(weights, axis=-1))
        rounded = lax.optimization_barrier((weights * value_factor[:, None, None, :]).astype(jnp.bfloat16))
        scaled = rounded.astype(jnp.float32)
        attended = jnp.einsum('gjrt,tgd->rgjd', scaled, value_rows) / jnp.transpose(totals, (2, 0, 1))[..., None]
        return attended.astype(jnp.bfloat16).reshape(QBLOCK, Q_HEADS * HEAD_DIM)
    attention = lax.map(one_block, (queries, lists, lengths)).reshape(ROWS, Q_HEADS * HEAD_DIM)
    updated = jnp.dot(attention, output_weight, preferred_element_type=jnp.float32) + inputs
    return updated.astype(jnp.bfloat16)

def reference(hidden, norm_gain, w_query, query_gain, w_output, key_cache, value_cache, key_scale, value_scale, page_table, page_tokens, page_list, list_len):
    results = []
    for section_id in range(N_SECTIONS):
        results.append(one_section(hidden[section_id], norm_gain[section_id], w_query[section_id], query_gain[section_id], w_output[section_id], key_cache[section_id], value_cache[section_id], key_scale[section_id], value_scale[section_id], page_table, page_tokens, page_list[section_id], list_len[section_id]))
    stacked = jnp.stack(results, axis=0)
    return jnp.roll(stacked, 1, axis=0)
```

```python
import functools
import math

import jax
import jax.numpy as jnp
from jax import lax
from jax.experimental import pallas as pl
from jax.experimental.pallas import tpu as pltpu
from jax.sharding import PartitionSpec as P

MOST = 8
ROW_PIECES = 2
SUM_PIECES = 4

tiny_eps = 1e-06
masked_score = -1e30
lowest_top = -1e29
MESH = pl.DeviceIdType.MESH


def lookup(entries, table):
    places = jnp.arange(table.shape[0], dtype=jnp.int32)
    matches = (entries[..., None] == places).astype(jnp.int32)
    return jnp.sum(matches * table, axis=-1)


def plan_pages(slots, counts, length, target, pages_dev):
    listed = slots.shape[-1]
    order = jnp.arange(listed, dtype=jnp.int32)
    chosen = (slots // pages_dev == target) & (order < length)
    flags = chosen.astype(jnp.int32)
    ranks = jnp.cumsum(flags) - flags
    wanted = jnp.arange(MOST, dtype=jnp.int32)
    picks = ((ranks[None, :] == wanted[:, None]) & chosen[None, :]).astype(jnp.int32)
    local = jnp.sum(picks * (slots % pages_dev)[None, :], axis=1)
    filled = jnp.sum(picks * counts[None, :], axis=1)
    return (local, filled)


def plan_blocks(slots, counts, lengths, target, pages_dev):
    return jax.vmap(
        lambda one_slots, one_counts, one_length: plan_pages(
            one_slots, one_counts, one_length, target, pages_dev
        )
    )(slots, counts, lengths)


def section_kernel(
    dims,
    hidden_ref,
    norm_gain_ref,
    w_query_ref,
    query_gain_ref,
    w_output_ref,
    key_ref,
    value_ref,
    slot_ref,
    factor_ref,
    out_ref,
    rows_ref,
    query_tiles,
    keys_ref,
    values_ref,
    normed_ref,
    queries_ref,
    lse_ref,
    residual_ref,
    near_ref,
    away_ref,
    sibling_ref,
    carry_ref,
    sum_ref,
    local_sems,
    tile_sems,
    row_recv,
    own_send,
    forward_send,
    sibling_send,
    lse_send,
    lse_recv,
    away_send,
    away_recv,
    carry_send,
    carry_recv,
    out_send,
    out_recv,
    credit,
    *spare,
):
    count, sections, kv_local, tight = dims
    acc_ref, output_tiles = (rows_ref, query_tiles) if tight else spare
    z = lax.axis_index("cache")
    core = lax.axis_index("heads")
    section = lax.axis_index("sections")
    rows, width = hidden_ref.shape[1:]
    heads_local, head_size = queries_ref.shape[1], queries_ref.shape[3]
    blocks, block_rows = queries_ref.shape[0], queries_ref.shape[2]
    tiles, depth, tile = query_tiles.shape
    half_rows, half_width = rows // 2, width // 2
    piece = half_rows // ROW_PIECES
    part = rows // SUM_PIECES
    most = slot_ref.shape[1]
    page_len = keys_ref.shape[1]
    group_size = heads_local // kv_local
    middle = count // 2
    first_pair = count if tight else middle
    pairs = count // 2
    twin = {"heads": 1 - core}
    following = {"sections": lax.rem(section + 1, sections)}
    previous = {"sections": lax.rem(section + sections - 1, sections)}

    def at(index):
        return {"cache": index}

    def remote(src, dst, send, recv, device):
        return pltpu.make_async_remote_copy(
            src_ref=src, dst_ref=dst, send_sem=send, recv_sem=recv, device_id=device, device_id_type=MESH
        )

    def piece_of(side, j):
        return pl.ds(pl.multiple_of(side * half_rows + j * piece, piece), piece)

    load_rows = pltpu.make_async_copy(hidden_ref.at[0], rows_ref.at[z], local_sems.at[0])
    load_keys = pltpu.make_async_copy(key_ref.at[0], keys_ref, local_sems.at[1])
    load_values = pltpu.make_async_copy(value_ref.at[0], values_ref, local_sems.at[2])
    load_residual = pltpu.make_async_copy(
        hidden_ref.at[0, :, pl.ds(pl.multiple_of(core * half_width, half_width), half_width)],
        residual_ref,
        local_sems.at[3],
    )

    def load_query_tile(i):
        return pltpu.make_async_copy(
            w_query_ref.at[0, :, pl.ds(pl.multiple_of(i * tile, tile), tile)], query_tiles.at[i], tile_sems.at[0, i]
        )

    def load_output_tile(i):
        per_half = tiles // 2
        own = jnp.where(i < per_half, 1 - core, core)
        column = own * half_width + lax.rem(i, per_half) * tile
        return pltpu.make_async_copy(
            w_output_ref.at[0, :, pl.ds(pl.multiple_of(column, tile), tile)], output_tiles.at[i], tile_sems.at[1, i]
        )

    load_rows.start()
    load_query_tile(0).start()
    barrier = pltpu.get_barrier_semaphore()
    for distance in range(1, count):
        pl.semaphore_signal(barrier, inc=1, device_id=at(lax.rem(z + distance, count)), device_id_type=MESH)
    for other in (twin, following, previous):
        pl.semaphore_signal(barrier, inc=1, device_id=other, device_id_type=MESH)
    for i in range(1, tiles):
        load_query_tile(i).start()
    load_keys.start()
    load_values.start()
    load_residual.start()
    if not tight:
        for i in range(tiles):
            load_output_tile(i).start()
    pl.semaphore_wait(barrier, count + 2)

    def own_copy(step, j):
        return remote(
            hidden_ref.at[0, piece_of(core, j)],
            rows_ref.at[z, piece_of(core, j)],
            own_send.at[(step + 1) // 2, j],
            row_recv.at[z, core, j],
            at(z + step),
        )

    def row_copy(owner, side, j, send, device):
        spot = rows_ref.at[owner, piece_of(side, j)]
        return remote(spot, spot, send, row_recv.at[owner, side, j], device)

    for j in range(ROW_PIECES):

        @pl.when(z > 0)
        def _():
            own_copy(-1, j).start()

        @pl.when(z < count - 1)
        def _():
            own_copy(1, j).start()

    def serve(distance, j):
        for step in (1, -1):
            owner = z - step * distance

            @pl.when((owner >= 0) & (owner < count))
            def _():
                row_copy(owner, core, j, forward_send.at[owner, j], twin).wait_recv()

                @pl.when((z + step >= 0) & (z + step < count))
                def _():
                    row_copy(owner, core, j, forward_send.at[owner, j], at(z + step)).start()

                row_copy(owner, core, j, sibling_send.at[owner, j], twin).start()

    def wait_row_sends(owner):
        step = jnp.where(owner < z, 1, -1)
        for j in range(ROW_PIECES):
            row_copy(owner, core, j, sibling_send.at[owner, j], twin).wait_send()

            @pl.when((z + step >= 0) & (z + step < count))
            def _():
                row_copy(owner, core, j, forward_send.at[owner, j], twin).wait_send()

    def owner_at(step):
        low = jnp.minimum(z, count - 1 - z)
        both = step <= 2 * low
        reach = jnp.where(both, (step + 1) // 2, step - low)
        right = jnp.where(both, lax.rem(step, 2) == 0, z < middle)
        return z + jnp.where(right, reach, -reach)

    def make_queries(owner, step):
        x = rows_ref[owner].astype(jnp.float32)
        inverse = lax.rsqrt(jnp.mean(x * x, axis=-1, keepdims=True) + tiny_eps)
        normed_ref[...] = (x * inverse * norm_gain_ref[...]).astype(jnp.bfloat16)

        def one_tile(i, _):
            @pl.when(step == 0)
            def _():
                load_query_tile(i).wait()

            projected = jnp.dot(normed_ref[...], query_tiles[i], preferred_element_type=jnp.float32)
            per_tile = tile // head_size
            for head in range(per_tile):
                own = projected[:, head * head_size : (head + 1) * head_size]
                turn = lax.rsqrt(jnp.mean(own * own, axis=-1, keepdims=True) + tiny_eps)
                scaled = (own * turn * query_gain_ref[...] / math.sqrt(head_size)).astype(jnp.bfloat16)
                for b in range(blocks):
                    queries_ref[b, i * per_tile + head] = scaled[b * block_rows : (b + 1) * block_rows]
            return 0

        lax.fori_loop(0, tiles, one_tile, 0)

    lanes = lax.broadcasted_iota(jnp.int32, (block_rows, 128), 1)
    together = 2

    def attend(owner, b):
        block = owner * blocks + b
        spot = pl.ds(pl.multiple_of(b * block_rows, block_rows), block_rows)
        keeper = factor_ref[block, 2 * kv_local : 2 * kv_local + 1, :] > 0.5
        lse_tile = jnp.full((block_rows, 128), masked_score, jnp.float32)
        for g in range(kv_local):
            columns = slice(g * head_size, (g + 1) * head_size)
            keys = jnp.concatenate([keys_ref[slot_ref[block, i], :, columns] for i in range(most)], axis=0)
            values = jnp.concatenate([values_ref[slot_ref[block, i], :, columns] for i in range(most)], axis=0)
            key_factor = factor_ref[block, g : g + 1, :]
            value_factor = factor_ref[block, kv_local + g : kv_local + g + 1, :]
            for j in range(0, group_size, together):
                head = g * group_size + j
                queries = queries_ref[b, head : head + together].reshape(together * block_rows, head_size)
                scores = lax.dot_general(
                    queries, keys, (((1,), (1,)), ((), ())), preferred_element_type=jnp.float32
                )
                scores = jnp.where(keeper, scores * key_factor, masked_score)
                top = jnp.maximum(jnp.max(scores, axis=-1, keepdims=True), lowest_top)
                weights = jnp.exp2(scores - top)
                total = jnp.sum(weights, axis=-1, keepdims=True)
                scaled = (weights * value_factor).astype(jnp.bfloat16)
                acc = jnp.dot(scaled, values, preferred_element_type=jnp.float32)
                some = total > 0.0
                total = jnp.where(some, total, 1.0)
                acc = acc / total
                lse = jnp.where(some, top + jnp.log2(total), masked_score)
                for k in range(together):
                    own = slice(k * block_rows, (k + 1) * block_rows)
                    place = slice((head + k) * head_size, (head + k + 1) * head_size)
                    acc_ref[owner, spot, place] = acc[own].astype(jnp.bfloat16)
                    lse_tile = jnp.where(lanes == head + k, lse[own], lse_tile)
        lse_ref[z, owner, b] = lse_tile.T[:heads_local, :]

    def lse_copy(owner, distance):
        spot = lse_ref.at[z, owner]
        other = lax.rem(z + distance, count)
        return remote(spot, spot, lse_send.at[distance - 1, owner], lse_recv.at[z, owner], at(other))

    def attention_step(step):
        owner = owner_at(step)

        @pl.when(step == 0)
        def _():
            load_rows.wait()

        @pl.when(step > 0)
        def _():
            for j in range(ROW_PIECES):
                row_copy(owner, 1 - core, j, sibling_send.at[owner, j], twin).wait_recv()
            if tight:
                wait_row_sends(owner)

        make_queries(owner, step)

        @pl.when(step == 0)
        def _():
            load_keys.wait()
            load_values.wait()

        def one_block(b, _):
            attend(owner, b)

            @pl.when((b < ROW_PIECES) & (step < count - 1))
            def _():
                serve(step + 1, b)

            return 0

        lax.fori_loop(0, max(blocks, ROW_PIECES), one_block, 0)

        def one_send(distance, _):
            lse_copy(owner, distance).start()
            return 0

        lax.fori_loop(1, count, one_send, 0)
        if tight:

            @pl.when(step == count - 1)
            def _():
                for i in range(tiles):
                    load_output_tile(i).start()

    def owner_of(pair, i):
        upper = (z < middle) == (i == 0)
        return jnp.where(upper, middle + pair, middle - 1 - pair)

    def away_copy(i):
        return remote(away_ref.at[i], sibling_ref.at[i], away_send.at[i], away_recv.at[i], twin)

    def sum_rows(j):
        return pl.ds(pl.multiple_of(j * part, part), part)

    def carry_copy(owner, i, j):
        step = jnp.where(owner > z, 1, -1)
        target = jnp.where(owner == z - 1, count, owner)
        return remote(
            sum_ref.at[i, sum_rows(j)],
            carry_ref.at[target, sum_rows(j)],
            carry_send.at[i, j],
            carry_recv.at[target, j],
            at(z + step),
        )

    def out_copy(i, j):
        return remote(
            sum_ref.at[i, sum_rows(j)], out_ref.at[0, sum_rows(j)], out_send.at[j], out_recv.at[j], following
        )

    def combine(pair, i, j):
        owner = owner_of(pair, i)
        spot = sum_rows(j)

        @pl.when((owner >= z) & (z > 0))
        def _():
            landed = carry_ref.at[owner, spot]
            remote(landed, landed, carry_send.at[i, j], carry_recv.at[owner, j], twin).wait_recv()
            near_ref[i, spot, :] += carry_ref[owner, spot, :].astype(jnp.float32)

        @pl.when((owner <= z) & (z < count - 1))
        def _():
            source = jnp.where(owner == z, count, owner)
            landed = carry_ref.at[source, spot]
            remote(landed, landed, carry_send.at[i, j], carry_recv.at[source, j], twin).wait_recv()
            near_ref[i, spot, :] += carry_ref[source, spot, :].astype(jnp.float32)

        value = near_ref[i, spot, :] + sibling_ref[i, spot, :].astype(jnp.float32)

        @pl.when((pair > 0) & (owner_of(pair - 1, i) != z))
        def _():
            carry_copy(owner, i, j).wait_send()

        @pl.when((pair > 0) & (owner_of(pair - 1, i) == z))
        def _():
            out_copy(i, j).wait_send()

        @pl.when(owner != z)
        def _():
            sum_ref[i, spot, :] = value.astype(jnp.bfloat16)
            carry_copy(owner, i, j).start()

        @pl.when(owner == z)
        def _():
            sum_ref[i, spot, :] = (value + residual_ref[spot, :].astype(jnp.float32)).astype(jnp.bfloat16)
            out_copy(i, j).start()

    def first_of_line(owner):
        return ((z == 0) & (owner > z)) | ((z == count - 1) & (owner < z))

    def give_credit(pair, i):
        @pl.when(pair < pairs - 1)
        def _():
            pl.semaphore_signal(credit.at[i], inc=1, device_id=twin, device_id_type=MESH)

    def finish_pair(pair):
        def one_part(j, _):
            for i in range(2):

                @pl.when(jnp.logical_not(first_of_line(owner_of(pair, i))))
                def _():
                    combine(pair, i, j)

            return 0

        lax.fori_loop(0, SUM_PIECES, one_part, 0)
        for i in range(2):

            @pl.when(jnp.logical_not(first_of_line(owner_of(pair, i))))
            def _():
                give_credit(pair, i)

    def project_pair(pair):
        def one_owner(i, _):
            owner = owner_of(pair, i)

            def one_wait(distance, _):
                other = lax.rem(z + distance, count)
                spot = lse_ref.at[other, owner]
                remote(spot, spot, lse_send.at[0, owner], lse_recv.at[other, owner], twin).wait_recv()
                return 0

            lax.fori_loop(1, count, one_wait, 0)

            def one_block(b, _):
                spot = pl.ds(pl.multiple_of(b * block_rows, block_rows), block_rows)
                terms = [lse_ref[k, owner, b] for k in range(count)]
                top = functools.reduce(jnp.maximum, terms)
                total = sum(jnp.exp2(term - top) for term in terms)
                share = jnp.exp2(lse_ref[z, owner, b] - top) / total
                share = jnp.concatenate([share, jnp.zeros((128 - heads_local, block_rows), jnp.float32)], axis=0).T
                for head in range(heads_local):
                    columns = slice(head * head_size, (head + 1) * head_size)
                    normed_ref[spot, columns] = (
                        acc_ref[owner, spot, columns].astype(jnp.float32) * share[:, head : head + 1]
                    ).astype(jnp.bfloat16)
                return 0

            lax.fori_loop(0, blocks, one_block, 0)

            @pl.when((pair == 0) & (i == 0))
            def _():
                for k in range(tiles):
                    load_output_tile(k).wait()

                load_residual.wait()

            @pl.when(pair > 0)
            def _():
                away_copy(i).wait_send()
                pl.semaphore_wait(credit.at[i], 1)

            per_half = tiles // 2
            for k in range(per_half):
                away_ref[i, :, k * tile : (k + 1) * tile] = jnp.dot(
                    normed_ref[...], output_tiles[k], preferred_element_type=jnp.float32
                ).astype(jnp.bfloat16)
            away_copy(i).start()
            for k in range(per_half):
                near_ref[i, :, k * tile : (k + 1) * tile] = jnp.dot(
                    normed_ref[...], output_tiles[per_half + k], preferred_element_type=jnp.float32
                )
            away_copy(i).wait_recv()

            @pl.when(first_of_line(owner))
            def _():
                def one_part(j, _):
                    combine(pair, i, j)
                    return 0

                lax.fori_loop(0, SUM_PIECES, one_part, 0)
                give_credit(pair, i)

            return 0

        lax.fori_loop(0, 2, one_owner, 0)

    def one_step(step, _):
        if tight:

            @pl.when(step < count)
            def _():
                attention_step(step)
        else:
            attention_step(step)

        @pl.when(step > first_pair)
        def _():
            finish_pair(step - first_pair - 1)

        @pl.when(step >= first_pair)
        def _():
            project_pair(step - first_pair)

        return 0

    lax.fori_loop(0, first_pair + pairs, one_step, 0)
    finish_pair(pairs - 1)

    for i in range(2):
        away_copy(i).wait_send()

        def one_part(j, _):
            @pl.when(owner_of(pairs - 1, i) != z)
            def _():
                carry_copy(owner_of(pairs - 1, i), i, j).wait_send()

            @pl.when(owner_of(pairs - 1, i) == z)
            def _():
                out_copy(i, j).wait_send()

            return 0

        lax.fori_loop(0, SUM_PIECES, one_part, 0)
    for j in range(ROW_PIECES):

        @pl.when(z > 0)
        def _():
            own_copy(-1, j).wait_send()

        @pl.when(z < count - 1)
        def _():
            own_copy(1, j).wait_send()

    def one_owner(owner, _):
        if not tight:

            @pl.when(owner != z)
            def _():
                wait_row_sends(owner)

        def one_send(distance, _):
            lse_copy(owner, distance).wait_send()
            return 0

        lax.fori_loop(1, count, one_send, 0)
        return 0

    lax.fori_loop(0, count, one_owner, 0)
    for j in range(SUM_PIECES):
        out_copy(0, j).wait_recv()


def run_section(dims, hidden, norm_gain, w_query, query_gain, w_output, key_cache, value_cache, slots, factors):
    count, sections, kv_local = dims
    rows, width = hidden.shape[1:]
    depth, columns = w_query.shape[1:]
    head_size = query_gain.shape[1]
    heads_local = columns // head_size
    blocks = slots.shape[0] // count
    block_rows = rows // blocks
    half_width = width // 2
    tile = min(512, half_width, columns)
    tiles = columns // tile
    bf16, f32 = jnp.bfloat16, jnp.float32
    fixed = 2 * (w_query.size + key_cache.size + value_cache.size) + 20 * rows * width
    tight = fixed + 2 * w_output.size + 5 * count * rows * width > 50 * 2**20
    anywhere = pl.BlockSpec(memory_space=pl.ANY)
    held = pl.BlockSpec(memory_space=pltpu.VMEM)
    dma = pltpu.SemaphoreType.DMA
    scratch = [
        pltpu.VMEM((count, rows, width), bf16),
        pltpu.VMEM((tiles, depth, tile), bf16),
        pltpu.VMEM(key_cache.shape[1:], bf16),
        pltpu.VMEM(value_cache.shape[1:], bf16),
        pltpu.VMEM((rows, width), bf16),
        pltpu.VMEM((blocks, heads_local, block_rows, head_size), bf16),
        pltpu.VMEM((count, count, blocks, heads_local, block_rows), f32),
        pltpu.VMEM((rows, half_width), bf16),
        pltpu.VMEM((2, rows, half_width), f32),
        pltpu.VMEM((2, rows, half_width), bf16),
        pltpu.VMEM((2, rows, half_width), bf16),
        pltpu.VMEM((count + 1, rows, half_width), bf16),
        pltpu.VMEM((2, rows, half_width), bf16),
        dma((4,)),
        dma((2, tiles)),
        dma((count, 2, ROW_PIECES)),
        dma((2, ROW_PIECES)),
        dma((count, ROW_PIECES)),
        dma((count, ROW_PIECES)),
        dma((count - 1, count)),
        dma((count, count)),
        dma((2,)),
        dma((2,)),
        dma((2, SUM_PIECES)),
        dma((count + 1, SUM_PIECES)),
        dma((SUM_PIECES,)),
        dma((SUM_PIECES,)),
        pltpu.SemaphoreType.REGULAR((2,)),
    ]
    if not tight:
        scratch += [
            pltpu.VMEM((count, rows, heads_local * head_size), bf16),
            pltpu.VMEM((tiles, heads_local * head_size, tile), bf16),
        ]
    return pl.pallas_call(
        functools.partial(section_kernel, (count, sections, kv_local, tight)),
        out_shape=jax.ShapeDtypeStruct((1, rows, half_width), bf16),
        in_specs=[
            anywhere,
            held,
            anywhere,
            held,
            anywhere,
            anywhere,
            anywhere,
            pl.BlockSpec(memory_space=pltpu.SMEM),
            held,
        ],
        out_specs=anywhere,
        scratch_shapes=scratch,
        compiler_params=pltpu.CompilerParams(
            collective_id=0, has_side_effects=True, vmem_limit_bytes=63 * 2**20
        ),
        name="section",
    )(hidden, norm_gain, w_query, query_gain, w_output, key_cache, value_cache, slots, factors)


def body(
    hidden,
    norm_gain,
    w_query,
    query_gain,
    w_output,
    key_cache,
    value_cache,
    key_scale,
    value_scale,
    page_table,
    page_tokens,
    page_list,
    list_len,
):
    kv_local = key_scale.shape[2]
    pages_dev, page_len = key_cache.shape[1:3]
    count = lax.axis_size("cache")
    sections = lax.axis_size("sections")
    own_shard = lax.axis_index("cache")
    all_slots = lookup(page_list[0], page_table)
    all_counts = lookup(page_list[0], page_tokens)
    local_all, filled_all = plan_blocks(all_slots, all_counts, list_len[0], own_shard, pages_dev)
    page_ids = jnp.arange(pages_dev, dtype=jnp.int32)
    picks = local_all[..., None] == page_ids

    def factor(scales):
        picked = jnp.sum(jnp.where(picks[:, None], scales.T[None, :, None, :], 0.0), axis=-1)
        return jnp.repeat(picked, page_len, axis=2)

    within = jnp.arange(page_len, dtype=jnp.int32)
    live_mask = (within < filled_all[..., None]).astype(jnp.float32)
    live_mask = live_mask.reshape(live_mask.shape[0], 1, -1)
    factors = jnp.concatenate(
        [factor(key_scale[0] * math.log2(math.e)), factor(value_scale[0]), live_mask], axis=1
    )
    return run_section(
        (count, sections, kv_local),
        hidden,
        norm_gain,
        w_query,
        query_gain,
        w_output,
        key_cache,
        value_cache,
        local_all,
        factors,
    )


def solution(mesh):
    return jax.shard_map(
        body,
        mesh=mesh,
        in_specs=(
            P("sections", "cache", None),
            P("sections", None),
            P("sections", None, "heads"),
            P("sections", None),
            P("sections", "heads", None),
            P("sections", "cache", None, "heads"),
            P("sections", "cache", None, "heads"),
            P("sections", "cache", "heads"),
            P("sections", "cache", "heads"),
            P(),
            P(),
            P("sections", None, None),
            P("sections", None),
        ),
        out_specs=P("sections", "cache", "heads"),
        check_vma=False,
    )
```

```python
import functools
import math

import jax
import jax.numpy as jnp
from jax import lax
from jax.experimental import pallas as pl
from jax.experimental.pallas import tpu as pltpu
from jax.sharding import PartitionSpec as P

MOST = 8
ROW_PIECES = 2
SUM_PIECES = 4

tiny_eps = 1e-06
masked_score = -1e30
lowest_top = -1e29
MESH = pl.DeviceIdType.MESH


def lookup(entries, table):
    places = jnp.arange(table.shape[0], dtype=jnp.int32)
    matches = (entries[..., None] == places).astype(jnp.int32)
    return jnp.sum(matches * table, axis=-1)


def plan_pages(slots, counts, length, target, pages_dev):
    listed = slots.shape[-1]
    order = jnp.arange(listed, dtype=jnp.int32)
    chosen = (slots // pages_dev == target) & (order < length)
    flags = chosen.astype(jnp.int32)
    ranks = jnp.cumsum(flags) - flags
    wanted = jnp.arange(MOST, dtype=jnp.int32)
    picks = ((ranks[None, :] == wanted[:, None]) & chosen[None, :]).astype(jnp.int32)
    local = jnp.sum(picks * (slots % pages_dev)[None, :], axis=1)
    filled = jnp.sum(picks * counts[None, :], axis=1)
    return (local, filled)


def plan_blocks(slots, counts, lengths, target, pages_dev):
    return jax.vmap(
        lambda one_slots, one_counts, one_length: plan_pages(
            one_slots, one_counts, one_length, target, pages_dev
        )
    )(slots, counts, lengths)


def section_kernel(
    dims,
    hidden_ref,
    norm_gain_ref,
    w_query_ref,
    query_gain_ref,
    w_output_ref,
    key_ref,
    value_ref,
    slot_ref,
    fill_ref,
    key_scale_ref,
    value_scale_ref,
    out_ref,
    rows_ref,
    query_tiles,
    keys_ref,
    values_ref,
    normed_ref,
    queries_ref,
    lse_ref,
    residual_ref,
    near_ref,
    away_ref,
    sibling_ref,
    carry_ref,
    sum_ref,
    local_sems,
    tile_sems,
    row_recv,
    own_send,
    forward_send,
    sibling_send,
    lse_send,
    lse_recv,
    away_send,
    away_recv,
    carry_send,
    carry_recv,
    out_send,
    out_recv,
    credit,
    *spare,
):
    count, sections, kv_local, tight = dims
    acc_ref, output_tiles = (rows_ref, query_tiles) if tight else spare
    z = lax.axis_index("cache")
    core = lax.axis_index("heads")
    section = lax.axis_index("sections")
    rows, width = hidden_ref.shape[1:]
    heads_local, head_size = queries_ref.shape[1], queries_ref.shape[3]
    blocks, block_rows = queries_ref.shape[0], queries_ref.shape[2]
    tiles, depth, tile = query_tiles.shape
    half_rows, half_width = rows // 2, width // 2
    piece = half_rows // ROW_PIECES
    part = rows // SUM_PIECES
    pages_dev, page_len = keys_ref.shape[:2]
    most = MOST
    group_size = heads_local // kv_local
    middle = count // 2
    first_pair = count if tight else middle
    pairs = count // 2
    twin = {"heads": 1 - core}
    following = {"sections": lax.rem(section + 1, sections)}
    previous = {"sections": lax.rem(section + sections - 1, sections)}

    def at(index):
        return {"cache": index}

    def remote(src, dst, send, recv, device):
        return pltpu.make_async_remote_copy(
            src_ref=src, dst_ref=dst, send_sem=send, recv_sem=recv, device_id=device, device_id_type=MESH
        )

    def piece_of(side, j):
        return pl.ds(pl.multiple_of(side * half_rows + j * piece, piece), piece)

    load_rows = pltpu.make_async_copy(hidden_ref.at[0], rows_ref.at[z], local_sems.at[0])
    load_keys = pltpu.make_async_copy(key_ref.at[0], keys_ref, local_sems.at[1])
    load_values = pltpu.make_async_copy(value_ref.at[0], values_ref, local_sems.at[2])
    load_residual = pltpu.make_async_copy(
        hidden_ref.at[0, :, pl.ds(pl.multiple_of(core * half_width, half_width), half_width)],
        residual_ref,
        local_sems.at[3],
    )

    def load_query_tile(i):
        return pltpu.make_async_copy(
            w_query_ref.at[0, :, pl.ds(pl.multiple_of(i * tile, tile), tile)], query_tiles.at[i], tile_sems.at[0, i]
        )

    def load_output_tile(i):
        per_half = tiles // 2
        own = jnp.where(i < per_half, 1 - core, core)
        column = own * half_width + lax.rem(i, per_half) * tile
        return pltpu.make_async_copy(
            w_output_ref.at[0, :, pl.ds(pl.multiple_of(column, tile), tile)], output_tiles.at[i], tile_sems.at[1, i]
        )

    load_rows.start()
    load_query_tile(0).start()
    barrier = pltpu.get_barrier_semaphore()
    for distance in range(1, count):
        pl.semaphore_signal(barrier, inc=1, device_id=at(lax.rem(z + distance, count)), device_id_type=MESH)
    for other in (twin, following, previous):
        pl.semaphore_signal(barrier, inc=1, device_id=other, device_id_type=MESH)
    for i in range(1, tiles):
        load_query_tile(i).start()
    load_keys.start()
    load_values.start()
    load_residual.start()
    if not tight:
        for i in range(tiles):
            load_output_tile(i).start()

    pl.semaphore_wait(barrier, count + 2)

    def own_copy(step, j):
        return remote(
            hidden_ref.at[0, piece_of(core, j)],
            rows_ref.at[z, piece_of(core, j)],
            own_send.at[(step + 1) // 2, j],
            row_recv.at[z, core, j],
            at(z + step),
        )

    def row_copy(owner, side, j, send, device):
        spot = rows_ref.at[owner, piece_of(side, j)]
        return remote(spot, spot, send, row_recv.at[owner, side, j], device)

    for j in range(ROW_PIECES):

        @pl.when(z > 0)
        def _():
            own_copy(-1, j).start()

        @pl.when(z < count - 1)
        def _():
            own_copy(1, j).start()

    def serve(distance, j):
        for step in (1, -1):
            owner = z - step * distance

            @pl.when((owner >= 0) & (owner < count))
            def _():
                row_copy(owner, core, j, forward_send.at[owner, j], twin).wait_recv()

                @pl.when((z + step >= 0) & (z + step < count))
                def _():
                    row_copy(owner, core, j, forward_send.at[owner, j], at(z + step)).start()

                row_copy(owner, core, j, sibling_send.at[owner, j], twin).start()

    def wait_row_sends(owner):
        step = jnp.where(owner < z, 1, -1)
        for j in range(ROW_PIECES):
            row_copy(owner, core, j, sibling_send.at[owner, j], twin).wait_send()

            @pl.when((z + step >= 0) & (z + step < count))
            def _():
                row_copy(owner, core, j, forward_send.at[owner, j], twin).wait_send()

    def owner_at(step):
        low = jnp.minimum(z, count - 1 - z)
        both = step <= 2 * low
        reach = jnp.where(both, (step + 1) // 2, step - low)
        right = jnp.where(both, lax.rem(step, 2) == 0, z < middle)
        return z + jnp.where(right, reach, -reach)

    def make_queries(owner, step):
        x = rows_ref[owner].astype(jnp.float32)
        inverse = lax.rsqrt(jnp.mean(x * x, axis=-1, keepdims=True) + tiny_eps)
        normed_ref[...] = (x * inverse * norm_gain_ref[...]).astype(jnp.bfloat16)

        def one_tile(i, _):
            @pl.when(step == 0)
            def _():
                load_query_tile(i).wait()

            projected = jnp.dot(normed_ref[...], query_tiles[i], preferred_element_type=jnp.float32)
            per_tile = tile // head_size
            for head in range(per_tile):
                own = projected[:, head * head_size : (head + 1) * head_size]
                turn = lax.rsqrt(jnp.mean(own * own, axis=-1, keepdims=True) + tiny_eps)
                scaled = (own * turn * query_gain_ref[...] / math.sqrt(head_size)).astype(jnp.bfloat16)
                for b in range(blocks):
                    queries_ref[b, i * per_tile + head] = scaled[b * block_rows : (b + 1) * block_rows]
            return 0

        lax.fori_loop(0, tiles, one_tile, 0)

    lanes = lax.broadcasted_iota(jnp.int32, (block_rows, 128), 1)
    together = 2

    def attend(owner, b):
        block = owner * blocks + b
        spot = pl.ds(pl.multiple_of(b * block_rows, block_rows), block_rows)
        slots = [slot_ref[block, i] for i in range(most)]
        token = lax.broadcasted_iota(jnp.int32, (1, most * page_len), 1)

        def spread(values):
            row = jnp.full(token.shape, values[0])
            for i in range(1, most):
                row = jnp.where(token >= i * page_len, values[i], row)
            return row

        keeper = token < spread([i * page_len + fill_ref[block, i] for i in range(most)])
        lse_tile = jnp.full((block_rows, 128), masked_score, jnp.float32)
        for g in range(kv_local):
            columns = slice(g * head_size, (g + 1) * head_size)
            keys = jnp.concatenate([keys_ref[slot, :, columns] for slot in slots], axis=0)
            values = jnp.concatenate([values_ref[slot, :, columns] for slot in slots], axis=0)
            key_factor = spread([key_scale_ref[slot * kv_local + g] for slot in slots]) * math.log2(math.e)
            value_factor = spread([value_scale_ref[slot * kv_local + g] for slot in slots])
            for j in range(0, group_size, together):
                head = g * group_size + j
                queries = queries_ref[b, head : head + together].reshape(together * block_rows, head_size)
                scores = lax.dot_general(
                    queries, keys, (((1,), (1,)), ((), ())), preferred_element_type=jnp.float32
                )
                scores = jnp.where(keeper, scores * key_factor, masked_score)
                top = jnp.maximum(jnp.max(scores, axis=-1, keepdims=True), lowest_top)
                weights = jnp.exp2(scores - top)
                total = jnp.sum(weights, axis=-1, keepdims=True)
                scaled = (weights * value_factor).astype(jnp.bfloat16)
                acc = jnp.dot(scaled, values, preferred_element_type=jnp.float32)
                some = total > 0.0
                total = jnp.where(some, total, 1.0)
                acc = acc / total
                lse = jnp.where(some, top + jnp.log2(total), masked_score)
                for k in range(together):
                    own = slice(k * block_rows, (k + 1) * block_rows)
                    place = slice((head + k) * head_size, (head + k + 1) * head_size)
                    acc_ref[owner, spot, place] = acc[own].astype(jnp.bfloat16)
                    lse_tile = jnp.where(lanes == head + k, lse[own], lse_tile)
        lse_ref[z, owner, b] = lse_tile.T[:heads_local, :]

    def lse_copy(owner, distance):
        spot = lse_ref.at[z, owner]
        other = lax.rem(z + distance, count)
        return remote(spot, spot, lse_send.at[distance - 1, owner], lse_recv.at[z, owner], at(other))

    def attention_step(step):
        owner = owner_at(step)

        @pl.when(step == 0)
        def _():
            load_rows.wait()

        @pl.when(step > 0)
        def _():
            for j in range(ROW_PIECES):
                row_copy(owner, 1 - core, j, sibling_send.at[owner, j], twin).wait_recv()
            if tight:
                wait_row_sends(owner)

        make_queries(owner, step)

        @pl.when(step == 0)
        def _():
            load_keys.wait()
            load_values.wait()

        def one_block(b, _):
            attend(owner, b)

            @pl.when((step < count - 1) & (b < blocks - 1))
            def _():
                for j in range(ROW_PIECES - 1):

                    @pl.when(b == j)
                    def _():
                        serve(step + 1, j)

            return 0

        lax.fori_loop(0, blocks, one_block, 0)

        def one_send(distance, _):
            lse_copy(owner, distance).start()
            return 0

        lax.fori_loop(1, count, one_send, 0)

        @pl.when(step < count - 1)
        def _():
            for j in range(min(ROW_PIECES, blocks) - 1, ROW_PIECES):
                serve(step + 1, j)

        if tight:

            @pl.when(step == count - 1)
            def _():
                for i in range(tiles):
                    load_output_tile(i).start()

    def owner_of(pair, i):
        upper = (z < middle) == (i == 0)
        return jnp.where(upper, middle + pair, middle - 1 - pair)

    def slot_of(pair, i):
        return 2 * (pair if pairs <= 2 else lax.rem(pair, 2)) + i

    def away_copy(i):
        return remote(away_ref.at[i], sibling_ref.at[i], away_send.at[i], away_recv.at[i], twin)

    def sum_rows(j):
        return pl.ds(pl.multiple_of(j * part, part), part)

    def carry_copy(owner, i, j):
        step = jnp.where(owner > z, 1, -1)
        target = jnp.where(owner == z - 1, count, owner)
        return remote(
            sum_ref.at[i, sum_rows(j)],
            carry_ref.at[target, sum_rows(j)],
            carry_send.at[i, j],
            carry_recv.at[target, j],
            at(z + step),
        )

    def out_copy(i, j):
        return remote(
            sum_ref.at[i, sum_rows(j)], out_ref.at[0, sum_rows(j)], out_send.at[j], out_recv.at[j], following
        )

    def combine(pair, i, j):
        owner = owner_of(pair, i)
        slot = slot_of(pair, i)
        spot = sum_rows(j)

        @pl.when((owner >= z) & (z > 0))
        def _():
            landed = carry_ref.at[owner, spot]
            remote(landed, landed, carry_send.at[slot, j], carry_recv.at[owner, j], twin).wait_recv()
            near_ref[slot, spot, :] += carry_ref[owner, spot, :].astype(jnp.float32)

        @pl.when((owner <= z) & (z < count - 1))
        def _():
            source = jnp.where(owner == z, count, owner)
            landed = carry_ref.at[source, spot]
            remote(landed, landed, carry_send.at[slot, j], carry_recv.at[source, j], twin).wait_recv()
            near_ref[slot, spot, :] += carry_ref[source, spot, :].astype(jnp.float32)

        value = near_ref[slot, spot, :] + sibling_ref[slot, spot, :].astype(jnp.float32)

        @pl.when(pair > 1)
        def _():
            wait_sum_send(pair - 2, i, j)

        @pl.when(owner != z)
        def _():
            sum_ref[slot, spot, :] = value.astype(jnp.bfloat16)
            carry_copy(owner, slot, j).start()

        @pl.when(owner == z)
        def _():
            sum_ref[slot, spot, :] = (value + residual_ref[spot, :].astype(jnp.float32)).astype(jnp.bfloat16)
            out_copy(slot, j).start()

    def wait_sum_send(pair, i, j):
        owner = owner_of(pair, i)
        slot = slot_of(pair, i)

        @pl.when(owner != z)
        def _():
            carry_copy(owner, slot, j).wait_send()

        @pl.when(owner == z)
        def _():
            out_copy(slot, j).wait_send()

    def first_of_line(owner):
        return ((z == 0) & (owner > z)) | ((z == count - 1) & (owner < z))

    def give_credit(pair, i):
        if pairs > 2:

            @pl.when(pair < pairs - 2)
            def _():
                pl.semaphore_signal(credit.at[slot_of(pair, i)], inc=1, device_id=twin, device_id_type=MESH)

    def finish_pair(pair, ends):
        def mine(i):
            owner = owner_of(pair, i)
            if ends:
                return owner == z
            return (owner != z) & jnp.logical_not(first_of_line(owner))

        def one_part(j, _):
            for i in range(2):

                @pl.when(mine(i))
                def _():
                    combine(pair, i, j)

            return 0

        lax.fori_loop(0, SUM_PIECES, one_part, 0)
        for i in range(2):

            @pl.when(mine(i))
            def _():
                give_credit(pair, i)

    def project_pair(pair):
        def one_owner(i, _):
            owner = owner_of(pair, i)
            slot = slot_of(pair, i)

            def one_wait(distance, _):
                other = lax.rem(z + distance, count)
                spot = lse_ref.at[other, owner]
                remote(spot, spot, lse_send.at[0, owner], lse_recv.at[other, owner], twin).wait_recv()
                return 0

            lax.fori_loop(1, count, one_wait, 0)

            def one_block(b, _):
                spot = pl.ds(pl.multiple_of(b * block_rows, block_rows), block_rows)
                terms = [lse_ref[k, owner, b] for k in range(count)]
                top = functools.reduce(jnp.maximum, terms)
                total = sum(jnp.exp2(term - top) for term in terms)
                share = jnp.exp2(lse_ref[z, owner, b] - top) / total
                share = jnp.concatenate([share, jnp.zeros((128 - heads_local, block_rows), jnp.float32)], axis=0).T
                for head in range(heads_local):
                    columns = slice(head * head_size, (head + 1) * head_size)
                    normed_ref[spot, columns] = (
                        acc_ref[owner, spot, columns].astype(jnp.float32) * share[:, head : head + 1]
                    ).astype(jnp.bfloat16)
                return 0

            lax.fori_loop(0, blocks, one_block, 0)

            @pl.when((pair == 0) & (i == 0))
            def _():
                for k in range(tiles):
                    load_output_tile(k).wait()

                load_residual.wait()

            if pairs > 2:

                @pl.when(pair > 1)
                def _():
                    away_copy(slot).wait_send()
                    pl.semaphore_wait(credit.at[slot], 1)

            per_half = tiles // 2
            for k in range(per_half):
                away_ref[slot, :, k * tile : (k + 1) * tile] = jnp.dot(
                    normed_ref[...], output_tiles[k], preferred_element_type=jnp.float32
                ).astype(jnp.bfloat16)
            away_copy(slot).start()
            for k in range(per_half):
                near_ref[slot, :, k * tile : (k + 1) * tile] = jnp.dot(
                    normed_ref[...], output_tiles[per_half + k], preferred_element_type=jnp.float32
                )
            away_copy(slot).wait_recv()

            @pl.when(first_of_line(owner))
            def _():
                def one_part(j, _):
                    combine(pair, i, j)
                    return 0

                lax.fori_loop(0, SUM_PIECES, one_part, 0)
                give_credit(pair, i)

            return 0

        lax.fori_loop(0, 2, one_owner, 0)

    def one_step(step, _):
        if tight:

            @pl.when(step < count)
            def _():
                attention_step(step)
        else:
            attention_step(step)

        @pl.when(step > first_pair)
        def _():
            finish_pair(step - first_pair - 1, False)

        @pl.when(step >= first_pair)
        def _():
            project_pair(step - first_pair)

        @pl.when(step > first_pair)
        def _():
            finish_pair(step - first_pair - 1, True)

        return 0

    lax.fori_loop(0, first_pair + pairs, one_step, 0)
    finish_pair(pairs - 1, False)
    finish_pair(pairs - 1, True)

    for pair in range(max(pairs - 2, 0), pairs):
        for i in range(2):
            away_copy(slot_of(pair, i)).wait_send()

            def one_part(j, _):
                wait_sum_send(pair, i, j)
                return 0

            lax.fori_loop(0, SUM_PIECES, one_part, 0)
    for j in range(ROW_PIECES):

        @pl.when(z > 0)
        def _():
            own_copy(-1, j).wait_send()

        @pl.when(z < count - 1)
        def _():
            own_copy(1, j).wait_send()

    def one_owner(owner, _):
        if not tight:

            @pl.when(owner != z)
            def _():
                wait_row_sends(owner)

        def one_send(distance, _):
            lse_copy(owner, distance).wait_send()
            return 0

        lax.fori_loop(1, count, one_send, 0)
        return 0

    lax.fori_loop(0, count, one_owner, 0)
    for j in range(SUM_PIECES):
        out_copy(0, j).wait_recv()


def run_section(dims, hidden, norm_gain, w_query, query_gain, w_output, key_cache, value_cache, *small):
    count, sections, kv_local = dims
    rows, width = hidden.shape[1:]
    depth, columns = w_query.shape[1:]
    head_size = query_gain.shape[1]
    heads_local = columns // head_size
    all_blocks = small[0].shape[0]
    blocks = all_blocks // count
    block_rows = rows // blocks
    half_width = width // 2
    tile = min(512, half_width, columns)
    tiles = columns // tile
    bf16, f32 = jnp.bfloat16, jnp.float32
    fixed = 2 * (w_query.size + key_cache.size + value_cache.size) + 28 * rows * width
    tight = fixed + 2 * w_output.size + 5 * count * rows * width > 50 * 2**20
    anywhere = pl.BlockSpec(memory_space=pl.ANY)
    held = pl.BlockSpec(memory_space=pltpu.VMEM)
    dma = pltpu.SemaphoreType.DMA
    scratch = [
        pltpu.VMEM((count, rows, width), bf16),
        pltpu.VMEM((tiles, depth, tile), bf16),
        pltpu.VMEM(key_cache.shape[1:], bf16),
        pltpu.VMEM(value_cache.shape[1:], bf16),
        pltpu.VMEM((rows, width), bf16),
        pltpu.VMEM((blocks, heads_local, block_rows, head_size), bf16),
        pltpu.VMEM((count, count, blocks, heads_local, block_rows), f32),
        pltpu.VMEM((rows, half_width), bf16),
        pltpu.VMEM((4, rows, half_width), f32),
        pltpu.VMEM((4, rows, half_width), bf16),
        pltpu.VMEM((4, rows, half_width), bf16),
        pltpu.VMEM((count + 1, rows, half_width), bf16),
        pltpu.VMEM((4, rows, half_width), bf16),
        dma((4,)),
        dma((2, tiles)),
        dma((count, 2, ROW_PIECES)),
        dma((2, ROW_PIECES)),
        dma((count, ROW_PIECES)),
        dma((count, ROW_PIECES)),
        dma((count - 1, count)),
        dma((count, count)),
        dma((4,)),
        dma((4,)),
        dma((4, SUM_PIECES)),
        dma((count + 1, SUM_PIECES)),
        dma((SUM_PIECES,)),
        dma((SUM_PIECES,)),
        pltpu.SemaphoreType.REGULAR((4,)),
    ]
    if not tight:
        scratch += [
            pltpu.VMEM((count, rows, heads_local * head_size), bf16),
            pltpu.VMEM((tiles, heads_local * head_size, tile), bf16),
        ]
    return pl.pallas_call(
        functools.partial(section_kernel, (count, sections, kv_local, tight)),
        out_shape=jax.ShapeDtypeStruct((1, rows, half_width), bf16),
        in_specs=[
            anywhere,
            held,
            anywhere,
            held,
            anywhere,
            anywhere,
            anywhere,
            *[pl.BlockSpec(memory_space=pltpu.SMEM)] * len(small),
        ],
        out_specs=anywhere,
        scratch_shapes=scratch,
        compiler_params=pltpu.CompilerParams(
            collective_id=0, has_side_effects=True, vmem_limit_bytes=63 * 2**20
        ),
        name="section",
    )(hidden, norm_gain, w_query, query_gain, w_output, key_cache, value_cache, *small)


def body(
    hidden,
    norm_gain,
    w_query,
    query_gain,
    w_output,
    key_cache,
    value_cache,
    key_scale,
    value_scale,
    page_table,
    page_tokens,
    page_list,
    list_len,
):
    kv_local = key_scale.shape[2]
    count = lax.axis_size("cache")
    sections = lax.axis_size("sections")
    all_slots = lookup(page_list[0], page_table)
    all_counts = lookup(page_list[0], page_tokens)
    local_all, filled_all = plan_blocks(
        all_slots, all_counts, list_len[0], lax.axis_index("cache"), key_cache.shape[1]
    )
    return run_section(
        (count, sections, kv_local),
        hidden,
        norm_gain,
        w_query,
        query_gain,
        w_output,
        key_cache,
        value_cache,
        local_all,
        filled_all,
        key_scale.reshape(-1),
        value_scale.reshape(-1),
    )


def solution(mesh):
    return jax.shard_map(
        body,
        mesh=mesh,
        in_specs=(
            P("sections", "cache", None),
            P("sections", None),
            P("sections", None, "heads"),
            P("sections", None),
            P("sections", "heads", None),
            P("sections", "cache", None, "heads"),
            P("sections", "cache", None, "heads"),
            P("sections", "cache", "heads"),
            P("sections", "cache", "heads"),
            P(),
            P(),
            P("sections", None, None),
            P("sections", None),
        ),
        out_specs=P("sections", "cache", "heads"),
        check_vma=False,
    )
```

```python
import functools
import math

import jax
import jax.numpy as jnp
from jax import lax
from jax.experimental import pallas as pl
from jax.experimental.pallas import tpu as pltpu
from jax.sharding import PartitionSpec as P

MOST = 8
ROW_PIECES = 2
SUM_PIECES = 8
EARLY_PIECES = 2
SKEW = 2

tiny_eps = 1e-06
masked_score = -1e30
lowest_top = -1e29
MESH = pl.DeviceIdType.MESH


def lookup(entries, table):
    places = jnp.arange(table.shape[0], dtype=jnp.int32)
    matches = (entries[..., None] == places).astype(jnp.int32)
    return jnp.sum(matches * table, axis=-1)


def plan_pages(slots, counts, length, target, pages_dev):
    listed = slots.shape[-1]
    order = jnp.arange(listed, dtype=jnp.int32)
    chosen = (slots // pages_dev == target) & (order < length)
    flags = chosen.astype(jnp.int32)
    ranks = jnp.cumsum(flags) - flags
    wanted = jnp.arange(MOST, dtype=jnp.int32)
    picks = ((ranks[None, :] == wanted[:, None]) & chosen[None, :]).astype(jnp.int32)
    local = jnp.sum(picks * (slots % pages_dev)[None, :], axis=1)
    filled = jnp.sum(picks * counts[None, :], axis=1)
    return (local, filled)


def plan_blocks(slots, counts, lengths, target, pages_dev):
    return jax.vmap(
        lambda one_slots, one_counts, one_length: plan_pages(
            one_slots, one_counts, one_length, target, pages_dev
        )
    )(slots, counts, lengths)


def section_kernel(
    dims,
    hidden_ref,
    norm_gain_ref,
    w_query_ref,
    query_gain_ref,
    w_output_ref,
    key_ref,
    value_ref,
    slot_ref,
    fill_ref,
    key_scale_ref,
    value_scale_ref,
    out_ref,
    rows_ref,
    query_tiles,
    keys_ref,
    values_ref,
    normed_ref,
    queries_ref,
    lse_ref,
    residual_ref,
    near_ref,
    away_ref,
    sibling_ref,
    carry_ref,
    sum_ref,
    local_sems,
    tile_sems,
    row_recv,
    own_send,
    forward_send,
    sibling_send,
    lse_send,
    lse_recv,
    away_send,
    away_recv,
    carry_send,
    carry_recv,
    out_send,
    out_recv,
    credit,
    *spare,
):
    count, sections, kv_local, tight = dims
    acc_ref, output_tiles = (rows_ref, query_tiles) if tight else spare
    z = lax.axis_index("cache")
    core = lax.axis_index("heads")
    section = lax.axis_index("sections")
    rows, width = hidden_ref.shape[1:]
    heads_local, head_size = queries_ref.shape[1], queries_ref.shape[3]
    blocks, block_rows = queries_ref.shape[0], queries_ref.shape[2]
    tiles, depth, tile = query_tiles.shape
    half_rows, half_width = rows // 2, width // 2
    piece = half_rows // ROW_PIECES
    part = rows // SUM_PIECES
    pages_dev, page_len = keys_ref.shape[:2]
    most = MOST
    group_size = heads_local // kv_local
    middle = count // 2
    first_pair = count if tight else middle
    pairs = count // 2
    twin = {"heads": 1 - core}
    following = {"sections": lax.rem(section + 1, sections)}
    previous = {"sections": lax.rem(section + sections - 1, sections)}

    def at(index):
        return {"cache": index}

    def remote(src, dst, send, recv, device):
        return pltpu.make_async_remote_copy(
            src_ref=src, dst_ref=dst, send_sem=send, recv_sem=recv, device_id=device, device_id_type=MESH
        )

    def piece_of(side, j):
        return pl.ds(pl.multiple_of(side * half_rows + j * piece, piece), piece)

    load_rows = pltpu.make_async_copy(hidden_ref.at[0], rows_ref.at[z], local_sems.at[0])
    load_keys = pltpu.make_async_copy(key_ref.at[0], keys_ref, local_sems.at[1])
    load_values = pltpu.make_async_copy(value_ref.at[0], values_ref, local_sems.at[2])
    load_residual = pltpu.make_async_copy(
        hidden_ref.at[0, :, pl.ds(pl.multiple_of(core * half_width, half_width), half_width)],
        residual_ref,
        local_sems.at[3],
    )

    def load_query_tile(i):
        return pltpu.make_async_copy(
            w_query_ref.at[0, :, pl.ds(pl.multiple_of(i * tile, tile), tile)], query_tiles.at[i], tile_sems.at[0, i]
        )

    def load_output_tile(i):
        per_half = tiles // 2
        own = jnp.where(i < per_half, 1 - core, core)
        column = own * half_width + lax.rem(i, per_half) * tile
        return pltpu.make_async_copy(
            w_output_ref.at[0, :, pl.ds(pl.multiple_of(column, tile), tile)], output_tiles.at[i], tile_sems.at[1, i]
        )

    load_rows.start()
    load_query_tile(0).start()
    barrier = pltpu.get_barrier_semaphore()
    for distance in range(1, count):
        pl.semaphore_signal(barrier, inc=1, device_id=at(lax.rem(z + distance, count)), device_id_type=MESH)
    for other in (twin, following, previous):
        pl.semaphore_signal(barrier, inc=1, device_id=other, device_id_type=MESH)
    for i in range(1, tiles):
        load_query_tile(i).start()
    load_keys.start()
    load_values.start()
    load_residual.start()
    if not tight:
        for i in range(tiles):
            load_output_tile(i).start()

    pl.semaphore_wait(barrier, count + 2)

    def own_copy(step, j):
        return remote(
            hidden_ref.at[0, piece_of(core, j)],
            rows_ref.at[z, piece_of(core, j)],
            own_send.at[(step + 1) // 2, j],
            row_recv.at[z, core, j],
            at(z + step),
        )

    def row_copy(owner, side, j, send, device):
        spot = rows_ref.at[owner, piece_of(side, j)]
        return remote(spot, spot, send, row_recv.at[owner, side, j], device)

    for j in range(ROW_PIECES):

        @pl.when(z > 0)
        def _():
            own_copy(-1, j).start()

        @pl.when(z < count - 1)
        def _():
            own_copy(1, j).start()

    def serve(distance, j):
        for step in (1, -1):
            owner = z - step * distance

            @pl.when((owner >= 0) & (owner < count))
            def _():
                row_copy(owner, core, j, forward_send.at[owner, j], twin).wait_recv()

                @pl.when((z + step >= 0) & (z + step < count))
                def _():
                    row_copy(owner, core, j, forward_send.at[owner, j], at(z + step)).start()

                row_copy(owner, core, j, sibling_send.at[owner, j], twin).start()

    def wait_row_sends(owner):
        step = jnp.where(owner < z, 1, -1)
        for j in range(ROW_PIECES):
            row_copy(owner, core, j, sibling_send.at[owner, j], twin).wait_send()

            @pl.when((z + step >= 0) & (z + step < count))
            def _():
                row_copy(owner, core, j, forward_send.at[owner, j], twin).wait_send()

    def owner_at(step):
        low = jnp.minimum(z, count - 1 - z)
        both = step <= 2 * low
        reach = jnp.where(both, (step + 1) // 2, step - low)
        right = jnp.where(both, lax.rem(step, 2) == 0, z < middle)
        return z + jnp.where(right, reach, -reach)

    def make_queries(owner, step):
        x = rows_ref[owner].astype(jnp.float32)
        inverse = lax.rsqrt(jnp.mean(x * x, axis=-1, keepdims=True) + tiny_eps)
        normed_ref[...] = (x * inverse * norm_gain_ref[...]).astype(jnp.bfloat16)

        def one_tile(i, _):
            @pl.when(step == 0)
            def _():
                load_query_tile(i).wait()

            projected = jnp.dot(normed_ref[...], query_tiles[i], preferred_element_type=jnp.float32)
            per_tile = tile // head_size
            for head in range(per_tile):
                own = projected[:, head * head_size : (head + 1) * head_size]
                turn = lax.rsqrt(jnp.mean(own * own, axis=-1, keepdims=True) + tiny_eps)
                scaled = (own * turn * query_gain_ref[...] / math.sqrt(head_size)).astype(jnp.bfloat16)
                for b in range(blocks):
                    queries_ref[b, i * per_tile + head] = scaled[b * block_rows : (b + 1) * block_rows]
            return 0

        lax.fori_loop(0, tiles, one_tile, 0)

    lanes = lax.broadcasted_iota(jnp.int32, (block_rows, 128), 1)
    together = 2

    def attend(owner, b):
        block = owner * blocks + b
        spot = pl.ds(pl.multiple_of(b * block_rows, block_rows), block_rows)
        slots = [slot_ref[block, i] for i in range(most)]
        token = lax.broadcasted_iota(jnp.int32, (1, most * page_len), 1)

        def spread(values):
            row = jnp.full(token.shape, values[0])
            for i in range(1, most):
                row = jnp.where(token >= i * page_len, values[i], row)
            return row

        keeper = token < spread([i * page_len + fill_ref[block, i] for i in range(most)])
        lse_tile = jnp.full((block_rows, 128), masked_score, jnp.float32)
        for g in range(kv_local):
            columns = slice(g * head_size, (g + 1) * head_size)
            keys = jnp.concatenate([keys_ref[slot, :, columns] for slot in slots], axis=0)
            values = jnp.concatenate([values_ref[slot, :, columns] for slot in slots], axis=0)
            key_factor = spread([key_scale_ref[slot * kv_local + g] for slot in slots]) * math.log2(math.e)
            value_factor = spread([value_scale_ref[slot * kv_local + g] for slot in slots])
            for j in range(0, group_size, together):
                head = g * group_size + j
                queries = queries_ref[b, head : head + together].reshape(together * block_rows, head_size)
                scores = lax.dot_general(
                    queries, keys, (((1,), (1,)), ((), ())), preferred_element_type=jnp.float32
                )
                scores = jnp.where(keeper, scores * key_factor, masked_score)
                top = jnp.maximum(jnp.max(scores, axis=-1, keepdims=True), lowest_top)
                weights = jnp.exp2(scores - top)
                total = jnp.sum(weights, axis=-1, keepdims=True)
                scaled = (weights * value_factor).astype(jnp.bfloat16)
                acc = jnp.dot(scaled, values, preferred_element_type=jnp.float32)
                some = total > 0.0
                total = jnp.where(some, total, 1.0)
                acc = acc / total
                lse = jnp.where(some, top + jnp.log2(total), masked_score)
                for k in range(together):
                    own = slice(k * block_rows, (k + 1) * block_rows)
                    place = slice((head + k) * head_size, (head + k + 1) * head_size)
                    acc_ref[owner, spot, place] = acc[own].astype(jnp.bfloat16)
                    lse_tile = jnp.where(lanes == head + k, lse[own], lse_tile)
        lse_ref[z, owner, b] = lse_tile.T[:heads_local, :]

    def lse_copy(owner, distance):
        spot = lse_ref.at[z, owner]
        other = lax.rem(z + distance, count)
        return remote(spot, spot, lse_send.at[distance - 1, owner], lse_recv.at[z, owner], at(other))

    def attention_step(step):
        owner = owner_at(step)

        @pl.when(step == 0)
        def _():
            load_rows.wait()

        @pl.when(step > 0)
        def _():
            for j in range(ROW_PIECES):
                row_copy(owner, 1 - core, j, sibling_send.at[owner, j], twin).wait_recv()
            if tight:
                wait_row_sends(owner)

        make_queries(owner, step)

        @pl.when(step == 0)
        def _():
            load_keys.wait()
            load_values.wait()

        def one_block(b, _):
            attend(owner, b)

            @pl.when((step < count - 1) & (b < blocks - 1))
            def _():
                for j in range(ROW_PIECES - 1):

                    @pl.when(b == j)
                    def _():
                        serve(step + 1, j)

            return 0

        lax.fori_loop(0, blocks, one_block, 0)

        def one_send(distance, _):
            lse_copy(owner, distance).start()
            return 0

        lax.fori_loop(1, count, one_send, 0)

        @pl.when(step < count - 1)
        def _():
            for j in range(min(ROW_PIECES, blocks) - 1, ROW_PIECES):
                serve(step + 1, j)

        if tight:

            @pl.when(step == count - 1)
            def _():
                for i in range(tiles):
                    load_output_tile(i).start()

    def owner_of(pair, i):
        upper = (z < middle) == (i == 0)
        return jnp.where(upper, middle + pair, middle - 1 - pair)

    def slot_of(pair, i):
        return 2 * (pair if pairs <= 2 else lax.rem(pair, 2)) + i

    def away_copy(i):
        return remote(away_ref.at[i], sibling_ref.at[i], away_send.at[i], away_recv.at[i], twin)

    def sum_rows(j):
        return pl.ds(pl.multiple_of(j * part, part), part)

    def carry_copy(owner, i, j):
        step = jnp.where(owner > z, 1, -1)
        target = jnp.where(owner == z - 1, count, owner)
        return remote(
            sum_ref.at[i, sum_rows(j)],
            carry_ref.at[target, sum_rows(j)],
            carry_send.at[i, j],
            carry_recv.at[target, j],
            at(z + step),
        )

    def out_copy(i, j):
        return remote(
            sum_ref.at[i, sum_rows(j)], out_ref.at[0, sum_rows(j)], out_send.at[j], out_recv.at[j], following
        )

    def combine(pair, i, j):
        owner = owner_of(pair, i)
        slot = slot_of(pair, i)
        spot = sum_rows(j)

        @pl.when((owner >= z) & (z > 0))
        def _():
            landed = carry_ref.at[owner, spot]
            remote(landed, landed, carry_send.at[slot, j], carry_recv.at[owner, j], twin).wait_recv()
            near_ref[slot, spot, :] += carry_ref[owner, spot, :].astype(jnp.float32)

        @pl.when((owner <= z) & (z < count - 1))
        def _():
            source = jnp.where(owner == z, count, owner)
            landed = carry_ref.at[source, spot]
            remote(landed, landed, carry_send.at[slot, j], carry_recv.at[source, j], twin).wait_recv()
            near_ref[slot, spot, :] += carry_ref[source, spot, :].astype(jnp.float32)

        value = near_ref[slot, spot, :] + sibling_ref[slot, spot, :].astype(jnp.float32)

        @pl.when(pair > 1)
        def _():
            wait_sum_send(pair - 2, i, j)

        @pl.when(owner != z)
        def _():
            sum_ref[slot, spot, :] = value.astype(jnp.bfloat16)
            carry_copy(owner, slot, j).start()

        @pl.when(owner == z)
        def _():
            sum_ref[slot, spot, :] = (value + residual_ref[spot, :].astype(jnp.float32)).astype(jnp.bfloat16)
            out_copy(slot, j).start()

    def wait_sum_send(pair, i, j):
        owner = owner_of(pair, i)
        slot = slot_of(pair, i)

        @pl.when(owner != z)
        def _():
            carry_copy(owner, slot, j).wait_send()

        @pl.when(owner == z)
        def _():
            out_copy(slot, j).wait_send()

    def first_of_line(owner):
        return ((z == 0) & (owner > z)) | ((z == count - 1) & (owner < z))

    def give_credit(pair, i):
        if pairs > 2:

            @pl.when(pair < pairs - 2)
            def _():
                pl.semaphore_signal(credit.at[slot_of(pair, i)], inc=1, device_id=twin, device_id_type=MESH)

    def finish_pair(pair, ends):
        def mine(i):
            owner = owner_of(pair, i)
            if ends:
                return owner == z
            return (owner != z) & jnp.logical_not(first_of_line(owner))

        def one_part(j, _):
            @pl.when((j < SUM_PIECES) & mine(0))
            def _():
                combine(pair, 0, j)

            @pl.when((j >= SKEW) & mine(1))
            def _():
                combine(pair, 1, j - SKEW)

            return 0

        lax.fori_loop(0, SUM_PIECES + SKEW, one_part, 0)
        for i in range(2):

            @pl.when(mine(i))
            def _():
                give_credit(pair, i)

    def start_line(pair, i, begin, end):
        def one_part(j, _):
            combine(pair, i, j)
            return 0

        lax.fori_loop(begin, end, one_part, 0)

    def project_pair(pair):
        def one_owner(i, _):
            owner = owner_of(pair, i)
            slot = slot_of(pair, i)

            def one_wait(distance, _):
                other = lax.rem(z + distance, count)
                spot = lse_ref.at[other, owner]
                remote(spot, spot, lse_send.at[0, owner], lse_recv.at[other, owner], twin).wait_recv()
                return 0

            lax.fori_loop(1, count, one_wait, 0)

            def one_block(b, _):
                spot = pl.ds(pl.multiple_of(b * block_rows, block_rows), block_rows)
                terms = [lse_ref[k, owner, b] for k in range(count)]
                top = functools.reduce(jnp.maximum, terms)
                total = sum(jnp.exp2(term - top) for term in terms)
                share = jnp.exp2(lse_ref[z, owner, b] - top) / total
                share = jnp.concatenate([share, jnp.zeros((128 - heads_local, block_rows), jnp.float32)], axis=0).T
                for head in range(heads_local):
                    columns = slice(head * head_size, (head + 1) * head_size)
                    normed_ref[spot, columns] = (
                        acc_ref[owner, spot, columns].astype(jnp.float32) * share[:, head : head + 1]
                    ).astype(jnp.bfloat16)
                return 0

            lax.fori_loop(0, blocks, one_block, 0)

            @pl.when((pair == 0) & (i == 0))
            def _():
                for k in range(tiles):
                    load_output_tile(k).wait()

                load_residual.wait()

            if pairs > 2:

                @pl.when(pair > 1)
                def _():
                    away_copy(slot).wait_send()
                    pl.semaphore_wait(credit.at[slot], 1)

            per_half = tiles // 2
            for k in range(per_half):
                away_ref[slot, :, k * tile : (k + 1) * tile] = jnp.dot(
                    normed_ref[...], output_tiles[k], preferred_element_type=jnp.float32
                ).astype(jnp.bfloat16)
            away_copy(slot).start()
            for k in range(per_half):
                near_ref[slot, :, k * tile : (k + 1) * tile] = jnp.dot(
                    normed_ref[...], output_tiles[per_half + k], preferred_element_type=jnp.float32
                )
            away_copy(slot).wait_recv()

            whole = (i == 0) | (pair == pairs - 1)

            @pl.when(first_of_line(owner))
            def _():
                start_line(pair, i, 0, jnp.where(whole, SUM_PIECES, EARLY_PIECES))

                @pl.when(whole)
                def _():
                    give_credit(pair, i)

            @pl.when((i == 0) & (pair > 0) & first_of_line(owner_of(pair - 1, 1)))
            def _():
                start_line(pair - 1, 1, 2 * EARLY_PIECES, SUM_PIECES)
                give_credit(pair - 1, 1)

            return 0

        lax.fori_loop(0, 2, one_owner, 0)

    def one_step(step, _):
        if tight:

            @pl.when(step < count)
            def _():
                attention_step(step)
        else:
            attention_step(step)

        @pl.when(step > first_pair)
        def _():
            pair = step - first_pair - 1

            @pl.when(first_of_line(owner_of(pair, 1)))
            def _():
                start_line(pair, 1, EARLY_PIECES, 2 * EARLY_PIECES)

            finish_pair(pair, False)

        if pairs > 2:

            @pl.when(step > first_pair + 1)
            def _():
                finish_pair(step - first_pair - 2, True)

        @pl.when(step >= first_pair)
        def _():
            project_pair(step - first_pair)

        return 0

    lax.fori_loop(0, first_pair + pairs, one_step, 0)
    finish_pair(pairs - 1, False)
    for pair in range(max(pairs - 2, 0), pairs):
        finish_pair(pair, True)

    for pair in range(max(pairs - 2, 0), pairs):
        for i in range(2):
            away_copy(slot_of(pair, i)).wait_send()

            def one_part(j, _):
                wait_sum_send(pair, i, j)
                return 0

            lax.fori_loop(0, SUM_PIECES, one_part, 0)
    for j in range(ROW_PIECES):

        @pl.when(z > 0)
        def _():
            own_copy(-1, j).wait_send()

        @pl.when(z < count - 1)
        def _():
            own_copy(1, j).wait_send()

    def one_owner(owner, _):
        if not tight:

            @pl.when(owner != z)
            def _():
                wait_row_sends(owner)

        def one_send(distance, _):
            lse_copy(owner, distance).wait_send()
            return 0

        lax.fori_loop(1, count, one_send, 0)
        return 0

    lax.fori_loop(0, count, one_owner, 0)
    for j in range(SUM_PIECES):
        out_copy(0, j).wait_recv()


def run_section(dims, hidden, norm_gain, w_query, query_gain, w_output, key_cache, value_cache, *small):
    count, sections, kv_local = dims
    rows, width = hidden.shape[1:]
    depth, columns = w_query.shape[1:]
    head_size = query_gain.shape[1]
    heads_local = columns // head_size
    all_blocks = small[0].shape[0]
    blocks = all_blocks // count
    block_rows = rows // blocks
    half_width = width // 2
    tile = min(512, half_width, columns)
    tiles = columns // tile
    bf16, f32 = jnp.bfloat16, jnp.float32
    fixed = 2 * (w_query.size + key_cache.size + value_cache.size) + 28 * rows * width
    tight = fixed + 2 * w_output.size + 5 * count * rows * width > 50 * 2**20
    anywhere = pl.BlockSpec(memory_space=pl.ANY)
    held = pl.BlockSpec(memory_space=pltpu.VMEM)
    dma = pltpu.SemaphoreType.DMA
    scratch = [
        pltpu.VMEM((count, rows, width), bf16),
        pltpu.VMEM((tiles, depth, tile), bf16),
        pltpu.VMEM(key_cache.shape[1:], bf16),
        pltpu.VMEM(value_cache.shape[1:], bf16),
        pltpu.VMEM((rows, width), bf16),
        pltpu.VMEM((blocks, heads_local, block_rows, head_size), bf16),
        pltpu.VMEM((count, count, blocks, heads_local, block_rows), f32),
        pltpu.VMEM((rows, half_width), bf16),
        pltpu.VMEM((4, rows, half_width), f32),
        pltpu.VMEM((4, rows, half_width), bf16),
        pltpu.VMEM((4, rows, half_width), bf16),
        pltpu.VMEM((count + 1, rows, half_width), bf16),
        pltpu.VMEM((4, rows, half_width), bf16),
        dma((4,)),
        dma((2, tiles)),
        dma((count, 2, ROW_PIECES)),
        dma((2, ROW_PIECES)),
        dma((count, ROW_PIECES)),
        dma((count, ROW_PIECES)),
        dma((count - 1, count)),
        dma((count, count)),
        dma((4,)),
        dma((4,)),
        dma((4, SUM_PIECES)),
        dma((count + 1, SUM_PIECES)),
        dma((SUM_PIECES,)),
        dma((SUM_PIECES,)),
        pltpu.SemaphoreType.REGULAR((4,)),
    ]
    if not tight:
        scratch += [
            pltpu.VMEM((count, rows, heads_local * head_size), bf16),
            pltpu.VMEM((tiles, heads_local * head_size, tile), bf16),
        ]
    return pl.pallas_call(
        functools.partial(section_kernel, (count, sections, kv_local, tight)),
        out_shape=jax.ShapeDtypeStruct((1, rows, half_width), bf16),
        in_specs=[
            anywhere,
            held,
            anywhere,
            held,
            anywhere,
            anywhere,
            anywhere,
            *[pl.BlockSpec(memory_space=pltpu.SMEM)] * len(small),
        ],
        out_specs=anywhere,
        scratch_shapes=scratch,
        compiler_params=pltpu.CompilerParams(
            collective_id=0, has_side_effects=True, vmem_limit_bytes=63 * 2**20
        ),
        name="section",
    )(hidden, norm_gain, w_query, query_gain, w_output, key_cache, value_cache, *small)


def body(
    hidden,
    norm_gain,
    w_query,
    query_gain,
    w_output,
    key_cache,
    value_cache,
    key_scale,
    value_scale,
    page_table,
    page_tokens,
    page_list,
    list_len,
):
    kv_local = key_scale.shape[2]
    count = lax.axis_size("cache")
    sections = lax.axis_size("sections")
    all_slots = lookup(page_list[0], page_table)
    all_counts = lookup(page_list[0], page_tokens)
    local_all, filled_all = plan_blocks(
        all_slots, all_counts, list_len[0], lax.axis_index("cache"), key_cache.shape[1]
    )
    return run_section(
        (count, sections, kv_local),
        hidden,
        norm_gain,
        w_query,
        query_gain,
        w_output,
        key_cache,
        value_cache,
        local_all,
        filled_all,
        key_scale.reshape(-1),
        value_scale.reshape(-1),
    )


def solution(mesh):
    return jax.shard_map(
        body,
        mesh=mesh,
        in_specs=(
            P("sections", "cache", None),
            P("sections", None),
            P("sections", None, "heads"),
            P("sections", None),
            P("sections", "heads", None),
            P("sections", "cache", None, "heads"),
            P("sections", "cache", None, "heads"),
            P("sections", "cache", "heads"),
            P("sections", "cache", "heads"),
            P(),
            P(),
            P("sections", None, None),
            P("sections", None),
        ),
        out_specs=P("sections", "cache", "heads"),
        check_vma=False,
    )
```

```python
import functools
import math

import jax
import jax.numpy as jnp
from jax import lax
from jax.experimental import pallas as pl
from jax.experimental.pallas import tpu as pltpu
from jax.sharding import PartitionSpec as P

MOST = 8
ROW_PIECES = 2
SUM_PIECES = 8
EARLY_PIECES = 3
SKEW = 2

tiny_eps = 1e-06
masked_score = -1e30
lowest_top = -1e29
MESH = pl.DeviceIdType.MESH


def plan_kernel(table_ref, token_ref, list_ref, length_ref, slot_ref, fill_ref):
    all_blocks, listed = list_ref.shape
    pages_dev = table_ref.shape[0] // lax.axis_size("cache")
    first = lax.axis_index("cache") * pages_dev

    def one_block(block, _):
        length = length_ref[block]
        for i in range(MOST + 1):
            slot_ref[block, i] = 0
            fill_ref[block, i] = 0

        def one_entry(entry, rank):
            page = list_ref[block, entry]
            local = table_ref[page] - first
            slot_ref[block, rank] = local
            fill_ref[block, rank] = token_ref[page]
            chosen = (local >= 0) & (local < pages_dev) & (entry < length)
            return rank + chosen.astype(jnp.int32)

        rank = lax.fori_loop(0, listed, one_entry, jnp.int32(0), unroll=8)
        slot_ref[block, rank] = 0
        fill_ref[block, rank] = 0
        return 0

    lax.fori_loop(0, all_blocks, one_block, 0)


def plan(page_table, page_tokens, page_list, list_len):
    shape = jax.ShapeDtypeStruct((page_list.shape[0], MOST + 1), jnp.int32)
    scalars = pl.BlockSpec(memory_space=pltpu.SMEM)
    return pl.pallas_call(
        plan_kernel,
        out_shape=(shape, shape),
        in_specs=[scalars] * 4,
        out_specs=(scalars, scalars),
        name="plan",
    )(page_table, page_tokens, page_list, list_len)


def section_kernel(
    dims,
    hidden_ref,
    norm_gain_ref,
    w_query_ref,
    query_gain_ref,
    w_output_ref,
    key_ref,
    value_ref,
    slot_ref,
    fill_ref,
    key_scale_ref,
    value_scale_ref,
    out_ref,
    rows_ref,
    query_tiles,
    keys_ref,
    values_ref,
    normed_ref,
    queries_ref,
    lse_ref,
    residual_ref,
    near_ref,
    away_ref,
    sibling_ref,
    carry_ref,
    sum_ref,
    local_sems,
    tile_sems,
    row_recv,
    own_send,
    forward_send,
    sibling_send,
    lse_send,
    lse_recv,
    away_send,
    away_recv,
    carry_send,
    carry_recv,
    out_send,
    out_recv,
    credit,
    *spare,
):
    count, sections, kv_local, tight = dims
    acc_ref, output_tiles = (rows_ref, query_tiles) if tight else spare
    z = lax.axis_index("cache")
    core = lax.axis_index("heads")
    section = lax.axis_index("sections")
    rows, width = hidden_ref.shape[1:]
    heads_local, head_size = queries_ref.shape[1], queries_ref.shape[3]
    blocks, block_rows = queries_ref.shape[0], queries_ref.shape[2]
    tiles, depth, tile = query_tiles.shape
    half_rows, half_width = rows // 2, width // 2
    piece = half_rows // ROW_PIECES
    part = rows // SUM_PIECES
    pages_dev, page_len = keys_ref.shape[:2]
    most = MOST
    group_size = heads_local // kv_local
    middle = count // 2
    first_pair = count if tight else middle
    pairs = count // 2
    twin = {"heads": 1 - core}
    following = {"sections": lax.rem(section + 1, sections)}
    previous = {"sections": lax.rem(section + sections - 1, sections)}

    def at(index):
        return {"cache": index}

    def remote(src, dst, send, recv, device):
        return pltpu.make_async_remote_copy(
            src_ref=src, dst_ref=dst, send_sem=send, recv_sem=recv, device_id=device, device_id_type=MESH
        )

    def piece_of(side, j):
        return pl.ds(pl.multiple_of(side * half_rows + j * piece, piece), piece)

    load_rows = pltpu.make_async_copy(hidden_ref.at[0], rows_ref.at[z], local_sems.at[0])
    load_keys = pltpu.make_async_copy(key_ref.at[0], keys_ref, local_sems.at[1])
    load_values = pltpu.make_async_copy(value_ref.at[0], values_ref, local_sems.at[2])
    load_residual = pltpu.make_async_copy(
        hidden_ref.at[0, :, pl.ds(pl.multiple_of(core * half_width, half_width), half_width)],
        residual_ref,
        local_sems.at[3],
    )

    def load_query_tile(i):
        return pltpu.make_async_copy(
            w_query_ref.at[0, :, pl.ds(pl.multiple_of(i * tile, tile), tile)], query_tiles.at[i], tile_sems.at[0, i]
        )

    def load_output_tile(i):
        per_half = tiles // 2
        own = jnp.where(i < per_half, 1 - core, core)
        column = own * half_width + lax.rem(i, per_half) * tile
        return pltpu.make_async_copy(
            w_output_ref.at[0, :, pl.ds(pl.multiple_of(column, tile), tile)], output_tiles.at[i], tile_sems.at[1, i]
        )

    load_rows.start()
    load_query_tile(0).start()
    barrier = pltpu.get_barrier_semaphore()
    for distance in range(1, count):
        pl.semaphore_signal(barrier, inc=1, device_id=at(lax.rem(z + distance, count)), device_id_type=MESH)
    for other in (twin, following, previous):
        pl.semaphore_signal(barrier, inc=1, device_id=other, device_id_type=MESH)
    for i in range(1, tiles):
        load_query_tile(i).start()
    load_keys.start()
    load_values.start()
    load_residual.start()
    if not tight:
        for i in range(tiles):
            load_output_tile(i).start()

    pl.semaphore_wait(barrier, count + 2)

    def own_copy(step, j):
        return remote(
            hidden_ref.at[0, piece_of(core, j)],
            rows_ref.at[z, piece_of(core, j)],
            own_send.at[(step + 1) // 2, j],
            row_recv.at[z, core, j],
            at(z + step),
        )

    def row_copy(owner, side, j, send, device):
        spot = rows_ref.at[owner, piece_of(side, j)]
        return remote(spot, spot, send, row_recv.at[owner, side, j], device)

    for j in range(ROW_PIECES):

        @pl.when(z > 0)
        def _():
            own_copy(-1, j).start()

        @pl.when(z < count - 1)
        def _():
            own_copy(1, j).start()

    def serve(distance, j):
        for step in (1, -1):
            owner = z - step * distance

            @pl.when((owner >= 0) & (owner < count))
            def _():
                row_copy(owner, core, j, forward_send.at[owner, j], twin).wait_recv()

                @pl.when((z + step >= 0) & (z + step < count))
                def _():
                    row_copy(owner, core, j, forward_send.at[owner, j], at(z + step)).start()

                row_copy(owner, core, j, sibling_send.at[owner, j], twin).start()

    def wait_row_sends(owner):
        step = jnp.where(owner < z, 1, -1)
        for j in range(ROW_PIECES):
            row_copy(owner, core, j, sibling_send.at[owner, j], twin).wait_send()

            @pl.when((z + step >= 0) & (z + step < count))
            def _():
                row_copy(owner, core, j, forward_send.at[owner, j], twin).wait_send()

    def owner_at(step):
        low = jnp.minimum(z, count - 1 - z)
        both = step <= 2 * low
        reach = jnp.where(both, (step + 1) // 2, step - low)
        right = jnp.where(both, lax.rem(step, 2) == 0, z < middle)
        return z + jnp.where(right, reach, -reach)

    def make_queries(owner, step):
        x = rows_ref[owner].astype(jnp.float32)
        inverse = lax.rsqrt(jnp.mean(x * x, axis=-1, keepdims=True) + tiny_eps)
        normed_ref[...] = (x * inverse * norm_gain_ref[...]).astype(jnp.bfloat16)

        def one_tile(i, _):
            @pl.when(step == 0)
            def _():
                load_query_tile(i).wait()

            projected = jnp.dot(normed_ref[...], query_tiles[i], preferred_element_type=jnp.float32)
            per_tile = tile // head_size
            for head in range(per_tile):
                own = projected[:, head * head_size : (head + 1) * head_size]
                turn = lax.rsqrt(jnp.mean(own * own, axis=-1, keepdims=True) + tiny_eps)
                scaled = (own * turn * query_gain_ref[...] / math.sqrt(head_size)).astype(jnp.bfloat16)
                for b in range(blocks):
                    queries_ref[b, i * per_tile + head] = scaled[b * block_rows : (b + 1) * block_rows]
            return 0

        lax.fori_loop(0, tiles, one_tile, 0)

    lanes = lax.broadcasted_iota(jnp.int32, (block_rows, 128), 1)
    together = 2

    def attend(owner, b):
        block = owner * blocks + b
        spot = pl.ds(pl.multiple_of(b * block_rows, block_rows), block_rows)
        slots = [slot_ref[block, i] for i in range(most)]
        token = lax.broadcasted_iota(jnp.int32, (1, most * page_len), 1)

        def spread(values):
            row = jnp.full(token.shape, values[0])
            for i in range(1, most):
                row = jnp.where(token >= i * page_len, values[i], row)
            return row

        keeper = token < spread([i * page_len + fill_ref[block, i] for i in range(most)])
        lse_tile = jnp.full((block_rows, 128), masked_score, jnp.float32)
        for g in range(kv_local):
            columns = slice(g * head_size, (g + 1) * head_size)
            keys = jnp.concatenate([keys_ref[slot, :, columns] for slot in slots], axis=0)
            values = jnp.concatenate([values_ref[slot, :, columns] for slot in slots], axis=0)
            key_factor = spread([key_scale_ref[g, slot] for slot in slots]) * math.log2(math.e)
            value_factor = spread([value_scale_ref[g, slot] for slot in slots])
            for j in range(0, group_size, together):
                head = g * group_size + j
                queries = queries_ref[b, head : head + together].reshape(together * block_rows, head_size)
                scores = lax.dot_general(
                    queries, keys, (((1,), (1,)), ((), ())), preferred_element_type=jnp.float32
                )
                scores = jnp.where(keeper, scores * key_factor, masked_score)
                top = jnp.maximum(jnp.max(scores, axis=-1, keepdims=True), lowest_top)
                weights = jnp.exp2(scores - top)
                total = jnp.sum(weights, axis=-1, keepdims=True)
                scaled = (weights * value_factor).astype(jnp.bfloat16)
                acc = jnp.dot(scaled, values, preferred_element_type=jnp.float32)
                some = total > 0.0
                total = jnp.where(some, total, 1.0)
                acc = acc / total
                lse = jnp.where(some, top + jnp.log2(total), masked_score)
                for k in range(together):
                    own = slice(k * block_rows, (k + 1) * block_rows)
                    place = slice((head + k) * head_size, (head + k + 1) * head_size)
                    acc_ref[owner, spot, place] = acc[own].astype(jnp.bfloat16)
                    lse_tile = jnp.where(lanes == head + k, lse[own], lse_tile)
        lse_ref[z, owner, b] = lse_tile.T[:heads_local, :]

    def lse_copy(owner, distance):
        spot = lse_ref.at[z, owner]
        other = lax.rem(z + distance, count)
        return remote(spot, spot, lse_send.at[distance - 1, owner], lse_recv.at[z, owner], at(other))

    def attention_step(step):
        owner = owner_at(step)

        @pl.when(step == 0)
        def _():
            load_rows.wait()

        @pl.when(step > 0)
        def _():
            for j in range(ROW_PIECES):
                row_copy(owner, 1 - core, j, sibling_send.at[owner, j], twin).wait_recv()
            if tight:
                wait_row_sends(owner)

        make_queries(owner, step)

        @pl.when(step == 0)
        def _():
            load_keys.wait()
            load_values.wait()

        def one_block(b, _):
            attend(owner, b)

            @pl.when((step < count - 1) & (b < blocks - 1))
            def _():
                for j in range(ROW_PIECES - 1):

                    @pl.when(b == j)
                    def _():
                        serve(step + 1, j)

            return 0

        lax.fori_loop(0, blocks, one_block, 0)

        def one_send(distance, _):
            lse_copy(owner, distance).start()
            return 0

        lax.fori_loop(1, count, one_send, 0)

        @pl.when(step < count - 1)
        def _():
            for j in range(min(ROW_PIECES, blocks) - 1, ROW_PIECES):
                serve(step + 1, j)

        if tight:

            @pl.when(step == count - 1)
            def _():
                for i in range(tiles):
                    load_output_tile(i).start()

    def owner_of(pair, i):
        upper = (z < middle) == (i == 0)
        return jnp.where(upper, middle + pair, middle - 1 - pair)

    def slot_of(pair, i):
        return 2 * (pair if pairs <= 2 else lax.rem(pair, 2)) + i

    def away_copy(i):
        return remote(away_ref.at[i], sibling_ref.at[i], away_send.at[i], away_recv.at[i], twin)

    def sum_rows(j):
        return pl.ds(pl.multiple_of(j * part, part), part)

    def carry_copy(owner, i, j):
        step = jnp.where(owner > z, 1, -1)
        target = jnp.where(owner == z - 1, count, owner)
        return remote(
            sum_ref.at[i, sum_rows(j)],
            carry_ref.at[target, sum_rows(j)],
            carry_send.at[i, j],
            carry_recv.at[target, j],
            at(z + step),
        )

    def out_copy(i, j):
        return remote(
            sum_ref.at[i, sum_rows(j)], out_ref.at[0, sum_rows(j)], out_send.at[j], out_recv.at[j], following
        )

    def combine(pair, i, j):
        owner = owner_of(pair, i)
        slot = slot_of(pair, i)
        spot = sum_rows(j)

        @pl.when((owner >= z) & (z > 0))
        def _():
            landed = carry_ref.at[owner, spot]
            remote(landed, landed, carry_send.at[slot, j], carry_recv.at[owner, j], twin).wait_recv()
            near_ref[slot, spot, :] += carry_ref[owner, spot, :].astype(jnp.float32)

        @pl.when((owner <= z) & (z < count - 1))
        def _():
            source = jnp.where(owner == z, count, owner)
            landed = carry_ref.at[source, spot]
            remote(landed, landed, carry_send.at[slot, j], carry_recv.at[source, j], twin).wait_recv()
            near_ref[slot, spot, :] += carry_ref[source, spot, :].astype(jnp.float32)

        value = near_ref[slot, spot, :] + sibling_ref[slot, spot, :].astype(jnp.float32)

        @pl.when(pair > 1)
        def _():
            wait_sum_send(pair - 2, i, j)

        @pl.when(owner != z)
        def _():
            sum_ref[slot, spot, :] = value.astype(jnp.bfloat16)
            carry_copy(owner, slot, j).start()

        @pl.when(owner == z)
        def _():
            sum_ref[slot, spot, :] = (value + residual_ref[spot, :].astype(jnp.float32)).astype(jnp.bfloat16)
            out_copy(slot, j).start()

    def wait_sum_send(pair, i, j):
        owner = owner_of(pair, i)
        slot = slot_of(pair, i)

        @pl.when(owner != z)
        def _():
            carry_copy(owner, slot, j).wait_send()

        @pl.when(owner == z)
        def _():
            out_copy(slot, j).wait_send()

    def first_of_line(owner):
        return ((z == 0) & (owner > z)) | ((z == count - 1) & (owner < z))

    def give_credit(pair, i):
        if pairs > 2:

            @pl.when(pair < pairs - 2)
            def _():
                pl.semaphore_signal(credit.at[slot_of(pair, i)], inc=1, device_id=twin, device_id_type=MESH)

    def finish_pair(pair, ends, begin=0, end=SUM_PIECES):
        def mine(i):
            owner = owner_of(pair, i)
            if ends:
                return owner == z
            return (owner != z) & jnp.logical_not(first_of_line(owner))

        def one_part(j, _):
            @pl.when((j < end) & mine(0))
            def _():
                combine(pair, 0, j)

            @pl.when((j >= begin + skew) & mine(1))
            def _():
                combine(pair, 1, j - skew)

            return 0

        skew = 0 if ends else SKEW
        lax.fori_loop(begin, end + skew, one_part, 0)
        if end == SUM_PIECES:
            for i in range(2):

                @pl.when(mine(i))
                def _():
                    give_credit(pair, i)

    def start_line(pair, i, begin, end):
        def one_part(j, _):
            combine(pair, i, j)
            return 0

        lax.fori_loop(begin, end, one_part, 0)

    def project_turn(turn):
        def one_turn(turn, _):
            pair, i = turn // 2, lax.rem(turn, 2)
            owner = owner_of(pair, i)
            slot = slot_of(pair, i)

            def one_wait(distance, _):
                other = lax.rem(z + distance, count)
                spot = lse_ref.at[other, owner]
                remote(spot, spot, lse_send.at[0, owner], lse_recv.at[other, owner], twin).wait_recv()
                return 0

            lax.fori_loop(1, count, one_wait, 0)

            def one_block(b, _):
                spot = pl.ds(pl.multiple_of(b * block_rows, block_rows), block_rows)
                terms = [lse_ref[k, owner, b] for k in range(count)]
                top = functools.reduce(jnp.maximum, terms)
                total = sum(jnp.exp2(term - top) for term in terms)
                share = jnp.exp2(lse_ref[z, owner, b] - top) / total
                share = jnp.concatenate([share, jnp.zeros((128 - heads_local, block_rows), jnp.float32)], axis=0).T
                for head in range(heads_local):
                    columns = slice(head * head_size, (head + 1) * head_size)
                    normed_ref[spot, columns] = (
                        acc_ref[owner, spot, columns].astype(jnp.float32) * share[:, head : head + 1]
                    ).astype(jnp.bfloat16)
                return 0

            lax.fori_loop(0, blocks, one_block, 0)

            @pl.when((pair == 0) & (i == 0))
            def _():
                for k in range(tiles):
                    load_output_tile(k).wait()

                load_residual.wait()

            if pairs > 2:

                @pl.when(pair > 1)
                def _():
                    away_copy(slot).wait_send()
                    pl.semaphore_wait(credit.at[slot], 1)

            per_half = tiles // 2
            for k in range(per_half):
                away_ref[slot, :, k * tile : (k + 1) * tile] = jnp.dot(
                    normed_ref[...], output_tiles[k], preferred_element_type=jnp.float32
                ).astype(jnp.bfloat16)
            away_copy(slot).start()
            for k in range(per_half):
                near_ref[slot, :, k * tile : (k + 1) * tile] = jnp.dot(
                    normed_ref[...], output_tiles[per_half + k], preferred_element_type=jnp.float32
                )
            away_copy(slot).wait_recv()

            whole = (i == 0) | (pair == pairs - 1)

            @pl.when(first_of_line(owner))
            def _():
                start_line(pair, i, 0, jnp.where(whole, SUM_PIECES, EARLY_PIECES))

                @pl.when(whole)
                def _():
                    give_credit(pair, i)

            @pl.when((i == 0) & (pair > 0) & first_of_line(owner_of(pair - 1, 1)))
            def _():
                start_line(pair - 1, 1, EARLY_PIECES, SUM_PIECES)
                give_credit(pair - 1, 1)

            return 0

        lax.fori_loop(turn, turn + 1, one_turn, 0)

    def one_step(step, _):
        if tight:

            @pl.when(step < count)
            def _():
                attention_step(step)
        else:
            attention_step(step)

        def one_turn(turn, _):
            pair = turn // 2

            @pl.when((turn >= 0) & (turn < count))
            def _():
                project_turn(turn)

            @pl.when((lax.rem(turn + 2, 2) == 1) & (turn > 0) & (turn < count - 1))
            def _():
                finish_pair(pair, False)

            if pairs > 2:

                @pl.when((lax.rem(turn + 2, 2) == 1) & (pair > 0) & (turn < count - 1))
                def _():
                    finish_pair(pair - 1, True)

            return 0

        begin = 2 * (step - first_pair) - 1
        end = jnp.where(step == first_pair + pairs - 1, count, begin + 2)
        lax.fori_loop(jnp.where(step >= first_pair, begin, 0), jnp.where(step >= first_pair, end, 0), one_turn, 0)
        return 0

    lax.fori_loop(0, first_pair + pairs, one_step, 0)
    if pairs > 1:
        finish_pair(pairs - 2, True, 0, EARLY_PIECES)
    finish_pair(pairs - 1, False)
    if pairs > 1:
        finish_pair(pairs - 2, True, EARLY_PIECES, SUM_PIECES)
    finish_pair(pairs - 1, True)

    for pair in range(max(pairs - 2, 0), pairs):
        for i in range(2):
            away_copy(slot_of(pair, i)).wait_send()

            def one_part(j, _):
                wait_sum_send(pair, i, j)
                return 0

            lax.fori_loop(0, SUM_PIECES, one_part, 0)
    for j in range(ROW_PIECES):

        @pl.when(z > 0)
        def _():
            own_copy(-1, j).wait_send()

        @pl.when(z < count - 1)
        def _():
            own_copy(1, j).wait_send()

    def one_owner(owner, _):
        if not tight:

            @pl.when(owner != z)
            def _():
                wait_row_sends(owner)

        def one_send(distance, _):
            lse_copy(owner, distance).wait_send()
            return 0

        lax.fori_loop(1, count, one_send, 0)
        return 0

    lax.fori_loop(0, count, one_owner, 0)
    for j in range(SUM_PIECES):
        out_copy(0, j).wait_recv()


def run_section(dims, hidden, norm_gain, w_query, query_gain, w_output, key_cache, value_cache, *small):
    count, sections, kv_local = dims
    rows, width = hidden.shape[1:]
    depth, columns = w_query.shape[1:]
    head_size = query_gain.shape[1]
    heads_local = columns // head_size
    all_blocks = small[0].shape[0]
    blocks = all_blocks // count
    block_rows = rows // blocks
    half_width = width // 2
    tile = min(512, half_width, columns)
    tiles = columns // tile
    bf16, f32 = jnp.bfloat16, jnp.float32
    fixed = 2 * (w_query.size + key_cache.size + value_cache.size) + 28 * rows * width
    tight = fixed + 2 * w_output.size + 5 * count * rows * width > 50 * 2**20
    anywhere = pl.BlockSpec(memory_space=pl.ANY)
    stored = pl.BlockSpec(memory_space=pltpu.HBM)
    held = pl.BlockSpec(memory_space=pltpu.VMEM)
    dma = pltpu.SemaphoreType.DMA
    scratch = [
        pltpu.VMEM((count, rows, width), bf16),
        pltpu.VMEM((tiles, depth, tile), bf16),
        pltpu.VMEM(key_cache.shape[1:], bf16),
        pltpu.VMEM(value_cache.shape[1:], bf16),
        pltpu.VMEM((rows, width), bf16),
        pltpu.VMEM((blocks, heads_local, block_rows, head_size), bf16),
        pltpu.VMEM((count, count, blocks, heads_local, block_rows), f32),
        pltpu.VMEM((rows, half_width), bf16),
        pltpu.VMEM((4, rows, half_width), f32),
        pltpu.VMEM((4, rows, half_width), bf16),
        pltpu.VMEM((4, rows, half_width), bf16),
        pltpu.VMEM((count + 1, rows, half_width), bf16),
        pltpu.VMEM((4, rows, half_width), bf16),
        dma((4,)),
        dma((2, tiles)),
        dma((count, 2, ROW_PIECES)),
        dma((2, ROW_PIECES)),
        dma((count, ROW_PIECES)),
        dma((count, ROW_PIECES)),
        dma((count - 1, count)),
        dma((count, count)),
        dma((4,)),
        dma((4,)),
        dma((4, SUM_PIECES)),
        dma((count + 1, SUM_PIECES)),
        dma((SUM_PIECES,)),
        dma((SUM_PIECES,)),
        pltpu.SemaphoreType.REGULAR((4,)),
    ]
    if not tight:
        scratch += [
            pltpu.VMEM((count, rows, heads_local * head_size), bf16),
            pltpu.VMEM((tiles, heads_local * head_size, tile), bf16),
        ]
    return pl.pallas_call(
        functools.partial(section_kernel, (count, sections, kv_local, tight)),
        out_shape=jax.ShapeDtypeStruct((1, rows, half_width), bf16),
        in_specs=[
            stored,
            held,
            stored,
            held,
            stored,
            stored,
            stored,
            *[pl.BlockSpec(memory_space=pltpu.SMEM)] * len(small),
        ],
        out_specs=anywhere,
        scratch_shapes=scratch,
        compiler_params=pltpu.CompilerParams(
            collective_id=0, has_side_effects=True, vmem_limit_bytes=(63 if tight else 52) * 2**20
        ),
        name="section",
    )(hidden, norm_gain, w_query, query_gain, w_output, key_cache, value_cache, *small)


def body(
    hidden,
    norm_gain,
    w_query,
    query_gain,
    w_output,
    key_cache,
    value_cache,
    key_scale,
    value_scale,
    page_table,
    page_tokens,
    page_list,
    list_len,
):
    kv_local = key_scale.shape[2]
    count = lax.axis_size("cache")
    sections = lax.axis_size("sections")
    slots, fills = plan(page_table, page_tokens, page_list[0], list_len[0])
    return run_section(
        (count, sections, kv_local),
        hidden,
        norm_gain,
        w_query,
        query_gain,
        w_output,
        key_cache,
        value_cache,
        slots,
        fills,
        key_scale[0].T,
        value_scale[0].T,
    )


def solution(mesh):
    return jax.shard_map(
        body,
        mesh=mesh,
        in_specs=(
            P("sections", "cache", None),
            P("sections", None),
            P("sections", None, "heads"),
            P("sections", None),
            P("sections", "heads", None),
            P("sections", "cache", None, "heads"),
            P("sections", "cache", None, "heads"),
            P("sections", "cache", "heads"),
            P("sections", "cache", "heads"),
            P(),
            P(),
            P("sections", None, None),
            P("sections", None),
        ),
        out_specs=P("sections", "cache", "heads"),
        check_vma=False,
    )
```

```python
import functools
import math

import jax
import jax.numpy as jnp
from jax import lax
from jax.experimental import pallas as pl
from jax.experimental.pallas import tpu as pltpu
from jax.sharding import PartitionSpec as P

MOST = 8
ROW_PIECES = 2
SUM_PIECES = 8
EARLY_PIECES = 3
SKEW = 2
RELAYS = (3, 5, 7)
PACK = 1024

tiny_eps = 1e-06
masked_score = -1e30
lowest_top = -1e29
MESH = pl.DeviceIdType.MESH


def plan_kernel(table_ref, token_ref, list_ref, length_ref, place_ref):
    all_blocks, listed = list_ref.shape
    pages_dev = table_ref.shape[0] // lax.axis_size("cache")
    first = lax.axis_index("cache") * pages_dev

    def one_block(block, _):
        length = length_ref[block]
        for i in range(MOST + 1):
            place_ref[block, i] = 0

        def one_entry(entry, rank):
            page = list_ref[block, entry]
            local = table_ref[page] - first
            place_ref[block, rank] = local * PACK + token_ref[page]
            chosen = (local >= 0) & (local < pages_dev) & (entry < length)
            return rank + chosen.astype(jnp.int32)

        rank = lax.fori_loop(0, listed, one_entry, jnp.int32(0), unroll=16)
        place_ref[block, rank] = 0
        return 0

    lax.fori_loop(0, all_blocks, one_block, 0)


def plan(page_table, page_tokens, page_list, list_len):
    shape = jax.ShapeDtypeStruct((page_list.shape[0], MOST + 1), jnp.int32)
    scalars = pl.BlockSpec(memory_space=pltpu.SMEM)
    return pl.pallas_call(
        plan_kernel,
        out_shape=shape,
        in_specs=[scalars] * 4,
        out_specs=scalars,
        name="plan",
    )(page_table, page_tokens, page_list, list_len)


def section_kernel(
    dims,
    hidden_ref,
    norm_gain_ref,
    w_query_ref,
    query_gain_ref,
    w_output_ref,
    key_ref,
    value_ref,
    place_ref,
    key_scale_ref,
    value_scale_ref,
    out_ref,
    rows_ref,
    query_tiles,
    keys_ref,
    values_ref,
    normed_ref,
    queries_ref,
    lse_ref,
    residual_ref,
    near_ref,
    away_ref,
    sibling_ref,
    carry_ref,
    sum_ref,
    local_sems,
    tile_sems,
    row_recv,
    own_send,
    forward_send,
    sibling_send,
    lse_send,
    lse_recv,
    away_send,
    away_recv,
    carry_send,
    carry_recv,
    out_send,
    out_recv,
    credit,
    *spare,
):
    count, sections, kv_local, tight = dims
    acc_ref, output_tiles = (rows_ref, query_tiles) if tight else spare
    z = lax.axis_index("cache")
    core = lax.axis_index("heads")
    section = lax.axis_index("sections")
    rows, width = hidden_ref.shape[1:]
    heads_local, head_size = queries_ref.shape[1], queries_ref.shape[3]
    blocks, block_rows = queries_ref.shape[0], queries_ref.shape[2]
    tiles, depth, tile = query_tiles.shape
    half_rows, half_width = rows // 2, width // 2
    piece = half_rows // ROW_PIECES
    part = rows // SUM_PIECES
    pages_dev, page_len = keys_ref.shape[:2]
    most = MOST
    group_size = heads_local // kv_local
    middle = count // 2
    first_pair = count if tight else middle
    pairs = count // 2
    twin = {"heads": 1 - core}
    following = {"sections": lax.rem(section + 1, sections)}
    previous = {"sections": lax.rem(section + sections - 1, sections)}

    def at(index):
        return {"cache": index}

    def remote(src, dst, send, recv, device):
        return pltpu.make_async_remote_copy(
            src_ref=src, dst_ref=dst, send_sem=send, recv_sem=recv, device_id=device, device_id_type=MESH
        )

    def piece_of(side, j):
        return pl.ds(pl.multiple_of(side * half_rows + j * piece, piece), piece)

    load_rows = pltpu.make_async_copy(hidden_ref.at[0], rows_ref.at[z], local_sems.at[0])
    load_keys = pltpu.make_async_copy(key_ref.at[0], keys_ref, local_sems.at[1])
    load_values = pltpu.make_async_copy(value_ref.at[0], values_ref, local_sems.at[2])
    load_residual = pltpu.make_async_copy(
        hidden_ref.at[0, :, pl.ds(pl.multiple_of(core * half_width, half_width), half_width)],
        residual_ref,
        local_sems.at[3],
    )

    def load_query_tile(i):
        return pltpu.make_async_copy(
            w_query_ref.at[0, :, pl.ds(pl.multiple_of(i * tile, tile), tile)], query_tiles.at[i], tile_sems.at[0, i]
        )

    def load_output_tile(i):
        per_half = tiles // 2
        own = jnp.where(i < per_half, 1 - core, core)
        column = own * half_width + lax.rem(i, per_half) * tile
        return pltpu.make_async_copy(
            w_output_ref.at[0, :, pl.ds(pl.multiple_of(column, tile), tile)], output_tiles.at[i], tile_sems.at[1, i]
        )

    load_rows.start()
    load_query_tile(0).start()
    barrier = pltpu.get_barrier_semaphore()
    for distance in range(1, count):
        pl.semaphore_signal(barrier, inc=1, device_id=at(lax.rem(z + distance, count)), device_id_type=MESH)
    for other in (twin, following, previous):
        pl.semaphore_signal(barrier, inc=1, device_id=other, device_id_type=MESH)
    for i in range(1, tiles):
        load_query_tile(i).start()
    load_keys.start()
    load_values.start()
    load_residual.start()
    if not tight:
        for i in range(tiles):
            load_output_tile(i).start()

    pl.semaphore_wait(barrier, count + 2)

    def own_copy(step, j):
        return remote(
            hidden_ref.at[0, piece_of(core, j)],
            rows_ref.at[z, piece_of(core, j)],
            own_send.at[(step + 1) // 2, j],
            row_recv.at[z, core, j],
            at(z + step),
        )

    def row_copy(owner, side, j, send, device):
        spot = rows_ref.at[owner, piece_of(side, j)]
        return remote(spot, spot, send, row_recv.at[owner, side, j], device)

    for j in range(ROW_PIECES):

        @pl.when(z > 0)
        def _():
            own_copy(-1, j).start()

        @pl.when(z < count - 1)
        def _():
            own_copy(1, j).start()

    def serve(distance, j):
        for step in (1, -1):
            owner = z - step * distance

            @pl.when((owner >= 0) & (owner < count))
            def _():
                row_copy(owner, core, j, forward_send.at[owner, j], twin).wait_recv()

                @pl.when((z + step >= 0) & (z + step < count))
                def _():
                    row_copy(owner, core, j, forward_send.at[owner, j], at(z + step)).start()

                row_copy(owner, core, j, sibling_send.at[owner, j], twin).start()

    def wait_row_sends(owner):
        step = jnp.where(owner < z, 1, -1)
        for j in range(ROW_PIECES):
            row_copy(owner, core, j, sibling_send.at[owner, j], twin).wait_send()

            @pl.when((z + step >= 0) & (z + step < count))
            def _():
                row_copy(owner, core, j, forward_send.at[owner, j], twin).wait_send()

    def owner_at(step):
        low = jnp.minimum(z, count - 1 - z)
        both = step <= 2 * low
        reach = jnp.where(both, (step + 1) // 2, step - low)
        right = jnp.where(both, lax.rem(step, 2) == 0, z < middle)
        return z + jnp.where(right, reach, -reach)

    def make_queries(owner, step):
        x = rows_ref[owner].astype(jnp.float32)
        inverse = lax.rsqrt(jnp.mean(x * x, axis=-1, keepdims=True) + tiny_eps)
        normed_ref[...] = (x * inverse * norm_gain_ref[...]).astype(jnp.bfloat16)

        def one_tile(i, _):
            @pl.when(step == 0)
            def _():
                load_query_tile(i).wait()

            projected = jnp.dot(normed_ref[...], query_tiles[i], preferred_element_type=jnp.float32)
            per_tile = tile // head_size
            for head in range(per_tile):
                own = projected[:, head * head_size : (head + 1) * head_size]
                turn = lax.rsqrt(jnp.mean(own * own, axis=-1, keepdims=True) + tiny_eps)
                scaled = (own * turn * query_gain_ref[...] / math.sqrt(head_size)).astype(jnp.bfloat16)
                for b in range(blocks):
                    queries_ref[b, i * per_tile + head] = scaled[b * block_rows : (b + 1) * block_rows]
            return 0

        lax.fori_loop(0, tiles, one_tile, 0)

    lanes = lax.broadcasted_iota(jnp.int32, (block_rows, 128), 1)
    together = 2

    def attend(owner, b):
        block = owner * blocks + b
        spot = pl.ds(pl.multiple_of(b * block_rows, block_rows), block_rows)
        places = [place_ref[block, i] for i in range(most)]
        slots = [place // PACK for place in places]
        fills = [lax.rem(place, PACK) for place in places]
        token = lax.broadcasted_iota(jnp.int32, (1, most * page_len), 1)

        def spread(values):
            row = jnp.full(token.shape, values[0])
            for i in range(1, most):
                row = jnp.where(token >= i * page_len, values[i], row)
            return row

        keeper = token < spread([i * page_len + fills[i] for i in range(most)])
        lse_tile = jnp.full((block_rows, 128), masked_score, jnp.float32)
        for g in range(kv_local):
            columns = slice(g * head_size, (g + 1) * head_size)
            keys = jnp.concatenate([keys_ref[slot, :, columns] for slot in slots], axis=0)
            values = jnp.concatenate([values_ref[slot, :, columns] for slot in slots], axis=0)
            key_factor = spread([key_scale_ref[g, slot] for slot in slots]) * math.log2(math.e)
            value_factor = spread([value_scale_ref[g, slot] for slot in slots])
            for j in range(0, group_size, together):
                head = g * group_size + j
                queries = queries_ref[b, head : head + together].reshape(together * block_rows, head_size)
                scores = lax.dot_general(
                    queries, keys, (((1,), (1,)), ((), ())), preferred_element_type=jnp.float32
                )
                scores = jnp.where(keeper, scores * key_factor, masked_score)
                top = jnp.maximum(jnp.max(scores, axis=-1, keepdims=True), lowest_top)
                weights = jnp.exp2(scores - top)
                total = jnp.sum(weights, axis=-1, keepdims=True)
                scaled = (weights * value_factor).astype(jnp.bfloat16)
                acc = jnp.dot(scaled, values, preferred_element_type=jnp.float32)
                some = total > 0.0
                total = jnp.where(some, total, 1.0)
                acc = acc / total
                lse = jnp.where(some, top + jnp.log2(total), masked_score)
                for k in range(together):
                    own = slice(k * block_rows, (k + 1) * block_rows)
                    place = slice((head + k) * head_size, (head + k + 1) * head_size)
                    acc_ref[owner, spot, place] = acc[own].astype(jnp.bfloat16)
                    lse_tile = jnp.where(lanes == head + k, lse[own], lse_tile)
        lse_ref[z, owner, b] = lse_tile.T[:heads_local, :]

    def lse_copy(owner, distance):
        spot = lse_ref.at[z, owner]
        other = lax.rem(z + distance, count)
        return remote(spot, spot, lse_send.at[distance - 1, owner], lse_recv.at[z, owner], at(other))

    def attention_step(step):
        owner = owner_at(step)

        @pl.when(step == 0)
        def _():
            load_rows.wait()

        @pl.when(step > 0)
        def _():
            for j in range(ROW_PIECES):
                row_copy(owner, 1 - core, j, sibling_send.at[owner, j], twin).wait_recv()
            if tight:
                wait_row_sends(owner)

        make_queries(owner, step)
        relay_early(step, 0, RELAYS[0])

        @pl.when(step == 0)
        def _():
            load_keys.wait()
            load_values.wait()

        def one_block(b, _):
            attend(owner, b)

            @pl.when((step < count - 1) & (b < blocks - 1))
            def _():
                for j in range(ROW_PIECES - 1):

                    @pl.when(b == j)
                    def _():
                        serve(step + 1, j)

            @pl.when(b == 0)
            def _():
                relay_early(step, RELAYS[0], RELAYS[1])

            return 0

        lax.fori_loop(0, blocks, one_block, 0)

        def one_send(distance, _):
            lse_copy(owner, distance).start()
            return 0

        lax.fori_loop(1, count, one_send, 0)
        relay_early(step, RELAYS[1], RELAYS[2])

        @pl.when(step < count - 1)
        def _():
            for j in range(min(ROW_PIECES, blocks) - 1, ROW_PIECES):
                serve(step + 1, j)

        if tight:

            @pl.when(step == count - 1)
            def _():
                for i in range(tiles):
                    load_output_tile(i).start()

    def owner_of(pair, i):
        upper = (z < middle) == (i == 0)
        return jnp.where(upper, middle + pair, middle - 1 - pair)

    def slot_of(pair, i):
        return 2 * (pair if pairs <= 2 else lax.rem(pair, 2)) + i

    def away_copy(i):
        return remote(away_ref.at[i], sibling_ref.at[i], away_send.at[i], away_recv.at[i], twin)

    def sum_rows(j):
        return pl.ds(pl.multiple_of(j * part, part), part)

    def carry_copy(owner, i, j):
        step = jnp.where(owner > z, 1, -1)
        target = jnp.where(owner == z - 1, count, owner)
        return remote(
            sum_ref.at[i, sum_rows(j)],
            carry_ref.at[target, sum_rows(j)],
            carry_send.at[i, j],
            carry_recv.at[target, j],
            at(z + step),
        )

    def out_copy(i, j):
        return remote(
            sum_ref.at[i, sum_rows(j)], out_ref.at[0, sum_rows(j)], out_send.at[j], out_recv.at[j], following
        )

    def combine(pair, i, j):
        owner = owner_of(pair, i)
        slot = slot_of(pair, i)
        spot = sum_rows(j)

        @pl.when((owner >= z) & (z > 0))
        def _():
            landed = carry_ref.at[owner, spot]
            remote(landed, landed, carry_send.at[slot, j], carry_recv.at[owner, j], twin).wait_recv()
            near_ref[slot, spot, :] += carry_ref[owner, spot, :].astype(jnp.float32)

        @pl.when((owner <= z) & (z < count - 1))
        def _():
            source = jnp.where(owner == z, count, owner)
            landed = carry_ref.at[source, spot]
            remote(landed, landed, carry_send.at[slot, j], carry_recv.at[source, j], twin).wait_recv()
            near_ref[slot, spot, :] += carry_ref[source, spot, :].astype(jnp.float32)

        value = near_ref[slot, spot, :] + sibling_ref[slot, spot, :].astype(jnp.float32)

        @pl.when(pair > 1)
        def _():
            wait_sum_send(pair - 2, i, j)

        @pl.when(owner != z)
        def _():
            sum_ref[slot, spot, :] = value.astype(jnp.bfloat16)
            carry_copy(owner, slot, j).start()

        @pl.when(owner == z)
        def _():
            sum_ref[slot, spot, :] = (value + residual_ref[spot, :].astype(jnp.float32)).astype(jnp.bfloat16)
            out_copy(slot, j).start()

    def wait_sum_send(pair, i, j):
        owner = owner_of(pair, i)
        slot = slot_of(pair, i)

        @pl.when(owner != z)
        def _():
            carry_copy(owner, slot, j).wait_send()

        @pl.when(owner == z)
        def _():
            out_copy(slot, j).wait_send()

    def first_of_line(owner):
        return ((z == 0) & (owner > z)) | ((z == count - 1) & (owner < z))

    def give_credit(pair, i):
        if pairs > 2:

            @pl.when(pair < pairs - 2)
            def _():
                pl.semaphore_signal(credit.at[slot_of(pair, i)], inc=1, device_id=twin, device_id_type=MESH)

    def relay_early(step, begin, end):
        if tight:
            return
        pair = step - first_pair - 1

        @pl.when((pair >= 0) & (z > 0) & (z < count - 1))
        def _():
            owner = owner_of(pair, 0)

            @pl.when(owner != z)
            def _():
                start_line(pair, 0, begin, end)

    def finish_pair(pair, ends, begin=0, end=SUM_PIECES, served=0):
        def mine(i):
            owner = owner_of(pair, i)
            if ends:
                return owner == z
            return (owner != z) & jnp.logical_not(first_of_line(owner))

        def one_part(j, _):
            @pl.when((j >= served) & (j < end) & mine(0))
            def _():
                combine(pair, 0, j)

            @pl.when((j >= begin + skew) & mine(1))
            def _():
                combine(pair, 1, j - skew)

            return 0

        skew = 0 if ends else SKEW
        lax.fori_loop(begin, end + skew, one_part, 0)
        if end == SUM_PIECES:
            for i in range(2):

                @pl.when(mine(i))
                def _():
                    give_credit(pair, i)

    def start_line(pair, i, begin, end):
        def one_part(j, _):
            combine(pair, i, j)
            return 0

        lax.fori_loop(begin, end, one_part, 0)

    def project_turn(turn):
        def one_turn(turn, _):
            pair, i = turn // 2, lax.rem(turn, 2)
            owner = owner_of(pair, i)
            slot = slot_of(pair, i)

            def one_wait(distance, _):
                other = lax.rem(z + distance, count)
                spot = lse_ref.at[other, owner]
                remote(spot, spot, lse_send.at[0, owner], lse_recv.at[other, owner], twin).wait_recv()
                return 0

            lax.fori_loop(1, count, one_wait, 0)

            def one_block(b, _):
                spot = pl.ds(pl.multiple_of(b * block_rows, block_rows), block_rows)
                terms = [lse_ref[k, owner, b] for k in range(count)]
                top = functools.reduce(jnp.maximum, terms)
                total = sum(jnp.exp2(term - top) for term in terms)
                share = jnp.exp2(lse_ref[z, owner, b] - top) / total
                share = jnp.concatenate([share, jnp.zeros((128 - heads_local, block_rows), jnp.float32)], axis=0).T
                for head in range(heads_local):
                    columns = slice(head * head_size, (head + 1) * head_size)
                    normed_ref[spot, columns] = (
                        acc_ref[owner, spot, columns].astype(jnp.float32) * share[:, head : head + 1]
                    ).astype(jnp.bfloat16)
                return 0

            lax.fori_loop(0, blocks, one_block, 0)

            @pl.when((pair == 0) & (i == 0))
            def _():
                for k in range(tiles):
                    load_output_tile(k).wait()

                load_residual.wait()

            if pairs > 2:

                @pl.when(pair > 1)
                def _():
                    away_copy(slot).wait_send()
                    pl.semaphore_wait(credit.at[slot], 1)

            per_half = tiles // 2
            for k in range(per_half):
                away_ref[slot, :, k * tile : (k + 1) * tile] = jnp.dot(
                    normed_ref[...], output_tiles[k], preferred_element_type=jnp.float32
                ).astype(jnp.bfloat16)
            away_copy(slot).start()
            for k in range(per_half):
                near_ref[slot, :, k * tile : (k + 1) * tile] = jnp.dot(
                    normed_ref[...], output_tiles[per_half + k], preferred_element_type=jnp.float32
                )
            away_copy(slot).wait_recv()

            whole = (i == 0) | (pair == pairs - 1)

            @pl.when(first_of_line(owner))
            def _():
                start_line(pair, i, 0, jnp.where(whole, SUM_PIECES, EARLY_PIECES))

                @pl.when(whole)
                def _():
                    give_credit(pair, i)

            @pl.when((i == 0) & (pair > 0) & first_of_line(owner_of(pair - 1, 1)))
            def _():
                start_line(pair - 1, 1, EARLY_PIECES, SUM_PIECES)
                give_credit(pair - 1, 1)

            return 0

        lax.fori_loop(turn, turn + 1, one_turn, 0)

    def one_step(step, _):
        if tight:

            @pl.when(step < count)
            def _():
                attention_step(step)
        else:
            attention_step(step)

        def one_turn(turn, _):
            pair = turn // 2

            @pl.when((turn >= 0) & (turn < count))
            def _():
                project_turn(turn)

            @pl.when((lax.rem(turn + 2, 2) == 1) & (turn > 0) & (turn < count - 1))
            def _():
                finish_pair(pair, False, served=0 if tight else RELAYS[2])

            if pairs > 2:

                @pl.when((lax.rem(turn + 2, 2) == 1) & (pair > 0) & (turn < count - 1))
                def _():
                    finish_pair(pair - 1, True)

            return 0

        begin = 2 * (step - first_pair) - 1
        end = jnp.where(step == first_pair + pairs - 1, count, begin + 2)
        lax.fori_loop(jnp.where(step >= first_pair, begin, 0), jnp.where(step >= first_pair, end, 0), one_turn, 0)
        return 0

    lax.fori_loop(0, first_pair + pairs, one_step, 0)
    if pairs > 1:
        finish_pair(pairs - 2, True, 0, EARLY_PIECES)
    finish_pair(pairs - 1, False)
    if pairs > 1:
        finish_pair(pairs - 2, True, EARLY_PIECES, SUM_PIECES)
    finish_pair(pairs - 1, True)

    for pair in range(max(pairs - 2, 0), pairs):
        for i in range(2):
            away_copy(slot_of(pair, i)).wait_send()

            def one_part(j, _):
                wait_sum_send(pair, i, j)
                return 0

            lax.fori_loop(0, SUM_PIECES, one_part, 0)
    for j in range(ROW_PIECES):

        @pl.when(z > 0)
        def _():
            own_copy(-1, j).wait_send()

        @pl.when(z < count - 1)
        def _():
            own_copy(1, j).wait_send()

    def one_owner(owner, _):
        if not tight:

            @pl.when(owner != z)
            def _():
                wait_row_sends(owner)

        def one_send(distance, _):
            lse_copy(owner, distance).wait_send()
            return 0

        lax.fori_loop(1, count, one_send, 0)
        return 0

    lax.fori_loop(0, count, one_owner, 0)
    for j in range(SUM_PIECES):
        out_copy(0, j).wait_recv()


def run_section(dims, hidden, norm_gain, w_query, query_gain, w_output, key_cache, value_cache, *small):
    count, sections, kv_local = dims
    rows, width = hidden.shape[1:]
    depth, columns = w_query.shape[1:]
    head_size = query_gain.shape[1]
    heads_local = columns // head_size
    all_blocks = small[0].shape[0]
    blocks = all_blocks // count
    block_rows = rows // blocks
    half_width = width // 2
    tile = min(512, half_width, columns)
    tiles = columns // tile
    bf16, f32 = jnp.bfloat16, jnp.float32
    fixed = 2 * (w_query.size + key_cache.size + value_cache.size) + 28 * rows * width
    tight = fixed + 2 * w_output.size + 5 * count * rows * width > 50 * 2**20
    anywhere = pl.BlockSpec(memory_space=pl.ANY)
    stored = pl.BlockSpec(memory_space=pltpu.HBM)
    held = pl.BlockSpec(memory_space=pltpu.VMEM)
    dma = pltpu.SemaphoreType.DMA
    scratch = [
        pltpu.VMEM((count, rows, width), bf16),
        pltpu.VMEM((tiles, depth, tile), bf16),
        pltpu.VMEM(key_cache.shape[1:], bf16),
        pltpu.VMEM(value_cache.shape[1:], bf16),
        pltpu.VMEM((rows, width), bf16),
        pltpu.VMEM((blocks, heads_local, block_rows, head_size), bf16),
        pltpu.VMEM((count, count, blocks, heads_local, block_rows), f32),
        pltpu.VMEM((rows, half_width), bf16),
        pltpu.VMEM((4, rows, half_width), f32),
        pltpu.VMEM((4, rows, half_width), bf16),
        pltpu.VMEM((4, rows, half_width), bf16),
        pltpu.VMEM((count + 1, rows, half_width), bf16),
        pltpu.VMEM((4, rows, half_width), bf16),
        dma((4,)),
        dma((2, tiles)),
        dma((count, 2, ROW_PIECES)),
        dma((2, ROW_PIECES)),
        dma((count, ROW_PIECES)),
        dma((count, ROW_PIECES)),
        dma((count - 1, count)),
        dma((count, count)),
        dma((4,)),
        dma((4,)),
        dma((4, SUM_PIECES)),
        dma((count + 1, SUM_PIECES)),
        dma((SUM_PIECES,)),
        dma((SUM_PIECES,)),
        pltpu.SemaphoreType.REGULAR((4,)),
    ]
    if not tight:
        scratch += [
            pltpu.VMEM((count, rows, heads_local * head_size), bf16),
            pltpu.VMEM((tiles, heads_local * head_size, tile), bf16),
        ]
    return pl.pallas_call(
        functools.partial(section_kernel, (count, sections, kv_local, tight)),
        out_shape=jax.ShapeDtypeStruct((1, rows, half_width), bf16),
        in_specs=[
            stored,
            held,
            stored,
            held,
            stored,
            stored,
            stored,
            *[pl.BlockSpec(memory_space=pltpu.SMEM)] * len(small),
        ],
        out_specs=anywhere,
        scratch_shapes=scratch,
        compiler_params=pltpu.CompilerParams(
            collective_id=0, has_side_effects=True, vmem_limit_bytes=63 * 2**20
        ),
        name="section",
    )(hidden, norm_gain, w_query, query_gain, w_output, key_cache, value_cache, *small)


def body(
    hidden,
    norm_gain,
    w_query,
    query_gain,
    w_output,
    key_cache,
    value_cache,
    key_scale,
    value_scale,
    page_table,
    page_tokens,
    page_list,
    list_len,
):
    kv_local = key_scale.shape[2]
    count = lax.axis_size("cache")
    sections = lax.axis_size("sections")
    places = plan(page_table, page_tokens, page_list[0], list_len[0])
    return run_section(
        (count, sections, kv_local),
        hidden,
        norm_gain,
        w_query,
        query_gain,
        w_output,
        key_cache,
        value_cache,
        places,
        key_scale[0].T,
        value_scale[0].T,
    )


def solution(mesh):
    return jax.shard_map(
        body,
        mesh=mesh,
        in_specs=(
            P("sections", "cache", None),
            P("sections", None),
            P("sections", None, "heads"),
            P("sections", None),
            P("sections", "heads", None),
            P("sections", "cache", None, "heads"),
            P("sections", "cache", None, "heads"),
            P("sections", "cache", "heads"),
            P("sections", "cache", "heads"),
            P(),
            P(),
            P("sections", None, None),
            P("sections", None),
        ),
        out_specs=P("sections", "cache", "heads"),
        check_vma=False,
    )
```

```python
import functools
import math

import jax
import jax.numpy as jnp
from jax import lax
from jax.experimental import pallas as pl
from jax.experimental.pallas import tpu as pltpu
from jax.sharding import PartitionSpec as P

MOST = 8
ROW_PIECES = 2
SUM_PIECES = 16
EARLY_PIECES = 6
SKEW = 3
RELAYS = (6, 10, 14)
PACK = 1024

tiny_eps = 1e-06
masked_score = -1e30
lowest_top = -1e29
MESH = pl.DeviceIdType.MESH


def plan_kernel(table_ref, token_ref, list_ref, length_ref, place_ref):
    all_blocks, listed = list_ref.shape
    pages_dev = table_ref.shape[0] // lax.axis_size("cache")
    first = lax.axis_index("cache") * pages_dev

    def one_block(block, _):
        length = length_ref[block]
        for i in range(MOST + 1):
            place_ref[block, i] = 0

        def one_entry(entry, rank):
            page = list_ref[block, entry]
            local = table_ref[page] - first
            place_ref[block, rank] = local * PACK + token_ref[page]
            chosen = (local >= 0) & (local < pages_dev) & (entry < length)
            return rank + chosen.astype(jnp.int32)

        rank = lax.fori_loop(0, listed, one_entry, jnp.int32(0), unroll=16)
        place_ref[block, rank] = 0
        return 0

    lax.fori_loop(0, all_blocks, one_block, 0)


def plan(page_table, page_tokens, page_list, list_len):
    shape = jax.ShapeDtypeStruct((page_list.shape[0], MOST + 1), jnp.int32)
    scalars = pl.BlockSpec(memory_space=pltpu.SMEM)
    return pl.pallas_call(
        plan_kernel,
        out_shape=shape,
        in_specs=[scalars] * 4,
        out_specs=scalars,
        name="plan",
    )(page_table, page_tokens, page_list, list_len)


def section_kernel(
    dims,
    hidden_ref,
    norm_gain_ref,
    w_query_ref,
    query_gain_ref,
    w_output_ref,
    key_ref,
    value_ref,
    place_ref,
    key_scale_ref,
    value_scale_ref,
    out_ref,
    rows_ref,
    query_tiles,
    keys_ref,
    values_ref,
    normed_ref,
    queries_ref,
    lse_ref,
    top_ref,
    residual_ref,
    near_ref,
    away_ref,
    sibling_ref,
    carry_ref,
    sum_ref,
    local_sems,
    tile_sems,
    row_recv,
    own_send,
    forward_send,
    sibling_send,
    lse_send,
    lse_recv,
    away_send,
    away_recv,
    carry_send,
    carry_recv,
    out_send,
    out_recv,
    credit,
    *spare,
):
    count, sections, kv_local, tight = dims
    acc_ref, output_tiles = (rows_ref, query_tiles) if tight else spare
    z = lax.axis_index("cache")
    core = lax.axis_index("heads")
    section = lax.axis_index("sections")
    rows, width = hidden_ref.shape[1:]
    heads_local, head_size = queries_ref.shape[1], queries_ref.shape[3]
    blocks, block_rows = queries_ref.shape[0], queries_ref.shape[2]
    tiles, depth, tile = query_tiles.shape
    half_rows, half_width = rows // 2, width // 2
    piece = half_rows // ROW_PIECES
    part = rows // SUM_PIECES
    pages_dev, page_len = keys_ref.shape[:2]
    most = MOST
    group_size = heads_local // kv_local
    middle = count // 2
    first_pair = count if tight else middle
    pairs = count // 2
    twin = {"heads": 1 - core}
    following = {"sections": lax.rem(section + 1, sections)}
    previous = {"sections": lax.rem(section + sections - 1, sections)}

    def at(index):
        return {"cache": index}

    def remote(src, dst, send, recv, device):
        return pltpu.make_async_remote_copy(
            src_ref=src, dst_ref=dst, send_sem=send, recv_sem=recv, device_id=device, device_id_type=MESH
        )

    def piece_of(side, j):
        return pl.ds(pl.multiple_of(side * half_rows + j * piece, piece), piece)

    load_rows = pltpu.make_async_copy(hidden_ref.at[0], rows_ref.at[z], local_sems.at[0])
    load_keys = pltpu.make_async_copy(key_ref.at[0], keys_ref, local_sems.at[1])
    load_values = pltpu.make_async_copy(value_ref.at[0], values_ref, local_sems.at[2])
    load_residual = pltpu.make_async_copy(
        hidden_ref.at[0, :, pl.ds(pl.multiple_of(core * half_width, half_width), half_width)],
        residual_ref,
        local_sems.at[3],
    )

    def load_query_tile(i):
        return pltpu.make_async_copy(
            w_query_ref.at[0, :, pl.ds(pl.multiple_of(i * tile, tile), tile)], query_tiles.at[i], tile_sems.at[0, i]
        )

    def load_output_tile(i):
        per_half = tiles // 2
        own = jnp.where(i < per_half, 1 - core, core)
        column = own * half_width + lax.rem(i, per_half) * tile
        return pltpu.make_async_copy(
            w_output_ref.at[0, :, pl.ds(pl.multiple_of(column, tile), tile)], output_tiles.at[i], tile_sems.at[1, i]
        )

    load_rows.start()
    load_query_tile(0).start()
    barrier = pltpu.get_barrier_semaphore()
    for distance in range(1, count):
        pl.semaphore_signal(barrier, inc=1, device_id=at(lax.rem(z + distance, count)), device_id_type=MESH)
    for other in (twin, following, previous):
        pl.semaphore_signal(barrier, inc=1, device_id=other, device_id_type=MESH)
    for i in range(1, tiles):
        load_query_tile(i).start()
    load_keys.start()
    load_values.start()
    load_residual.start()
    if not tight:
        for i in range(tiles):
            load_output_tile(i).start()

    pl.semaphore_wait(barrier, count + 2)

    def own_copy(step, j):
        return remote(
            hidden_ref.at[0, piece_of(core, j)],
            rows_ref.at[z, piece_of(core, j)],
            own_send.at[(step + 1) // 2, j],
            row_recv.at[z, core, j],
            at(z + step),
        )

    def row_copy(owner, side, j, send, device):
        spot = rows_ref.at[owner, piece_of(side, j)]
        return remote(spot, spot, send, row_recv.at[owner, side, j], device)

    for j in range(ROW_PIECES):

        @pl.when(z > 0)
        def _():
            own_copy(-1, j).start()

        @pl.when(z < count - 1)
        def _():
            own_copy(1, j).start()

    def serve(distance, j):
        for step in (1, -1):
            owner = z - step * distance

            @pl.when((owner >= 0) & (owner < count))
            def _():
                row_copy(owner, core, j, forward_send.at[owner, j], twin).wait_recv()

                @pl.when((z + step >= 0) & (z + step < count))
                def _():
                    row_copy(owner, core, j, forward_send.at[owner, j], at(z + step)).start()

                row_copy(owner, core, j, sibling_send.at[owner, j], twin).start()

    def wait_row_sends(owner):
        step = jnp.where(owner < z, 1, -1)
        for j in range(ROW_PIECES):
            row_copy(owner, core, j, sibling_send.at[owner, j], twin).wait_send()

            @pl.when((z + step >= 0) & (z + step < count))
            def _():
                row_copy(owner, core, j, forward_send.at[owner, j], twin).wait_send()

    def owner_at(step):
        low = jnp.minimum(z, count - 1 - z)
        both = step <= 2 * low
        reach = jnp.where(both, (step + 1) // 2, step - low)
        right = jnp.where(both, lax.rem(step, 2) == 0, z < middle)
        return z + jnp.where(right, reach, -reach)

    def make_queries(owner, step):
        x = rows_ref[owner].astype(jnp.float32)
        inverse = lax.rsqrt(jnp.mean(x * x, axis=-1, keepdims=True) + tiny_eps)
        normed_ref[...] = (x * inverse * norm_gain_ref[...]).astype(jnp.bfloat16)

        @pl.when(step == 0)
        def _():
            for i in range(tiles):
                load_query_tile(i).wait()

        for i in range(tiles):
            projected = jnp.dot(normed_ref[...], query_tiles[i], preferred_element_type=jnp.float32)
            per_tile = tile // head_size
            for head in range(per_tile):
                own = projected[:, head * head_size : (head + 1) * head_size]
                turn = lax.rsqrt(jnp.mean(own * own, axis=-1, keepdims=True) + tiny_eps)
                scaled = (own * turn * query_gain_ref[...] / math.sqrt(head_size)).astype(jnp.bfloat16)
                for b in range(blocks):
                    queries_ref[b, i * per_tile + head] = scaled[b * block_rows : (b + 1) * block_rows]

    lanes = lax.broadcasted_iota(jnp.int32, (block_rows, 128), 1)
    together = min(4, group_size)

    def attend(owner, b):
        block = owner * blocks + b
        spot = pl.ds(pl.multiple_of(b * block_rows, block_rows), block_rows)
        places = [place_ref[block, i] for i in range(most)]
        slots = [place // PACK for place in places]
        fills = [lax.rem(place, PACK) for place in places]
        token = lax.broadcasted_iota(jnp.int32, (1, most * page_len), 1)

        def spread(values):
            row = jnp.full(token.shape, values[0])
            for i in range(1, most):
                row = jnp.where(token >= i * page_len, values[i], row)
            return row

        keeper = token < spread([i * page_len + fills[i] for i in range(most)])
        bias = jnp.where(keeper, 0.0, masked_score)
        top_tile = jnp.zeros((block_rows, 128), jnp.float32)
        total_tile = jnp.zeros((block_rows, 128), jnp.float32)
        for g in range(kv_local):
            columns = slice(g * head_size, (g + 1) * head_size)
            keys = jnp.concatenate([keys_ref[slot, :, columns] for slot in slots], axis=0)
            values = jnp.concatenate([values_ref[slot, :, columns] for slot in slots], axis=0)
            key_factor = spread([key_scale_ref[g, slot] for slot in slots]) * math.log2(math.e)
            key_factor = jnp.where(keeper, key_factor, 0.0)
            value_factor = spread([value_scale_ref[g, slot] for slot in slots])
            for j in range(0, group_size, together):
                head = g * group_size + j
                queries = queries_ref[b, head : head + together].reshape(together * block_rows, head_size)
                scores = lax.dot_general(
                    queries, keys, (((1,), (1,)), ((), ())), preferred_element_type=jnp.float32
                )
                scores = scores * key_factor + bias
                top = jnp.maximum(jnp.max(scores, axis=-1, keepdims=True), lowest_top)
                weights = jnp.exp2(scores - top)
                total = jnp.sum(weights, axis=-1, keepdims=True)
                scaled = (weights * value_factor).astype(jnp.bfloat16)
                acc = jnp.dot(scaled, values, preferred_element_type=jnp.float32)
                for k in range(together):
                    own = slice(k * block_rows, (k + 1) * block_rows)
                    place = slice((head + k) * head_size, (head + k + 1) * head_size)
                    acc_ref[owner, spot, place] = acc[own].astype(jnp.bfloat16)
                    top_tile = jnp.where(lanes == head + k, top[own], top_tile)
                    total_tile = jnp.where(lanes == head + k, total[own], total_tile)
        top = top_tile.T[:heads_local, :]
        total = total_tile.T[:heads_local, :]
        some = total > 0.0
        top_ref[owner, b] = top
        lse_ref[z, owner, b] = jnp.where(some, top + jnp.log2(jnp.where(some, total, 1.0)), masked_score)

    def lse_copy(owner, distance):
        spot = lse_ref.at[z, owner]
        other = lax.rem(z + distance, count)
        return remote(spot, spot, lse_send.at[distance - 1, owner], lse_recv.at[z, owner], at(other))

    def attention_step(step):
        owner = owner_at(step)

        @pl.when(step == 0)
        def _():
            load_rows.wait()

        @pl.when(step > 0)
        def _():
            for j in range(ROW_PIECES):
                row_copy(owner, 1 - core, j, sibling_send.at[owner, j], twin).wait_recv()
            if tight:
                wait_row_sends(owner)

        make_queries(owner, step)
        relay_early(step, 0, RELAYS[0])

        @pl.when(step == 0)
        def _():
            load_keys.wait()
            load_values.wait()

        def one_block(b, _):
            attend(owner, b)

            @pl.when((step < count - 1) & (b < blocks - 1))
            def _():
                for j in range(ROW_PIECES - 1):

                    @pl.when(b == j)
                    def _():
                        serve(step + 1, j)

            @pl.when(b == 0)
            def _():
                relay_early(step, RELAYS[0], RELAYS[1])

            return 0

        lax.fori_loop(0, blocks, one_block, 0)

        def one_send(distance, _):
            lse_copy(owner, distance).start()
            return 0

        lax.fori_loop(1, count, one_send, 0)
        relay_early(step, RELAYS[1], RELAYS[2])

        @pl.when(step < count - 1)
        def _():
            for j in range(min(ROW_PIECES, blocks) - 1, ROW_PIECES):
                serve(step + 1, j)

        if tight:

            @pl.when(step == count - 1)
            def _():
                for i in range(tiles):
                    load_output_tile(i).start()

    def owner_of(pair, i):
        upper = (z < middle) == (i == 0)
        return jnp.where(upper, middle + pair, middle - 1 - pair)

    def slot_of(pair, i):
        return 2 * (pair if pairs <= 2 else lax.rem(pair, 2)) + i

    def away_copy(i):
        return remote(away_ref.at[i], sibling_ref.at[i], away_send.at[i], away_recv.at[i], twin)

    def sum_rows(j):
        return pl.ds(pl.multiple_of(j * part, part), part)

    def carry_copy(owner, i, j):
        step = jnp.where(owner > z, 1, -1)
        target = jnp.where(owner == z - 1, count, owner)
        return remote(
            sum_ref.at[i, sum_rows(j)],
            carry_ref.at[target, sum_rows(j)],
            carry_send.at[i, j],
            carry_recv.at[target, j],
            at(z + step),
        )

    def out_copy(i, j):
        return remote(
            sum_ref.at[i, sum_rows(j)], out_ref.at[0, sum_rows(j)], out_send.at[j], out_recv.at[j], following
        )

    def combine(pair, i, j):
        owner = owner_of(pair, i)
        slot = slot_of(pair, i)
        spot = sum_rows(j)

        @pl.when((owner >= z) & (z > 0))
        def _():
            landed = carry_ref.at[owner, spot]
            remote(landed, landed, carry_send.at[slot, j], carry_recv.at[owner, j], twin).wait_recv()
            near_ref[slot, spot, :] += carry_ref[owner, spot, :].astype(jnp.float32)

        @pl.when((owner <= z) & (z < count - 1))
        def _():
            source = jnp.where(owner == z, count, owner)
            landed = carry_ref.at[source, spot]
            remote(landed, landed, carry_send.at[slot, j], carry_recv.at[source, j], twin).wait_recv()
            near_ref[slot, spot, :] += carry_ref[source, spot, :].astype(jnp.float32)

        value = near_ref[slot, spot, :] + sibling_ref[slot, spot, :].astype(jnp.float32)

        @pl.when(pair > 1)
        def _():
            wait_sum_send(pair - 2, i, j)

        @pl.when(owner != z)
        def _():
            sum_ref[slot, spot, :] = value.astype(jnp.bfloat16)
            carry_copy(owner, slot, j).start()

        @pl.when(owner == z)
        def _():
            sum_ref[slot, spot, :] = (value + residual_ref[spot, :].astype(jnp.float32)).astype(jnp.bfloat16)
            out_copy(slot, j).start()

    def wait_sum_send(pair, i, j):
        owner = owner_of(pair, i)
        slot = slot_of(pair, i)

        @pl.when(owner != z)
        def _():
            carry_copy(owner, slot, j).wait_send()

        @pl.when(owner == z)
        def _():
            out_copy(slot, j).wait_send()

    def first_of_line(owner):
        return ((z == 0) & (owner > z)) | ((z == count - 1) & (owner < z))

    def give_credit(pair, i):
        if pairs > 2:

            @pl.when(pair < pairs - 2)
            def _():
                pl.semaphore_signal(credit.at[slot_of(pair, i)], inc=1, device_id=twin, device_id_type=MESH)

    def relay_early(step, begin, end):
        if tight:
            return
        pair = step - first_pair - 1

        @pl.when((pair >= 0) & (z > 0) & (z < count - 1))
        def _():
            owner = owner_of(pair, 0)

            @pl.when(owner != z)
            def _():
                start_line(pair, 0, begin, end)

    def finish_pair(pair, ends, begin=0, end=SUM_PIECES, served=0):
        def mine(i):
            owner = owner_of(pair, i)
            if ends:
                return owner == z
            return (owner != z) & jnp.logical_not(first_of_line(owner))

        def one_part(j, _):
            @pl.when((j >= served) & (j < end) & mine(0))
            def _():
                combine(pair, 0, j)

            @pl.when((j >= begin + skew) & mine(1))
            def _():
                combine(pair, 1, j - skew)

            return 0

        skew = 0 if ends else SKEW
        lax.fori_loop(begin, end + skew, one_part, 0)
        if end == SUM_PIECES:
            for i in range(2):

                @pl.when(mine(i))
                def _():
                    give_credit(pair, i)

    def start_line(pair, i, begin, end):
        def one_part(j, _):
            combine(pair, i, j)
            return 0

        lax.fori_loop(begin, end, one_part, 0)

    def project_turn(turn):
        def one_turn(turn, _):
            pair, i = turn // 2, lax.rem(turn, 2)
            owner = owner_of(pair, i)
            slot = slot_of(pair, i)

            def one_wait(distance, _):
                other = lax.rem(z + distance, count)
                spot = lse_ref.at[other, owner]
                remote(spot, spot, lse_send.at[0, owner], lse_recv.at[other, owner], twin).wait_recv()
                return 0

            lax.fori_loop(1, count, one_wait, 0)

            @pl.when((pair == 0) & (i == 0))
            def _():
                for k in range(tiles):
                    load_output_tile(k).wait()

                load_residual.wait()

            for b in range(blocks):
                spot = slice(b * block_rows, (b + 1) * block_rows)
                terms = [lse_ref[k, owner, b] for k in range(count)]
                top = functools.reduce(jnp.maximum, terms)
                total = sum(jnp.exp2(term - top) for term in terms)
                share = jnp.exp2(top_ref[owner, b] - top) / total
                share = jnp.concatenate([share, jnp.zeros((128 - heads_local, block_rows), jnp.float32)], axis=0).T
                share = jnp.concatenate(
                    [
                        jnp.broadcast_to(share[:, head : head + 1], (block_rows, head_size))
                        for head in range(heads_local)
                    ],
                    axis=1,
                )
                normed_ref[spot, :] = (acc_ref[owner, spot, :].astype(jnp.float32) * share).astype(jnp.bfloat16)

            if pairs > 2:

                @pl.when(pair > 1)
                def _():
                    away_copy(slot).wait_send()
                    pl.semaphore_wait(credit.at[slot], 1)

            per_half = tiles // 2
            for k in range(per_half):
                away_ref[slot, :, k * tile : (k + 1) * tile] = jnp.dot(
                    normed_ref[...], output_tiles[k], preferred_element_type=jnp.float32
                ).astype(jnp.bfloat16)
            away_copy(slot).start()
            for k in range(per_half):
                near_ref[slot, :, k * tile : (k + 1) * tile] = jnp.dot(
                    normed_ref[...], output_tiles[per_half + k], preferred_element_type=jnp.float32
                )
            away_copy(slot).wait_recv()

            whole = (i == 0) | (pair == pairs - 1)

            @pl.when(first_of_line(owner))
            def _():
                start_line(pair, i, 0, jnp.where(whole, SUM_PIECES, EARLY_PIECES))

                @pl.when(whole)
                def _():
                    give_credit(pair, i)

            @pl.when((i == 0) & (pair > 0) & first_of_line(owner_of(pair - 1, 1)))
            def _():
                start_line(pair - 1, 1, EARLY_PIECES, SUM_PIECES)
                give_credit(pair - 1, 1)

            return 0

        lax.fori_loop(turn, turn + 1, one_turn, 0)

    def one_step(step, _):
        if tight:

            @pl.when(step < count)
            def _():
                attention_step(step)
        else:
            attention_step(step)

        def one_turn(turn, _):
            pair = turn // 2

            @pl.when((turn >= 0) & (turn < count))
            def _():
                project_turn(turn)

            @pl.when((lax.rem(turn + 2, 2) == 1) & (turn > 0) & (turn < count - 1))
            def _():
                finish_pair(pair, False, served=0 if tight else RELAYS[2])

            if pairs > 2:

                @pl.when((lax.rem(turn + 2, 2) == 1) & (pair > 0) & (turn < count - 1))
                def _():
                    finish_pair(pair - 1, True)

            return 0

        begin = 2 * (step - first_pair) - 1
        end = jnp.where(step == first_pair + pairs - 1, count, begin + 2)
        lax.fori_loop(jnp.where(step >= first_pair, begin, 0), jnp.where(step >= first_pair, end, 0), one_turn, 0)
        return 0

    lax.fori_loop(0, first_pair + pairs, one_step, 0)
    if pairs > 1:
        finish_pair(pairs - 2, True, 0, EARLY_PIECES)
    finish_pair(pairs - 1, False)
    if pairs > 1:
        finish_pair(pairs - 2, True, EARLY_PIECES, SUM_PIECES)
    finish_pair(pairs - 1, True)

    for pair in range(max(pairs - 2, 0), pairs):
        for i in range(2):
            away_copy(slot_of(pair, i)).wait_send()

            def one_part(j, _):
                wait_sum_send(pair, i, j)
                return 0

            lax.fori_loop(0, SUM_PIECES, one_part, 0)
    for j in range(ROW_PIECES):

        @pl.when(z > 0)
        def _():
            own_copy(-1, j).wait_send()

        @pl.when(z < count - 1)
        def _():
            own_copy(1, j).wait_send()

    def one_owner(owner, _):
        if not tight:

            @pl.when(owner != z)
            def _():
                wait_row_sends(owner)

        def one_send(distance, _):
            lse_copy(owner, distance).wait_send()
            return 0

        lax.fori_loop(1, count, one_send, 0)
        return 0

    lax.fori_loop(0, count, one_owner, 0)
    for j in range(SUM_PIECES):
        out_copy(0, j).wait_recv()


def run_section(dims, hidden, norm_gain, w_query, query_gain, w_output, key_cache, value_cache, *small):
    count, sections, kv_local = dims
    rows, width = hidden.shape[1:]
    depth, columns = w_query.shape[1:]
    head_size = query_gain.shape[1]
    heads_local = columns // head_size
    all_blocks = small[0].shape[0]
    blocks = all_blocks // count
    block_rows = rows // blocks
    half_width = width // 2
    tile = min(512, half_width, columns)
    tiles = columns // tile
    bf16, f32 = jnp.bfloat16, jnp.float32
    fixed = 2 * (w_query.size + key_cache.size + value_cache.size) + 28 * rows * width
    tight = fixed + 2 * w_output.size + 5 * count * rows * width > 50 * 2**20
    anywhere = pl.BlockSpec(memory_space=pl.ANY)
    stored = pl.BlockSpec(memory_space=pltpu.HBM)
    held = pl.BlockSpec(memory_space=pltpu.VMEM)
    dma = pltpu.SemaphoreType.DMA
    scratch = [
        pltpu.VMEM((count, rows, width), bf16),
        pltpu.VMEM((tiles, depth, tile), bf16),
        pltpu.VMEM(key_cache.shape[1:], bf16),
        pltpu.VMEM(value_cache.shape[1:], bf16),
        pltpu.VMEM((rows, width), bf16),
        pltpu.VMEM((blocks, heads_local, block_rows, head_size), bf16),
        pltpu.VMEM((count, count, blocks, heads_local, block_rows), f32),
        pltpu.VMEM((count, blocks, heads_local, block_rows), f32),
        pltpu.VMEM((rows, half_width), bf16),
        pltpu.VMEM((4, rows, half_width), f32),
        pltpu.VMEM((4, rows, half_width), bf16),
        pltpu.VMEM((4, rows, half_width), bf16),
        pltpu.VMEM((count + 1, rows, half_width), bf16),
        pltpu.VMEM((4, rows, half_width), bf16),
        dma((4,)),
        dma((2, tiles)),
        dma((count, 2, ROW_PIECES)),
        dma((2, ROW_PIECES)),
        dma((count, ROW_PIECES)),
        dma((count, ROW_PIECES)),
        dma((count - 1, count)),
        dma((count, count)),
        dma((4,)),
        dma((4,)),
        dma((4, SUM_PIECES)),
        dma((count + 1, SUM_PIECES)),
        dma((SUM_PIECES,)),
        dma((SUM_PIECES,)),
        pltpu.SemaphoreType.REGULAR((4,)),
    ]
    if not tight:
        scratch += [
            pltpu.VMEM((count, rows, heads_local * head_size), bf16),
            pltpu.VMEM((tiles, heads_local * head_size, tile), bf16),
        ]
    return pl.pallas_call(
        functools.partial(section_kernel, (count, sections, kv_local, tight)),
        out_shape=jax.ShapeDtypeStruct((1, rows, half_width), bf16),
        in_specs=[
            stored,
            held,
            stored,
            held,
            stored,
            stored,
            stored,
            *[pl.BlockSpec(memory_space=pltpu.SMEM)] * len(small),
        ],
        out_specs=anywhere,
        scratch_shapes=scratch,
        compiler_params=pltpu.CompilerParams(
            collective_id=0, has_side_effects=True, vmem_limit_bytes=63 * 2**20
        ),
        name="section",
    )(hidden, norm_gain, w_query, query_gain, w_output, key_cache, value_cache, *small)


def body(
    hidden,
    norm_gain,
    w_query,
    query_gain,
    w_output,
    key_cache,
    value_cache,
    key_scale,
    value_scale,
    page_table,
    page_tokens,
    page_list,
    list_len,
):
    kv_local = key_scale.shape[2]
    count = lax.axis_size("cache")
    sections = lax.axis_size("sections")
    places = plan(page_table, page_tokens, page_list[0], list_len[0])
    return run_section(
        (count, sections, kv_local),
        hidden,
        norm_gain,
        w_query,
        query_gain,
        w_output,
        key_cache,
        value_cache,
        places,
        key_scale[0].T,
        value_scale[0].T,
    )


def solution(mesh):
    return jax.shard_map(
        body,
        mesh=mesh,
        in_specs=(
            P("sections", "cache", None),
            P("sections", None),
            P("sections", None, "heads"),
            P("sections", None),
            P("sections", "heads", None),
            P("sections", "cache", None, "heads"),
            P("sections", "cache", None, "heads"),
            P("sections", "cache", "heads"),
            P("sections", "cache", "heads"),
            P(),
            P(),
            P("sections", None, None),
            P("sections", None),
        ),
        out_specs=P("sections", "cache", "heads"),
        check_vma=False,
    )
```

```python
import functools
import math

import jax
import jax.numpy as jnp
from jax import lax
from jax.experimental import pallas as pl
from jax.experimental.pallas import tpu as pltpu
from jax.sharding import PartitionSpec as P

MOST = 8
ROW_PIECES = 2
SUM_PIECES = 16
EARLY_PIECES = 6
SKEW = 3
RELAYS = (3, 6, 8, 12)
PACK = 1024

tiny_eps = 1e-06
masked_score = -1e30
lowest_top = -1e29
MESH = pl.DeviceIdType.MESH


def plan_kernel(table_ref, token_ref, list_ref, length_ref, place_ref):
    all_blocks, listed = list_ref.shape
    pages_dev = table_ref.shape[0] // lax.axis_size("cache")
    first = lax.axis_index("cache") * pages_dev

    def one_block(block, _):
        length = length_ref[block]
        for i in range(MOST + 1):
            place_ref[block, i] = 0

        def one_entry(entry, rank):
            page = list_ref[block, entry]
            local = table_ref[page] - first
            place_ref[block, rank] = local * PACK + token_ref[page]
            chosen = (local >= 0) & (local < pages_dev) & (entry < length)
            return rank + chosen.astype(jnp.int32)

        rank = lax.fori_loop(0, listed, one_entry, jnp.int32(0), unroll=16)
        place_ref[block, rank] = 0
        return 0

    lax.fori_loop(0, all_blocks, one_block, 0)


def plan(page_table, page_tokens, page_list, list_len):
    shape = jax.ShapeDtypeStruct((page_list.shape[0], MOST + 1), jnp.int32)
    scalars = pl.BlockSpec(memory_space=pltpu.SMEM)
    return pl.pallas_call(
        plan_kernel,
        out_shape=shape,
        in_specs=[scalars] * 4,
        out_specs=scalars,
        name="plan",
    )(page_table, page_tokens, page_list, list_len)


def section_kernel(
    dims,
    hidden_ref,
    norm_gain_ref,
    w_query_ref,
    query_gain_ref,
    w_output_ref,
    key_ref,
    value_ref,
    place_ref,
    key_scale_ref,
    value_scale_ref,
    out_ref,
    rows_ref,
    query_tiles,
    keys_ref,
    values_ref,
    normed_ref,
    queries_ref,
    lse_ref,
    top_ref,
    residual_ref,
    near_ref,
    away_ref,
    sibling_ref,
    carry_ref,
    sum_ref,
    local_sems,
    tile_sems,
    row_recv,
    own_send,
    forward_send,
    sibling_send,
    lse_send,
    lse_recv,
    away_send,
    away_recv,
    carry_send,
    carry_recv,
    out_send,
    out_recv,
    credit,
    *spare,
):
    count, sections, kv_local, tight = dims
    acc_ref, output_tiles = (rows_ref, query_tiles) if tight else spare
    z = lax.axis_index("cache")
    core = lax.axis_index("heads")
    section = lax.axis_index("sections")
    rows, width = hidden_ref.shape[1:]
    heads_local, head_size = queries_ref.shape[1], queries_ref.shape[3]
    blocks, block_rows = queries_ref.shape[0], queries_ref.shape[2]
    tiles, depth, tile = query_tiles.shape
    half_rows, half_width = rows // 2, width // 2
    piece = half_rows // ROW_PIECES
    part = rows // SUM_PIECES
    pages_dev, page_len = keys_ref.shape[:2]
    most = MOST
    group_size = heads_local // kv_local
    middle = count // 2
    first_pair = count if tight else middle
    pairs = count // 2
    twin = {"heads": 1 - core}
    following = {"sections": lax.rem(section + 1, sections)}
    previous = {"sections": lax.rem(section + sections - 1, sections)}

    def at(index):
        return {"cache": index}

    def remote(src, dst, send, recv, device):
        return pltpu.make_async_remote_copy(
            src_ref=src, dst_ref=dst, send_sem=send, recv_sem=recv, device_id=device, device_id_type=MESH
        )

    def piece_of(side, j):
        return pl.ds(pl.multiple_of(side * half_rows + j * piece, piece), piece)

    load_rows = pltpu.make_async_copy(hidden_ref.at[0], rows_ref.at[z], local_sems.at[0])
    load_keys = pltpu.make_async_copy(key_ref.at[0], keys_ref, local_sems.at[1])
    load_values = pltpu.make_async_copy(value_ref.at[0], values_ref, local_sems.at[2])
    load_residual = pltpu.make_async_copy(
        hidden_ref.at[0, :, pl.ds(pl.multiple_of(core * half_width, half_width), half_width)],
        residual_ref,
        local_sems.at[3],
    )

    def load_query_tile(i):
        return pltpu.make_async_copy(
            w_query_ref.at[0, :, pl.ds(pl.multiple_of(i * tile, tile), tile)], query_tiles.at[i], tile_sems.at[0, i]
        )

    def load_output_tile(i):
        per_half = tiles // 2
        own = jnp.where(i < per_half, 1 - core, core)
        column = own * half_width + lax.rem(i, per_half) * tile
        return pltpu.make_async_copy(
            w_output_ref.at[0, :, pl.ds(pl.multiple_of(column, tile), tile)], output_tiles.at[i], tile_sems.at[1, i]
        )

    load_rows.start()
    load_query_tile(0).start()
    barrier = pltpu.get_barrier_semaphore()
    for distance in range(1, count):
        pl.semaphore_signal(barrier, inc=1, device_id=at(lax.rem(z + distance, count)), device_id_type=MESH)
    for other in (twin, following, previous):
        pl.semaphore_signal(barrier, inc=1, device_id=other, device_id_type=MESH)
    for i in range(1, tiles):
        load_query_tile(i).start()
    load_keys.start()
    load_values.start()
    load_residual.start()
    if not tight:
        for i in range(tiles):
            load_output_tile(i).start()

    pl.semaphore_wait(barrier, count + 2)

    def own_copy(step, j):
        return remote(
            hidden_ref.at[0, piece_of(core, j)],
            rows_ref.at[z, piece_of(core, j)],
            own_send.at[(step + 1) // 2, j],
            row_recv.at[z, core, j],
            at(z + step),
        )

    def row_copy(owner, side, j, send, device):
        spot = rows_ref.at[owner, piece_of(side, j)]
        return remote(spot, spot, send, row_recv.at[owner, side, j], device)

    for j in range(ROW_PIECES):

        @pl.when(z > 0)
        def _():
            own_copy(-1, j).start()

        @pl.when(z < count - 1)
        def _():
            own_copy(1, j).start()

    def serve(distance, j):
        for step in (1, -1):
            owner = z - step * distance

            @pl.when((owner >= 0) & (owner < count))
            def _():
                row_copy(owner, core, j, forward_send.at[owner, j], twin).wait_recv()

                @pl.when((z + step >= 0) & (z + step < count))
                def _():
                    row_copy(owner, core, j, forward_send.at[owner, j], at(z + step)).start()

                row_copy(owner, core, j, sibling_send.at[owner, j], twin).start()

    def wait_row_sends(owner):
        step = jnp.where(owner < z, 1, -1)
        for j in range(ROW_PIECES):
            row_copy(owner, core, j, sibling_send.at[owner, j], twin).wait_send()

            @pl.when((z + step >= 0) & (z + step < count))
            def _():
                row_copy(owner, core, j, forward_send.at[owner, j], twin).wait_send()

    def owner_at(step):
        low = jnp.minimum(z, count - 1 - z)
        both = step <= 2 * low
        reach = jnp.where(both, (step + 1) // 2, step - low)
        right = jnp.where(both, lax.rem(step, 2) == 0, z < middle)
        return z + jnp.where(right, reach, -reach)

    def make_queries(owner, step):
        x = rows_ref[owner].astype(jnp.float32)
        inverse = lax.rsqrt(jnp.mean(x * x, axis=-1, keepdims=True) + tiny_eps)
        normed_ref[...] = (x * inverse * norm_gain_ref[...]).astype(jnp.bfloat16)

        @pl.when(step == 0)
        def _():
            for i in range(tiles):
                load_query_tile(i).wait()

        for i in range(tiles):
            projected = jnp.dot(normed_ref[...], query_tiles[i], preferred_element_type=jnp.float32)
            per_tile = tile // head_size
            for head in range(per_tile):
                own = projected[:, head * head_size : (head + 1) * head_size]
                turn = lax.rsqrt(jnp.mean(own * own, axis=-1, keepdims=True) + tiny_eps)
                scaled = (own * turn * query_gain_ref[...] / math.sqrt(head_size)).astype(jnp.bfloat16)
                for b in range(blocks):
                    queries_ref[b, i * per_tile + head] = scaled[b * block_rows : (b + 1) * block_rows]

    lanes = lax.broadcasted_iota(jnp.int32, (block_rows, 128), 1)
    together = min(4, group_size)

    def attend(owner, b):
        block = owner * blocks + b
        spot = pl.ds(pl.multiple_of(b * block_rows, block_rows), block_rows)
        places = [place_ref[block, i] for i in range(most)]
        slots = [place // PACK for place in places]
        fills = [lax.rem(place, PACK) for place in places]
        token = lax.broadcasted_iota(jnp.int32, (1, most * page_len), 1)

        def spread(values):
            row = jnp.full(token.shape, values[0])
            for i in range(1, most):
                row = jnp.where(token >= i * page_len, values[i], row)
            return row

        keeper = token < spread([i * page_len + fills[i] for i in range(most)])
        bias = jnp.where(keeper, 0.0, masked_score)
        top_tile = jnp.zeros((block_rows, 128), jnp.float32)
        total_tile = jnp.zeros((block_rows, 128), jnp.float32)
        for g in range(kv_local):
            columns = slice(g * head_size, (g + 1) * head_size)
            keys = jnp.concatenate([keys_ref[slot, :, columns] for slot in slots], axis=0)
            values = jnp.concatenate([values_ref[slot, :, columns] for slot in slots], axis=0)
            key_factor = spread([key_scale_ref[g, slot] for slot in slots]) * math.log2(math.e)
            key_factor = jnp.where(keeper, key_factor, 0.0)
            value_factor = spread([value_scale_ref[g, slot] for slot in slots])
            for j in range(0, group_size, together):
                head = g * group_size + j
                queries = queries_ref[b, head : head + together].reshape(together * block_rows, head_size)
                scores = lax.dot_general(
                    queries, keys, (((1,), (1,)), ((), ())), preferred_element_type=jnp.float32
                )
                scores = scores * key_factor + bias
                top = jnp.maximum(jnp.max(scores, axis=-1, keepdims=True), lowest_top)
                weights = jnp.exp2(scores - top)
                total = jnp.sum(weights, axis=-1, keepdims=True)
                scaled = (weights * value_factor).astype(jnp.bfloat16)
                acc = jnp.dot(scaled, values, preferred_element_type=jnp.float32)
                for k in range(together):
                    own = slice(k * block_rows, (k + 1) * block_rows)
                    place = slice((head + k) * head_size, (head + k + 1) * head_size)
                    acc_ref[owner, spot, place] = acc[own].astype(jnp.bfloat16)
                    top_tile = jnp.where(lanes == head + k, top[own], top_tile)
                    total_tile = jnp.where(lanes == head + k, total[own], total_tile)
        top = top_tile.T[:heads_local, :]
        total = total_tile.T[:heads_local, :]
        some = total > 0.0
        top_ref[owner, b] = top
        lse_ref[z, owner, b] = jnp.where(some, top + jnp.log2(jnp.where(some, total, 1.0)), masked_score)

    def lse_copy(owner, distance):
        spot = lse_ref.at[z, owner]
        other = lax.rem(z + distance, count)
        return remote(spot, spot, lse_send.at[distance - 1, owner], lse_recv.at[z, owner], at(other))

    def attention_step(step):
        owner = owner_at(step)

        @pl.when(step == 0)
        def _():
            load_rows.wait()

        @pl.when(step > 0)
        def _():
            for j in range(ROW_PIECES):
                row_copy(owner, 1 - core, j, sibling_send.at[owner, j], twin).wait_recv()
            if tight:
                wait_row_sends(owner)

        make_queries(owner, step)
        relay_early(step, 0, RELAYS[0])

        @pl.when(step == 0)
        def _():
            load_keys.wait()
            load_values.wait()

        def one_block(b, _):
            attend(owner, b)

            @pl.when((step < count - 1) & (b < blocks - 1))
            def _():
                for j in range(ROW_PIECES - 1):

                    @pl.when(b == j)
                    def _():
                        serve(step + 1, j)

            @pl.when(b == 0)
            def _():
                relay_early(step, RELAYS[0], RELAYS[1])

            return 0

        lax.fori_loop(0, blocks, one_block, 0)

        def one_send(distance, _):
            lse_copy(owner, distance).start()
            return 0

        lax.fori_loop(1, count, one_send, 0)
        relay_early(step, RELAYS[1], RELAYS[2])

        if tight:

            @pl.when(step == count - 1)
            def _():
                for i in range(tiles):
                    load_output_tile(i).start()

    def owner_of(pair, i):
        upper = (z < middle) == (i == 0)
        return jnp.where(upper, middle + pair, middle - 1 - pair)

    def slot_of(pair, i):
        return 2 * (pair if pairs <= 2 else lax.rem(pair, 2)) + i

    def away_copy(i):
        return remote(away_ref.at[i], sibling_ref.at[i], away_send.at[i], away_recv.at[i], twin)

    def sum_rows(j):
        return pl.ds(pl.multiple_of(j * part, part), part)

    def carry_copy(owner, i, j):
        step = jnp.where(owner > z, 1, -1)
        target = jnp.where(owner == z - 1, count, owner)
        return remote(
            sum_ref.at[i, sum_rows(j)],
            carry_ref.at[target, sum_rows(j)],
            carry_send.at[i, j],
            carry_recv.at[target, j],
            at(z + step),
        )

    def out_copy(i, j):
        return remote(
            sum_ref.at[i, sum_rows(j)], out_ref.at[0, sum_rows(j)], out_send.at[j], out_recv.at[j], following
        )

    def combine(pair, i, j):
        owner = owner_of(pair, i)
        slot = slot_of(pair, i)
        spot = sum_rows(j)

        @pl.when((owner >= z) & (z > 0))
        def _():
            landed = carry_ref.at[owner, spot]
            remote(landed, landed, carry_send.at[slot, j], carry_recv.at[owner, j], twin).wait_recv()
            near_ref[slot, spot, :] += carry_ref[owner, spot, :].astype(jnp.float32)

        @pl.when((owner <= z) & (z < count - 1))
        def _():
            source = jnp.where(owner == z, count, owner)
            landed = carry_ref.at[source, spot]
            remote(landed, landed, carry_send.at[slot, j], carry_recv.at[source, j], twin).wait_recv()
            near_ref[slot, spot, :] += carry_ref[source, spot, :].astype(jnp.float32)

        value = near_ref[slot, spot, :] + sibling_ref[slot, spot, :].astype(jnp.float32)

        @pl.when(pair > 1)
        def _():
            wait_sum_send(pair - 2, i, j)

        @pl.when(owner != z)
        def _():
            sum_ref[slot, spot, :] = value.astype(jnp.bfloat16)
            carry_copy(owner, slot, j).start()

        @pl.when(owner == z)
        def _():
            sum_ref[slot, spot, :] = (value + residual_ref[spot, :].astype(jnp.float32)).astype(jnp.bfloat16)
            out_copy(slot, j).start()

    def wait_sum_send(pair, i, j):
        owner = owner_of(pair, i)
        slot = slot_of(pair, i)

        @pl.when(owner != z)
        def _():
            carry_copy(owner, slot, j).wait_send()

        @pl.when(owner == z)
        def _():
            out_copy(slot, j).wait_send()

    def first_of_line(owner):
        return ((z == 0) & (owner > z)) | ((z == count - 1) & (owner < z))

    def give_credit(pair, i):
        if pairs > 2:

            @pl.when(pair < pairs - 2)
            def _():
                pl.semaphore_signal(credit.at[slot_of(pair, i)], inc=1, device_id=twin, device_id_type=MESH)

    def relay_early(step, begin, end):
        if tight:
            return
        pair = step - first_pair - 1

        @pl.when((pair >= 0) & (z > 0) & (z < count - 1))
        def _():
            owner = owner_of(pair, 0)

            @pl.when(owner != z)
            def _():
                start_line(pair, 0, begin, end)

    def finish_pair(pair, ends, begin=0, end=SUM_PIECES, served=0):
        def mine(i):
            owner = owner_of(pair, i)
            if ends:
                return owner == z
            return (owner != z) & jnp.logical_not(first_of_line(owner))

        def one_part(j, _):
            @pl.when((j >= served) & (j < end) & mine(0))
            def _():
                combine(pair, 0, j)

            @pl.when((j >= begin + skew) & mine(1))
            def _():
                combine(pair, 1, j - skew)

            return 0

        skew = 0 if ends else SKEW
        lax.fori_loop(begin, end + skew, one_part, 0)
        if end == SUM_PIECES:
            for i in range(2):

                @pl.when(mine(i))
                def _():
                    give_credit(pair, i)

    def start_line(pair, i, begin, end):
        def one_part(j, _):
            combine(pair, i, j)
            return 0

        lax.fori_loop(begin, end, one_part, 0)

    def project_turn(turn):
        def one_turn(turn, _):
            pair, i = turn // 2, lax.rem(turn, 2)
            owner = owner_of(pair, i)
            slot = slot_of(pair, i)

            def one_wait(distance, _):
                other = lax.rem(z + distance, count)
                spot = lse_ref.at[other, owner]
                remote(spot, spot, lse_send.at[0, owner], lse_recv.at[other, owner], twin).wait_recv()
                return 0

            lax.fori_loop(1, count, one_wait, 0)

            @pl.when((pair == 0) & (i == 0))
            def _():
                for k in range(tiles):
                    load_output_tile(k).wait()

                load_residual.wait()

            for b in range(blocks):
                spot = slice(b * block_rows, (b + 1) * block_rows)
                terms = [lse_ref[k, owner, b] for k in range(count)]
                top = functools.reduce(jnp.maximum, terms)
                total = sum(jnp.exp2(term - top) for term in terms)
                share = jnp.exp2(top_ref[owner, b] - top) / total
                share = jnp.concatenate([share, jnp.zeros((128 - heads_local, block_rows), jnp.float32)], axis=0).T
                share = jnp.concatenate(
                    [
                        jnp.broadcast_to(share[:, head : head + 1], (block_rows, head_size))
                        for head in range(heads_local)
                    ],
                    axis=1,
                )
                normed_ref[spot, :] = (acc_ref[owner, spot, :].astype(jnp.float32) * share).astype(jnp.bfloat16)

            if pairs > 2:

                @pl.when(pair > 1)
                def _():
                    away_copy(slot).wait_send()
                    pl.semaphore_wait(credit.at[slot], 1)

            per_half = tiles // 2
            for k in range(per_half):
                away_ref[slot, :, k * tile : (k + 1) * tile] = jnp.dot(
                    normed_ref[...], output_tiles[k], preferred_element_type=jnp.float32
                ).astype(jnp.bfloat16)
            away_copy(slot).start()
            for k in range(per_half):
                near_ref[slot, :, k * tile : (k + 1) * tile] = jnp.dot(
                    normed_ref[...], output_tiles[per_half + k], preferred_element_type=jnp.float32
                )
            away_copy(slot).wait_recv()

            whole = (i == 0) | (pair == pairs - 1)

            @pl.when(first_of_line(owner))
            def _():
                start_line(pair, i, 0, jnp.where(whole, SUM_PIECES, EARLY_PIECES))

                @pl.when(whole)
                def _():
                    give_credit(pair, i)

            @pl.when((i == 0) & (pair > 0) & first_of_line(owner_of(pair - 1, 1)))
            def _():
                start_line(pair - 1, 1, EARLY_PIECES, SUM_PIECES)
                give_credit(pair - 1, 1)

            return 0

        lax.fori_loop(turn, turn + 1, one_turn, 0)

    def one_step(step, _):
        if tight:

            @pl.when(step < count)
            def _():
                attention_step(step)
        else:
            attention_step(step)

        def one_turn(turn, _):
            pair = turn // 2

            @pl.when((turn >= 0) & (turn < count))
            def _():
                project_turn(turn)

            @pl.when((lax.rem(turn + 2, 2) == 1) & (turn > 0) & (turn < count - 1))
            def _():
                relay_early(step, RELAYS[2], RELAYS[3])

            @pl.when((lax.rem(turn + 2, 2) == 0) & (turn > 0) & (turn < count))
            def _():
                finish_pair(pair - 1, False, served=0 if tight else RELAYS[3])

            if pairs > 2:

                @pl.when((lax.rem(turn + 2, 2) == 1) & (pair > 0) & (turn < count - 1))
                def _():
                    finish_pair(pair - 1, True)

            return 0

        begin = 2 * (step - first_pair) - 1
        end = jnp.where(step == first_pair + pairs - 1, count, begin + 2)
        lax.fori_loop(jnp.where(step >= first_pair, begin, 0), jnp.where(step >= first_pair, end, 0), one_turn, 0)

        @pl.when(step < count - 1)
        def _():
            for j in range(min(ROW_PIECES, blocks) - 1, ROW_PIECES):
                serve(step + 1, j)

        return 0

    lax.fori_loop(0, first_pair + pairs, one_step, 0)
    if pairs > 1:
        finish_pair(pairs - 2, True, 0, EARLY_PIECES)
    finish_pair(pairs - 1, False)
    if pairs > 1:
        finish_pair(pairs - 2, True, EARLY_PIECES, SUM_PIECES)
    finish_pair(pairs - 1, True)

    for pair in range(max(pairs - 2, 0), pairs):
        for i in range(2):
            away_copy(slot_of(pair, i)).wait_send()

            def one_part(j, _):
                wait_sum_send(pair, i, j)
                return 0

            lax.fori_loop(0, SUM_PIECES, one_part, 0)
    for j in range(ROW_PIECES):

        @pl.when(z > 0)
        def _():
            own_copy(-1, j).wait_send()

        @pl.when(z < count - 1)
        def _():
            own_copy(1, j).wait_send()

    def one_owner(owner, _):
        if not tight:

            @pl.when(owner != z)
            def _():
                wait_row_sends(owner)

        def one_send(distance, _):
            lse_copy(owner, distance).wait_send()
            return 0

        lax.fori_loop(1, count, one_send, 0)
        return 0

    lax.fori_loop(0, count, one_owner, 0)
    for j in range(SUM_PIECES):
        out_copy(0, j).wait_recv()


def run_section(dims, hidden, norm_gain, w_query, query_gain, w_output, key_cache, value_cache, *small):
    count, sections, kv_local = dims
    rows, width = hidden.shape[1:]
    depth, columns = w_query.shape[1:]
    head_size = query_gain.shape[1]
    heads_local = columns // head_size
    all_blocks = small[0].shape[0]
    blocks = all_blocks // count
    block_rows = rows // blocks
    half_width = width // 2
    tile = min(512, half_width, columns)
    tiles = columns // tile
    bf16, f32 = jnp.bfloat16, jnp.float32
    fixed = 2 * (w_query.size + key_cache.size + value_cache.size) + 28 * rows * width
    tight = fixed + 2 * w_output.size + 5 * count * rows * width > 50 * 2**20
    anywhere = pl.BlockSpec(memory_space=pl.ANY)
    stored = pl.BlockSpec(memory_space=pltpu.HBM)
    held = pl.BlockSpec(memory_space=pltpu.VMEM)
    dma = pltpu.SemaphoreType.DMA
    scratch = [
        pltpu.VMEM((count, rows, width), bf16),
        pltpu.VMEM((tiles, depth, tile), bf16),
        pltpu.VMEM(key_cache.shape[1:], bf16),
        pltpu.VMEM(value_cache.shape[1:], bf16),
        pltpu.VMEM((rows, width), bf16),
        pltpu.VMEM((blocks, heads_local, block_rows, head_size), bf16),
        pltpu.VMEM((count, count, blocks, heads_local, block_rows), f32),
        pltpu.VMEM((count, blocks, heads_local, block_rows), f32),
        pltpu.VMEM((rows, half_width), bf16),
        pltpu.VMEM((4, rows, half_width), f32),
        pltpu.VMEM((4, rows, half_width), bf16),
        pltpu.VMEM((4, rows, half_width), bf16),
        pltpu.VMEM((count + 1, rows, half_width), bf16),
        pltpu.VMEM((4, rows, half_width), bf16),
        dma((4,)),
        dma((2, tiles)),
        dma((count, 2, ROW_PIECES)),
        dma((2, ROW_PIECES)),
        dma((count, ROW_PIECES)),
        dma((count, ROW_PIECES)),
        dma((count - 1, count)),
        dma((count, count)),
        dma((4,)),
        dma((4,)),
        dma((4, SUM_PIECES)),
        dma((count + 1, SUM_PIECES)),
        dma((SUM_PIECES,)),
        dma((SUM_PIECES,)),
        pltpu.SemaphoreType.REGULAR((4,)),
    ]
    if not tight:
        scratch += [
            pltpu.VMEM((count, rows, heads_local * head_size), bf16),
            pltpu.VMEM((tiles, heads_local * head_size, tile), bf16),
        ]
    return pl.pallas_call(
        functools.partial(section_kernel, (count, sections, kv_local, tight)),
        out_shape=jax.ShapeDtypeStruct((1, rows, half_width), bf16),
        in_specs=[
            stored,
            held,
            stored,
            held,
            stored,
            stored,
            stored,
            *[pl.BlockSpec(memory_space=pltpu.SMEM)] * len(small),
        ],
        out_specs=anywhere,
        scratch_shapes=scratch,
        compiler_params=pltpu.CompilerParams(
            collective_id=0, has_side_effects=True, vmem_limit_bytes=63 * 2**20
        ),
        name="section",
    )(hidden, norm_gain, w_query, query_gain, w_output, key_cache, value_cache, *small)


def body(
    hidden,
    norm_gain,
    w_query,
    query_gain,
    w_output,
    key_cache,
    value_cache,
    key_scale,
    value_scale,
    page_table,
    page_tokens,
    page_list,
    list_len,
):
    kv_local = key_scale.shape[2]
    count = lax.axis_size("cache")
    sections = lax.axis_size("sections")
    places = plan(page_table, page_tokens, page_list[0], list_len[0])
    return run_section(
        (count, sections, kv_local),
        hidden,
        norm_gain,
        w_query,
        query_gain,
        w_output,
        key_cache,
        value_cache,
        places,
        key_scale[0].T,
        value_scale[0].T,
    )


def solution(mesh):
    return jax.shard_map(
        body,
        mesh=mesh,
        in_specs=(
            P("sections", "cache", None),
            P("sections", None),
            P("sections", None, "heads"),
            P("sections", None),
            P("sections", "heads", None),
            P("sections", "cache", None, "heads"),
            P("sections", "cache", None, "heads"),
            P("sections", "cache", "heads"),
            P("sections", "cache", "heads"),
            P(),
            P(),
            P("sections", None, None),
            P("sections", None),
        ),
        out_specs=P("sections", "cache", "heads"),
        check_vma=False,
    )
```

```python
import functools
import math

import jax
import jax.numpy as jnp
from jax import lax
from jax.experimental import pallas as pl
from jax.experimental.pallas import tpu as pltpu
from jax.sharding import PartitionSpec as P

MOST = 8
ROW_PIECES = 2
SUM_PIECES = 16
EARLY_PIECES = 6
SKEW = 6
RELAYS = (3, 6, 8, 12)
PACK = 1024

tiny_eps = 1e-06
masked_score = -1e30
lowest_top = -1e29
MESH = pl.DeviceIdType.MESH


def plan_kernel(table_ref, token_ref, list_ref, length_ref, place_ref):
    all_blocks, listed = list_ref.shape
    pages_dev = table_ref.shape[0] // lax.axis_size("cache")
    first = lax.axis_index("cache") * pages_dev

    def one_block(block, _):
        length = length_ref[block]
        for i in range(MOST + 1):
            place_ref[block, i] = 0

        def one_entry(entry, rank):
            page = list_ref[block, entry]
            local = table_ref[page] - first
            place_ref[block, rank] = local * PACK + token_ref[page]
            chosen = (local >= 0) & (local < pages_dev) & (entry < length)
            return rank + chosen.astype(jnp.int32)

        rank = lax.fori_loop(0, listed, one_entry, jnp.int32(0), unroll=16)
        place_ref[block, rank] = 0
        return 0

    lax.fori_loop(0, all_blocks, one_block, 0)


def plan(page_table, page_tokens, page_list, list_len):
    shape = jax.ShapeDtypeStruct((page_list.shape[0], MOST + 1), jnp.int32)
    scalars = pl.BlockSpec(memory_space=pltpu.SMEM)
    return pl.pallas_call(
        plan_kernel,
        out_shape=shape,
        in_specs=[scalars] * 4,
        out_specs=scalars,
        name="plan",
    )(page_table, page_tokens, page_list, list_len)


def section_kernel(
    dims,
    hidden_ref,
    norm_gain_ref,
    w_query_ref,
    query_gain_ref,
    w_output_ref,
    key_ref,
    value_ref,
    place_ref,
    key_scale_ref,
    value_scale_ref,
    out_ref,
    rows_ref,
    query_tiles,
    keys_ref,
    values_ref,
    normed_ref,
    queries_ref,
    lse_ref,
    top_ref,
    residual_ref,
    near_ref,
    away_ref,
    sibling_ref,
    carry_ref,
    sum_ref,
    local_sems,
    tile_sems,
    row_recv,
    own_send,
    forward_send,
    sibling_send,
    lse_send,
    lse_recv,
    away_send,
    away_recv,
    carry_send,
    carry_recv,
    out_send,
    out_recv,
    credit,
    *spare,
):
    count, sections, kv_local, tight = dims
    acc_ref, output_tiles = (rows_ref, query_tiles) if tight else spare
    z = lax.axis_index("cache")
    core = lax.axis_index("heads")
    section = lax.axis_index("sections")
    rows, width = hidden_ref.shape[1:]
    heads_local, head_size = queries_ref.shape[1], queries_ref.shape[3]
    blocks, block_rows = queries_ref.shape[0], queries_ref.shape[2]
    tiles, depth, tile = query_tiles.shape
    half_rows, half_width = rows // 2, width // 2
    piece = half_rows // ROW_PIECES
    part = rows // SUM_PIECES
    pages_dev, page_len = keys_ref.shape[:2]
    most = MOST
    group_size = heads_local // kv_local
    middle = count // 2
    first_pair = count if tight else middle
    pairs = count // 2
    twin = {"heads": 1 - core}
    following = {"sections": lax.rem(section + 1, sections)}
    previous = {"sections": lax.rem(section + sections - 1, sections)}

    def at(index):
        return {"cache": index}

    def remote(src, dst, send, recv, device):
        return pltpu.make_async_remote_copy(
            src_ref=src, dst_ref=dst, send_sem=send, recv_sem=recv, device_id=device, device_id_type=MESH
        )

    def piece_of(side, j):
        return pl.ds(pl.multiple_of(side * half_rows + j * piece, piece), piece)

    load_rows = pltpu.make_async_copy(hidden_ref.at[0], rows_ref.at[z], local_sems.at[0])
    load_keys = pltpu.make_async_copy(key_ref.at[0], keys_ref, local_sems.at[1])
    load_values = pltpu.make_async_copy(value_ref.at[0], values_ref, local_sems.at[2])
    load_residual = pltpu.make_async_copy(
        hidden_ref.at[0, :, pl.ds(pl.multiple_of(core * half_width, half_width), half_width)],
        residual_ref,
        local_sems.at[3],
    )

    def load_query_tile(i):
        return pltpu.make_async_copy(
            w_query_ref.at[0, :, pl.ds(pl.multiple_of(i * tile, tile), tile)], query_tiles.at[i], tile_sems.at[0, i]
        )

    def load_output_tile(i):
        per_half = tiles // 2
        own = jnp.where(i < per_half, 1 - core, core)
        column = own * half_width + lax.rem(i, per_half) * tile
        return pltpu.make_async_copy(
            w_output_ref.at[0, :, pl.ds(pl.multiple_of(column, tile), tile)], output_tiles.at[i], tile_sems.at[1, i]
        )

    load_rows.start()
    load_query_tile(0).start()
    barrier = pltpu.get_barrier_semaphore()
    for distance in range(1, count):
        pl.semaphore_signal(barrier, inc=1, device_id=at(lax.rem(z + distance, count)), device_id_type=MESH)
    for other in (twin, following, previous):
        pl.semaphore_signal(barrier, inc=1, device_id=other, device_id_type=MESH)
    for i in range(1, tiles):
        load_query_tile(i).start()
    load_keys.start()
    load_values.start()
    load_residual.start()
    if not tight:
        for i in range(tiles):
            load_output_tile(i).start()

    pl.semaphore_wait(barrier, count + 2)

    def own_copy(step, j):
        return remote(
            hidden_ref.at[0, piece_of(core, j)],
            rows_ref.at[z, piece_of(core, j)],
            own_send.at[(step + 1) // 2, j],
            row_recv.at[z, core, j],
            at(z + step),
        )

    def row_copy(owner, side, j, send, device):
        spot = rows_ref.at[owner, piece_of(side, j)]
        return remote(spot, spot, send, row_recv.at[owner, side, j], device)

    for j in range(ROW_PIECES):

        @pl.when(z > 0)
        def _():
            own_copy(-1, j).start()

        @pl.when(z < count - 1)
        def _():
            own_copy(1, j).start()

    def serve(distance, j):
        for step in (1, -1):
            owner = z - step * distance

            @pl.when((owner >= 0) & (owner < count))
            def _():
                row_copy(owner, core, j, forward_send.at[owner, j], twin).wait_recv()

                @pl.when((z + step >= 0) & (z + step < count))
                def _():
                    row_copy(owner, core, j, forward_send.at[owner, j], at(z + step)).start()

                row_copy(owner, core, j, sibling_send.at[owner, j], twin).start()

    def wait_row_sends(owner):
        step = jnp.where(owner < z, 1, -1)
        for j in range(ROW_PIECES):
            row_copy(owner, core, j, sibling_send.at[owner, j], twin).wait_send()

            @pl.when((z + step >= 0) & (z + step < count))
            def _():
                row_copy(owner, core, j, forward_send.at[owner, j], twin).wait_send()

    def owner_at(step):
        low = jnp.minimum(z, count - 1 - z)
        both = step <= 2 * low
        reach = jnp.where(both, (step + 1) // 2, step - low)
        right = (z < middle) == (jnp.logical_not(both) | (lax.rem(step, 2) == 1))
        return z + jnp.where(right, reach, -reach)

    def make_queries(owner, step):
        x = rows_ref[owner].astype(jnp.float32)
        inverse = lax.rsqrt(jnp.mean(x * x, axis=-1, keepdims=True) + tiny_eps)
        normed_ref[...] = (x * inverse * norm_gain_ref[...]).astype(jnp.bfloat16)

        @pl.when(step == 0)
        def _():
            for i in range(tiles):
                load_query_tile(i).wait()

        for i in range(tiles):
            projected = jnp.dot(normed_ref[...], query_tiles[i], preferred_element_type=jnp.float32)
            per_tile = tile // head_size
            for head in range(per_tile):
                own = projected[:, head * head_size : (head + 1) * head_size]
                turn = lax.rsqrt(jnp.mean(own * own, axis=-1, keepdims=True) + tiny_eps)
                scaled = (own * turn * query_gain_ref[...] / math.sqrt(head_size)).astype(jnp.bfloat16)
                for b in range(blocks):
                    queries_ref[b, i * per_tile + head] = scaled[b * block_rows : (b + 1) * block_rows]

    lanes = lax.broadcasted_iota(jnp.int32, (block_rows, 128), 1)
    together = min(4, group_size)

    def attend(owner, b):
        block = owner * blocks + b
        spot = pl.ds(pl.multiple_of(b * block_rows, block_rows), block_rows)
        places = [place_ref[block, i] for i in range(most)]
        slots = [place // PACK for place in places]
        fills = [lax.rem(place, PACK) for place in places]
        token = lax.broadcasted_iota(jnp.int32, (1, most * page_len), 1)

        def spread(values):
            row = jnp.full(token.shape, values[0])
            for i in range(1, most):
                row = jnp.where(token >= i * page_len, values[i], row)
            return row

        keeper = token < spread([i * page_len + fills[i] for i in range(most)])
        bias = jnp.where(keeper, 0.0, masked_score)
        top_tile = jnp.zeros((block_rows, 128), jnp.float32)
        total_tile = jnp.zeros((block_rows, 128), jnp.float32)
        for g in range(kv_local):
            columns = slice(g * head_size, (g + 1) * head_size)
            keys = jnp.concatenate([keys_ref[slot, :, columns] for slot in slots], axis=0)
            values = jnp.concatenate([values_ref[slot, :, columns] for slot in slots], axis=0)
            key_factor = spread([key_scale_ref[g, slot] for slot in slots]) * math.log2(math.e)
            key_factor = jnp.where(keeper, key_factor, 0.0)
            value_factor = spread([value_scale_ref[g, slot] for slot in slots])
            for j in range(0, group_size, together):
                head = g * group_size + j
                queries = queries_ref[b, head : head + together].reshape(together * block_rows, head_size)
                scores = lax.dot_general(
                    queries, keys, (((1,), (1,)), ((), ())), preferred_element_type=jnp.float32
                )
                scores = scores * key_factor + bias
                top = jnp.maximum(jnp.max(scores, axis=-1, keepdims=True), lowest_top)
                weights = jnp.exp2(scores - top)
                total = jnp.sum(weights, axis=-1, keepdims=True)
                scaled = (weights * value_factor).astype(jnp.bfloat16)
                acc = jnp.dot(scaled, values, preferred_element_type=jnp.float32)
                for k in range(together):
                    own = slice(k * block_rows, (k + 1) * block_rows)
                    place = slice((head + k) * head_size, (head + k + 1) * head_size)
                    acc_ref[owner, spot, place] = acc[own].astype(jnp.bfloat16)
                    top_tile = jnp.where(lanes == head + k, top[own], top_tile)
                    total_tile = jnp.where(lanes == head + k, total[own], total_tile)
        top = top_tile.T[:heads_local, :]
        total = total_tile.T[:heads_local, :]
        some = total > 0.0
        top_ref[owner, b] = top
        lse_ref[z, owner, b] = jnp.where(some, top + jnp.log2(jnp.where(some, total, 1.0)), masked_score)

    def lse_copy(owner, distance):
        spot = lse_ref.at[z, owner]
        other = lax.rem(z + distance, count)
        return remote(spot, spot, lse_send.at[distance - 1, owner], lse_recv.at[z, owner], at(other))

    def attention_step(step):
        owner = owner_at(step)

        @pl.when(step == 0)
        def _():
            load_rows.wait()

        @pl.when(step > 0)
        def _():
            for j in range(ROW_PIECES):
                row_copy(owner, 1 - core, j, sibling_send.at[owner, j], twin).wait_recv()
            if tight:
                wait_row_sends(owner)

        make_queries(owner, step)
        relay_early(step, 0, RELAYS[0])

        @pl.when(step == 0)
        def _():
            load_keys.wait()
            load_values.wait()

        def one_block(b, _):
            attend(owner, b)

            @pl.when((step < count - 1) & (b < blocks - 1))
            def _():
                for j in range(ROW_PIECES - 1):

                    @pl.when(b == j)
                    def _():
                        serve(step + 1, j)

            @pl.when(b == 0)
            def _():
                relay_early(step, RELAYS[0], RELAYS[1])

            return 0

        lax.fori_loop(0, blocks, one_block, 0)

        def one_send(distance, _):
            lse_copy(owner, distance).start()
            return 0

        lax.fori_loop(1, count, one_send, 0)
        relay_early(step, RELAYS[1], RELAYS[2])

        if tight:

            @pl.when(step == count - 1)
            def _():
                for i in range(tiles):
                    load_output_tile(i).start()

    def owner_of(pair, i):
        upper = (z < middle) == (i == 0)
        return jnp.where(upper, middle + pair, middle - 1 - pair)

    def slot_of(pair, i):
        return 2 * (pair if pairs <= 2 else lax.rem(pair, 2)) + i

    def away_copy(i, k):
        columns = pl.ds(k * tile, tile)
        return remote(
            away_ref.at[i, :, columns], sibling_ref.at[i, :, columns], away_send.at[i, k], away_recv.at[i, k], twin
        )

    def sum_rows(j):
        return pl.ds(pl.multiple_of(j * part, part), part)

    def carry_copy(owner, i, j):
        step = jnp.where(owner > z, 1, -1)
        target = jnp.where(owner == z - 1, count, owner)
        return remote(
            sum_ref.at[i, sum_rows(j)],
            carry_ref.at[target, sum_rows(j)],
            carry_send.at[i, j],
            carry_recv.at[target, j],
            at(z + step),
        )

    def out_copy(i, j):
        return remote(
            sum_ref.at[i, sum_rows(j)], out_ref.at[0, sum_rows(j)], out_send.at[j], out_recv.at[j], following
        )

    def combine(pair, i, j):
        owner = owner_of(pair, i)
        slot = slot_of(pair, i)
        spot = sum_rows(j)

        @pl.when((owner >= z) & (z > 0))
        def _():
            landed = carry_ref.at[owner, spot]
            remote(landed, landed, carry_send.at[slot, j], carry_recv.at[owner, j], twin).wait_recv()
            near_ref[slot, spot, :] += carry_ref[owner, spot, :].astype(jnp.float32)

        @pl.when((owner <= z) & (z < count - 1))
        def _():
            source = jnp.where(owner == z, count, owner)
            landed = carry_ref.at[source, spot]
            remote(landed, landed, carry_send.at[slot, j], carry_recv.at[source, j], twin).wait_recv()
            near_ref[slot, spot, :] += carry_ref[source, spot, :].astype(jnp.float32)

        value = near_ref[slot, spot, :] + sibling_ref[slot, spot, :].astype(jnp.float32)

        @pl.when(pair > 1)
        def _():
            wait_sum_send(pair - 2, i, j)

        @pl.when(owner != z)
        def _():
            sum_ref[slot, spot, :] = value.astype(jnp.bfloat16)
            carry_copy(owner, slot, j).start()

        @pl.when(owner == z)
        def _():
            sum_ref[slot, spot, :] = (value + residual_ref[spot, :].astype(jnp.float32)).astype(jnp.bfloat16)
            out_copy(slot, j).start()

    def wait_sum_send(pair, i, j):
        owner = owner_of(pair, i)
        slot = slot_of(pair, i)

        @pl.when(owner != z)
        def _():
            carry_copy(owner, slot, j).wait_send()

        @pl.when(owner == z)
        def _():
            out_copy(slot, j).wait_send()

    def first_of_line(owner):
        return ((z == 0) & (owner > z)) | ((z == count - 1) & (owner < z))

    def give_credit(pair, i):
        if pairs > 2:

            @pl.when(pair < pairs - 2)
            def _():
                pl.semaphore_signal(credit.at[slot_of(pair, i)], inc=1, device_id=twin, device_id_type=MESH)

    def relay_early(step, begin, end):
        if tight:
            return
        pair = step - first_pair - 1

        @pl.when((pair >= 0) & (z > 0) & (z < count - 1))
        def _():
            owner = owner_of(pair, 0)

            @pl.when(owner != z)
            def _():
                start_line(pair, 0, begin, end)

    def finish_pair(pair, ends, begin=0, end=SUM_PIECES, served=0):
        def mine(i):
            owner = owner_of(pair, i)
            if ends:
                return owner == z
            return (owner != z) & jnp.logical_not(first_of_line(owner))

        def one_part(j, _):
            @pl.when((j >= served) & (j < end) & mine(0))
            def _():
                combine(pair, 0, j)

            @pl.when((j >= begin + skew) & mine(1))
            def _():
                combine(pair, 1, j - skew)

            return 0

        skew = 0 if ends else SKEW
        lax.fori_loop(begin, end + skew, one_part, 0)
        if end == SUM_PIECES:
            for i in range(2):

                @pl.when(mine(i))
                def _():
                    give_credit(pair, i)

    def start_line(pair, i, begin, end):
        def one_part(j, _):
            combine(pair, i, j)
            return 0

        lax.fori_loop(begin, end, one_part, 0)

    def project_turn(turn):
        def one_turn(turn, _):
            pair, i = turn // 2, lax.rem(turn, 2)
            owner = owner_of(pair, i)
            slot = slot_of(pair, i)

            def one_wait(distance, _):
                other = lax.rem(z + distance, count)
                spot = lse_ref.at[other, owner]
                remote(spot, spot, lse_send.at[0, owner], lse_recv.at[other, owner], twin).wait_recv()
                return 0

            lax.fori_loop(1, count, one_wait, 0)

            @pl.when((pair == 0) & (i == 0))
            def _():
                for k in range(tiles):
                    load_output_tile(k).wait()

                load_residual.wait()

            for b in range(blocks):
                spot = slice(b * block_rows, (b + 1) * block_rows)
                terms = [lse_ref[k, owner, b] for k in range(count)]
                top = functools.reduce(jnp.maximum, terms)
                total = sum(jnp.exp2(term - top) for term in terms)
                share = jnp.exp2(top_ref[owner, b] - top) / total
                share = jnp.concatenate([share, jnp.zeros((128 - heads_local, block_rows), jnp.float32)], axis=0).T
                share = jnp.concatenate(
                    [
                        jnp.broadcast_to(share[:, head : head + 1], (block_rows, head_size))
                        for head in range(heads_local)
                    ],
                    axis=1,
                )
                normed_ref[spot, :] = (acc_ref[owner, spot, :].astype(jnp.float32) * share).astype(jnp.bfloat16)

            if pairs > 2:

                @pl.when(pair > 1)
                def _():
                    for k in range(tiles // 2):
                        away_copy(slot, k).wait_send()
                    pl.semaphore_wait(credit.at[slot], 1)

            per_half = tiles // 2
            for k in range(per_half):
                away_ref[slot, :, k * tile : (k + 1) * tile] = jnp.dot(
                    normed_ref[...], output_tiles[k], preferred_element_type=jnp.float32
                ).astype(jnp.bfloat16)
                away_copy(slot, k).start()
            for k in range(per_half):
                near_ref[slot, :, k * tile : (k + 1) * tile] = jnp.dot(
                    normed_ref[...], output_tiles[per_half + k], preferred_element_type=jnp.float32
                )
            for k in range(per_half):
                away_copy(slot, k).wait_recv()

            whole = (i == 0) | (pair == pairs - 1)

            @pl.when(first_of_line(owner))
            def _():
                start_line(pair, i, 0, jnp.where(whole, SUM_PIECES, EARLY_PIECES))

                @pl.when(whole)
                def _():
                    give_credit(pair, i)

            @pl.when((i == 0) & (pair > 0) & first_of_line(owner_of(pair - 1, 1)))
            def _():
                start_line(pair - 1, 1, EARLY_PIECES, SUM_PIECES)
                give_credit(pair - 1, 1)

            return 0

        lax.fori_loop(turn, turn + 1, one_turn, 0)

    def one_step(step, _):
        if tight:

            @pl.when(step < count)
            def _():
                attention_step(step)
        else:
            attention_step(step)

        def one_turn(turn, _):
            pair = turn // 2

            @pl.when((turn >= 0) & (turn < count))
            def _():
                project_turn(turn)

            @pl.when((lax.rem(turn + 2, 2) == 1) & (turn > 0) & (turn < count - 1))
            def _():
                relay_early(step, RELAYS[2], RELAYS[3])

            @pl.when((lax.rem(turn + 2, 2) == 0) & (turn > 0) & (turn < count))
            def _():
                finish_pair(pair - 1, False, served=0 if tight else RELAYS[3])

            if pairs > 2:

                @pl.when((lax.rem(turn + 2, 2) == 1) & (pair > 0) & (turn < count - 1))
                def _():
                    finish_pair(pair - 1, True)

            return 0

        begin = 2 * (step - first_pair) - 1
        end = jnp.where(step == first_pair + pairs - 1, count, begin + 2)
        lax.fori_loop(jnp.where(step >= first_pair, begin, 0), jnp.where(step >= first_pair, end, 0), one_turn, 0)

        @pl.when(step < count - 1)
        def _():
            for j in range(min(ROW_PIECES, blocks) - 1, ROW_PIECES):
                serve(step + 1, j)

        return 0

    lax.fori_loop(0, first_pair + pairs, one_step, 0)
    if pairs > 1:
        finish_pair(pairs - 2, True, 0, EARLY_PIECES)
    finish_pair(pairs - 1, False)
    if pairs > 1:
        finish_pair(pairs - 2, True, EARLY_PIECES, SUM_PIECES)
    finish_pair(pairs - 1, True)

    for pair in range(max(pairs - 2, 0), pairs):
        for i in range(2):
            for k in range(tiles // 2):
                away_copy(slot_of(pair, i), k).wait_send()

            def one_part(j, _):
                wait_sum_send(pair, i, j)
                return 0

            lax.fori_loop(0, SUM_PIECES, one_part, 0)
    for j in range(ROW_PIECES):

        @pl.when(z > 0)
        def _():
            own_copy(-1, j).wait_send()

        @pl.when(z < count - 1)
        def _():
            own_copy(1, j).wait_send()

    def one_owner(owner, _):
        if not tight:

            @pl.when(owner != z)
            def _():
                wait_row_sends(owner)

        def one_send(distance, _):
            lse_copy(owner, distance).wait_send()
            return 0

        lax.fori_loop(1, count, one_send, 0)
        return 0

    lax.fori_loop(0, count, one_owner, 0)
    for j in range(SUM_PIECES):
        out_copy(0, j).wait_recv()


def run_section(dims, hidden, norm_gain, w_query, query_gain, w_output, key_cache, value_cache, *small):
    count, sections, kv_local = dims
    rows, width = hidden.shape[1:]
    depth, columns = w_query.shape[1:]
    head_size = query_gain.shape[1]
    heads_local = columns // head_size
    all_blocks = small[0].shape[0]
    blocks = all_blocks // count
    block_rows = rows // blocks
    half_width = width // 2
    tile = min(512, half_width, columns)
    tiles = columns // tile
    bf16, f32 = jnp.bfloat16, jnp.float32
    fixed = 2 * (w_query.size + key_cache.size + value_cache.size) + 28 * rows * width
    tight = fixed + 2 * w_output.size + 5 * count * rows * width > 50 * 2**20
    anywhere = pl.BlockSpec(memory_space=pl.ANY)
    stored = pl.BlockSpec(memory_space=pltpu.HBM)
    held = pl.BlockSpec(memory_space=pltpu.VMEM)
    dma = pltpu.SemaphoreType.DMA
    scratch = [
        pltpu.VMEM((count, rows, width), bf16),
        pltpu.VMEM((tiles, depth, tile), bf16),
        pltpu.VMEM(key_cache.shape[1:], bf16),
        pltpu.VMEM(value_cache.shape[1:], bf16),
        pltpu.VMEM((rows, width), bf16),
        pltpu.VMEM((blocks, heads_local, block_rows, head_size), bf16),
        pltpu.VMEM((count, count, blocks, heads_local, block_rows), f32),
        pltpu.VMEM((count, blocks, heads_local, block_rows), f32),
        pltpu.VMEM((rows, half_width), bf16),
        pltpu.VMEM((4, rows, half_width), f32),
        pltpu.VMEM((4, rows, half_width), bf16),
        pltpu.VMEM((4, rows, half_width), bf16),
        pltpu.VMEM((count + 1, rows, half_width), bf16),
        pltpu.VMEM((4, rows, half_width), bf16),
        dma((4,)),
        dma((2, tiles)),
        dma((count, 2, ROW_PIECES)),
        dma((2, ROW_PIECES)),
        dma((count, ROW_PIECES)),
        dma((count, ROW_PIECES)),
        dma((count - 1, count)),
        dma((count, count)),
        dma((4, tiles // 2)),
        dma((4, tiles // 2)),
        dma((4, SUM_PIECES)),
        dma((count + 1, SUM_PIECES)),
        dma((SUM_PIECES,)),
        dma((SUM_PIECES,)),
        pltpu.SemaphoreType.REGULAR((4,)),
    ]
    if not tight:
        scratch += [
            pltpu.VMEM((count, rows, heads_local * head_size), bf16),
            pltpu.VMEM((tiles, heads_local * head_size, tile), bf16),
        ]
    return pl.pallas_call(
        functools.partial(section_kernel, (count, sections, kv_local, tight)),
        out_shape=jax.ShapeDtypeStruct((1, rows, half_width), bf16),
        in_specs=[
            stored,
            held,
            stored,
            held,
            stored,
            stored,
            stored,
            *[pl.BlockSpec(memory_space=pltpu.SMEM)] * len(small),
        ],
        out_specs=anywhere,
        scratch_shapes=scratch,
        compiler_params=pltpu.CompilerParams(
            collective_id=0, has_side_effects=True, vmem_limit_bytes=63 * 2**20
        ),
        name="section",
    )(hidden, norm_gain, w_query, query_gain, w_output, key_cache, value_cache, *small)


def body(
    hidden,
    norm_gain,
    w_query,
    query_gain,
    w_output,
    key_cache,
    value_cache,
    key_scale,
    value_scale,
    page_table,
    page_tokens,
    page_list,
    list_len,
):
    kv_local = key_scale.shape[2]
    count = lax.axis_size("cache")
    sections = lax.axis_size("sections")
    places = plan(page_table, page_tokens, page_list[0], list_len[0])
    return run_section(
        (count, sections, kv_local),
        hidden,
        norm_gain,
        w_query,
        query_gain,
        w_output,
        key_cache,
        value_cache,
        places,
        key_scale[0].T,
        value_scale[0].T,
    )


def solution(mesh):
    return jax.shard_map(
        body,
        mesh=mesh,
        in_specs=(
            P("sections", "cache", None),
            P("sections", None),
            P("sections", None, "heads"),
            P("sections", None),
            P("sections", "heads", None),
            P("sections", "cache", None, "heads"),
            P("sections", "cache", None, "heads"),
            P("sections", "cache", "heads"),
            P("sections", "cache", "heads"),
            P(),
            P(),
            P("sections", None, None),
            P("sections", None),
        ),
        out_specs=P("sections", "cache", "heads"),
        check_vma=False,
    )
```

```python
import functools
import math

import jax
import jax.numpy as jnp
from jax import lax
from jax.experimental import pallas as pl
from jax.experimental.pallas import tpu as pltpu
from jax.sharding import PartitionSpec as P

MOST = 8
ROW_PIECES = 2
SUM_PIECES = 16
EARLY_PIECES = 6
SKEW = 6
RELAYS = (0, 3, 6, 11)
PACK = 1024

tiny_eps = 1e-06
masked_score = -1e30
lowest_top = -1e29
MESH = pl.DeviceIdType.MESH


def plan_kernel(table_ref, token_ref, list_ref, length_ref, place_ref):
    all_blocks, listed = list_ref.shape
    pages_dev = table_ref.shape[0] // lax.axis_size("cache")
    first = lax.axis_index("cache") * pages_dev

    def one_block(block, _):
        length = length_ref[block]
        for i in range(MOST + 1):
            place_ref[block, i] = 0

        def one_entry(entry, rank):
            page = list_ref[block, entry]
            local = table_ref[page] - first
            place_ref[block, rank] = local * PACK + token_ref[page]
            chosen = (local >= 0) & (local < pages_dev) & (entry < length)
            return rank + chosen.astype(jnp.int32)

        rank = lax.fori_loop(0, listed, one_entry, jnp.int32(0), unroll=16)
        place_ref[block, rank] = 0
        return 0

    lax.fori_loop(0, all_blocks, one_block, 0)


def plan(page_table, page_tokens, page_list, list_len):
    shape = jax.ShapeDtypeStruct((page_list.shape[0], MOST + 1), jnp.int32)
    scalars = pl.BlockSpec(memory_space=pltpu.SMEM)
    return pl.pallas_call(
        plan_kernel,
        out_shape=shape,
        in_specs=[scalars] * 4,
        out_specs=scalars,
        name="plan",
    )(page_table, page_tokens, page_list, list_len)


def section_kernel(
    dims,
    hidden_ref,
    norm_gain_ref,
    w_query_ref,
    query_gain_ref,
    w_output_ref,
    key_ref,
    value_ref,
    place_ref,
    key_scale_ref,
    value_scale_ref,
    out_ref,
    rows_ref,
    query_tiles,
    keys_ref,
    values_ref,
    normed_ref,
    queries_ref,
    lse_ref,
    top_ref,
    residual_ref,
    near_ref,
    away_ref,
    sibling_ref,
    carry_ref,
    sum_ref,
    local_sems,
    tile_sems,
    row_recv,
    own_send,
    forward_send,
    sibling_send,
    lse_send,
    lse_recv,
    away_send,
    away_recv,
    carry_send,
    carry_recv,
    out_send,
    out_recv,
    credit,
    *spare,
):
    count, sections, kv_local, tight = dims
    acc_ref, output_tiles = (rows_ref, query_tiles) if tight else spare
    z = lax.axis_index("cache")
    core = lax.axis_index("heads")
    section = lax.axis_index("sections")
    rows, width = hidden_ref.shape[1:]
    heads_local, head_size = queries_ref.shape[1], queries_ref.shape[3]
    blocks, block_rows = queries_ref.shape[0], queries_ref.shape[2]
    tiles, depth, tile = query_tiles.shape
    half_rows, half_width = rows // 2, width // 2
    piece = half_rows // ROW_PIECES
    part = rows // SUM_PIECES
    pages_dev, page_len = keys_ref.shape[:2]
    most = MOST
    group_size = heads_local // kv_local
    middle = count // 2
    first_pair = count if tight else middle
    pairs = count // 2
    twin = {"heads": 1 - core}
    following = {"sections": lax.rem(section + 1, sections)}
    previous = {"sections": lax.rem(section + sections - 1, sections)}

    def at(index):
        return {"cache": index}

    def remote(src, dst, send, recv, device):
        return pltpu.make_async_remote_copy(
            src_ref=src, dst_ref=dst, send_sem=send, recv_sem=recv, device_id=device, device_id_type=MESH
        )

    def piece_of(side, j):
        return pl.ds(pl.multiple_of(side * half_rows + j * piece, piece), piece)

    load_rows = pltpu.make_async_copy(hidden_ref.at[0], rows_ref.at[z], local_sems.at[0])
    load_keys = pltpu.make_async_copy(key_ref.at[0], keys_ref, local_sems.at[1])
    load_values = pltpu.make_async_copy(value_ref.at[0], values_ref, local_sems.at[2])
    load_residual = pltpu.make_async_copy(
        hidden_ref.at[0, :, pl.ds(pl.multiple_of(core * half_width, half_width), half_width)],
        residual_ref,
        local_sems.at[3],
    )

    def load_query_tile(i):
        return pltpu.make_async_copy(
            w_query_ref.at[0, :, pl.ds(pl.multiple_of(i * tile, tile), tile)], query_tiles.at[i], tile_sems.at[0, i]
        )

    def load_output_tile(i):
        per_half = tiles // 2
        own = jnp.where(i < per_half, 1 - core, core)
        column = own * half_width + lax.rem(i, per_half) * tile
        return pltpu.make_async_copy(
            w_output_ref.at[0, :, pl.ds(pl.multiple_of(column, tile), tile)], output_tiles.at[i], tile_sems.at[1, i]
        )

    load_rows.start()
    load_query_tile(0).start()
    barrier = pltpu.get_barrier_semaphore()
    for distance in range(1, count):
        pl.semaphore_signal(barrier, inc=1, device_id=at(lax.rem(z + distance, count)), device_id_type=MESH)
    for other in (twin, following, previous):
        pl.semaphore_signal(barrier, inc=1, device_id=other, device_id_type=MESH)
    for i in range(1, tiles):
        load_query_tile(i).start()
    load_keys.start()
    load_values.start()
    load_residual.start()
    if not tight:
        for i in range(tiles):
            load_output_tile(i).start()

    pl.semaphore_wait(barrier, count + 2)

    def own_copy(step, j):
        return remote(
            hidden_ref.at[0, piece_of(core, j)],
            rows_ref.at[z, piece_of(core, j)],
            own_send.at[(step + 1) // 2, j],
            row_recv.at[z, core, j],
            at(z + step),
        )

    def row_copy(owner, side, j, send, device):
        spot = rows_ref.at[owner, piece_of(side, j)]
        return remote(spot, spot, send, row_recv.at[owner, side, j], device)

    for j in range(ROW_PIECES):

        @pl.when(z > 0)
        def _():
            own_copy(-1, j).start()

        @pl.when(z < count - 1)
        def _():
            own_copy(1, j).start()

    def serve(distance, j):
        for step in (1, -1):
            owner = z - step * distance

            @pl.when((owner >= 0) & (owner < count))
            def _():
                row_copy(owner, core, j, forward_send.at[owner, j], twin).wait_recv()

                @pl.when((z + step >= 0) & (z + step < count))
                def _():
                    row_copy(owner, core, j, forward_send.at[owner, j], at(z + step)).start()

                row_copy(owner, core, j, sibling_send.at[owner, j], twin).start()

    def wait_row_sends(owner):
        step = jnp.where(owner < z, 1, -1)
        for j in range(ROW_PIECES):
            row_copy(owner, core, j, sibling_send.at[owner, j], twin).wait_send()

            @pl.when((z + step >= 0) & (z + step < count))
            def _():
                row_copy(owner, core, j, forward_send.at[owner, j], twin).wait_send()

    def owner_at(step):
        low = jnp.minimum(z, count - 1 - z)
        both = step <= 2 * low
        reach = jnp.where(both, (step + 1) // 2, step - low)
        right = (z < middle) == (jnp.logical_not(both) | (lax.rem(step, 2) == 1))
        return z + jnp.where(right, reach, -reach)

    def make_queries(owner, step):
        x = rows_ref[owner].astype(jnp.float32)
        inverse = lax.rsqrt(jnp.mean(x * x, axis=-1, keepdims=True) + tiny_eps)
        normed_ref[...] = (x * inverse * norm_gain_ref[...]).astype(jnp.bfloat16)

        @pl.when(step == 0)
        def _():
            for i in range(tiles):
                load_query_tile(i).wait()

        for i in range(tiles):
            projected = jnp.dot(normed_ref[...], query_tiles[i], preferred_element_type=jnp.float32)
            per_tile = tile // head_size
            for head in range(per_tile):
                own = projected[:, head * head_size : (head + 1) * head_size]
                turn = lax.rsqrt(jnp.mean(own * own, axis=-1, keepdims=True) + tiny_eps)
                scaled = (own * turn * query_gain_ref[...] / math.sqrt(head_size)).astype(jnp.bfloat16)
                for b in range(blocks):
                    queries_ref[b, i * per_tile + head] = scaled[b * block_rows : (b + 1) * block_rows]

    lanes = lax.broadcasted_iota(jnp.int32, (block_rows, 128), 1)
    together = min(4, group_size)

    def attend(owner, b):
        block = owner * blocks + b
        spot = pl.ds(pl.multiple_of(b * block_rows, block_rows), block_rows)
        places = [place_ref[block, i] for i in range(most)]
        slots = [place // PACK for place in places]
        fills = [lax.rem(place, PACK) for place in places]
        token = lax.broadcasted_iota(jnp.int32, (1, most * page_len), 1)

        def spread(values):
            row = jnp.full(token.shape, values[0])
            for i in range(1, most):
                row = jnp.where(token >= i * page_len, values[i], row)
            return row

        keeper = token < spread([i * page_len + fills[i] for i in range(most)])
        bias = jnp.where(keeper, 0.0, masked_score)
        top_tile = jnp.zeros((block_rows, 128), jnp.float32)
        total_tile = jnp.zeros((block_rows, 128), jnp.float32)
        for g in range(kv_local):
            columns = slice(g * head_size, (g + 1) * head_size)
            keys = jnp.concatenate([keys_ref[slot, :, columns] for slot in slots], axis=0)
            values = jnp.concatenate([values_ref[slot, :, columns] for slot in slots], axis=0)
            key_factor = spread([key_scale_ref[g, slot] for slot in slots]) * math.log2(math.e)
            key_factor = jnp.where(keeper, key_factor, 0.0)
            value_factor = spread([value_scale_ref[g, slot] for slot in slots])
            for j in range(0, group_size, together):
                head = g * group_size + j
                queries = queries_ref[b, head : head + together].reshape(together * block_rows, head_size)
                scores = lax.dot_general(
                    queries, keys, (((1,), (1,)), ((), ())), preferred_element_type=jnp.float32
                )
                scores = scores * key_factor + bias
                top = jnp.maximum(jnp.max(scores, axis=-1, keepdims=True), lowest_top)
                weights = jnp.exp2(scores - top)
                total = jnp.sum(weights, axis=-1, keepdims=True)
                scaled = (weights * value_factor).astype(jnp.bfloat16)
                acc = jnp.dot(scaled, values, preferred_element_type=jnp.float32)
                for k in range(together):
                    own = slice(k * block_rows, (k + 1) * block_rows)
                    place = slice((head + k) * head_size, (head + k + 1) * head_size)
                    acc_ref[owner, spot, place] = acc[own].astype(jnp.bfloat16)
                    top_tile = jnp.where(lanes == head + k, top[own], top_tile)
                    total_tile = jnp.where(lanes == head + k, total[own], total_tile)
        top = top_tile.T[:heads_local, :]
        total = total_tile.T[:heads_local, :]
        some = total > 0.0
        top_ref[owner, b] = top
        lse_ref[z, owner, b] = jnp.where(some, top + jnp.log2(jnp.where(some, total, 1.0)), masked_score)

    def lse_copy(owner, distance):
        spot = lse_ref.at[z, owner]
        other = lax.rem(z + distance, count)
        return remote(spot, spot, lse_send.at[distance - 1, owner], lse_recv.at[z, owner], at(other))

    def made_early(step):
        return (step == first_pair + 1) & (jnp.abs(owner_at(step) - z) < step)

    def prepare(step):
        owner = owner_at(step)

        @pl.when(step == 0)
        def _():
            load_rows.wait()

        @pl.when(step > 0)
        def _():
            for j in range(ROW_PIECES):
                row_copy(owner, 1 - core, j, sibling_send.at[owner, j], twin).wait_recv()
            if tight:
                wait_row_sends(owner)

        make_queries(owner, step)

    def attention_step(step):
        owner = owner_at(step)
        if tight:
            prepare(step)
        else:

            @pl.when(jnp.logical_not(made_early(step)))
            def _():
                prepare(step)

        @pl.when(step == 0)
        def _():
            load_keys.wait()
            load_values.wait()

        def one_block(b, _):
            attend(owner, b)

            @pl.when((step < count - 1) & (b < blocks - 1))
            def _():
                for j in range(ROW_PIECES - 1):

                    @pl.when(b == j)
                    def _():
                        serve(step + 1, j)

            @pl.when(b == 0)
            def _():
                relay_early(step, RELAYS[0], RELAYS[1])

            return 0

        lax.fori_loop(0, blocks, one_block, 0)

        def one_send(distance, _):
            lse_copy(owner, distance).start()
            return 0

        lax.fori_loop(1, count, one_send, 0)
        relay_early(step, RELAYS[1], RELAYS[2])
        if not tight:

            @pl.when((step < count - 1) & made_early(step + 1))
            def _():
                prepare(step + 1)


        if tight:

            @pl.when(step == count - 1)
            def _():
                for i in range(tiles):
                    load_output_tile(i).start()

    def owner_of(pair, i):
        upper = (z < middle) == (i == 0)
        return jnp.where(upper, middle + pair, middle - 1 - pair)

    def slot_of(pair, i):
        return 2 * (pair if pairs <= 2 else lax.rem(pair, 2)) + i

    def away_copy(i, k):
        columns = pl.ds(k * tile, tile)
        return remote(
            away_ref.at[i, :, columns], sibling_ref.at[i, :, columns], away_send.at[i, k], away_recv.at[i, k], twin
        )

    def sum_rows(j):
        return pl.ds(pl.multiple_of(j * part, part), part)

    def carry_copy(owner, i, j):
        step = jnp.where(owner > z, 1, -1)
        target = jnp.where(owner == z - 1, count, owner)
        return remote(
            sum_ref.at[i, sum_rows(j)],
            carry_ref.at[target, sum_rows(j)],
            carry_send.at[i, j],
            carry_recv.at[target, j],
            at(z + step),
        )

    def out_copy(i, j):
        return remote(
            sum_ref.at[i, sum_rows(j)], out_ref.at[0, sum_rows(j)], out_send.at[j], out_recv.at[j], following
        )

    def combine(pair, i, j):
        owner = owner_of(pair, i)
        slot = slot_of(pair, i)
        spot = sum_rows(j)

        @pl.when((owner >= z) & (z > 0))
        def _():
            landed = carry_ref.at[owner, spot]
            remote(landed, landed, carry_send.at[slot, j], carry_recv.at[owner, j], twin).wait_recv()
            near_ref[slot, spot, :] += carry_ref[owner, spot, :].astype(jnp.float32)

        @pl.when((owner <= z) & (z < count - 1))
        def _():
            source = jnp.where(owner == z, count, owner)
            landed = carry_ref.at[source, spot]
            remote(landed, landed, carry_send.at[slot, j], carry_recv.at[source, j], twin).wait_recv()
            near_ref[slot, spot, :] += carry_ref[source, spot, :].astype(jnp.float32)

        value = near_ref[slot, spot, :] + sibling_ref[slot, spot, :].astype(jnp.float32)

        @pl.when(pair > 1)
        def _():
            wait_sum_send(pair - 2, i, j)

        @pl.when(owner != z)
        def _():
            sum_ref[slot, spot, :] = value.astype(jnp.bfloat16)
            carry_copy(owner, slot, j).start()

        @pl.when(owner == z)
        def _():
            sum_ref[slot, spot, :] = (value + residual_ref[spot, :].astype(jnp.float32)).astype(jnp.bfloat16)
            out_copy(slot, j).start()

    def wait_sum_send(pair, i, j):
        owner = owner_of(pair, i)
        slot = slot_of(pair, i)

        @pl.when(owner != z)
        def _():
            carry_copy(owner, slot, j).wait_send()

        @pl.when(owner == z)
        def _():
            out_copy(slot, j).wait_send()

    def first_of_line(owner):
        return ((z == 0) & (owner > z)) | ((z == count - 1) & (owner < z))

    def give_credit(pair, i):
        if pairs > 2:

            @pl.when(pair < pairs - 2)
            def _():
                pl.semaphore_signal(credit.at[slot_of(pair, i)], inc=1, device_id=twin, device_id_type=MESH)

    def relay_early(step, begin, end):
        if tight:
            return
        pair = step - first_pair - 1

        @pl.when((pair >= 0) & (z > 0) & (z < count - 1))
        def _():
            owner = owner_of(pair, 0)

            @pl.when(owner != z)
            def _():
                start_line(pair, 0, begin, end)

    def finish_pair(pair, ends, begin=0, end=SUM_PIECES, served=0):
        def mine(i):
            owner = owner_of(pair, i)
            if ends:
                return owner == z
            return (owner != z) & jnp.logical_not(first_of_line(owner))

        def one_part(j, _):
            @pl.when((j >= served) & (j < end) & mine(0))
            def _():
                combine(pair, 0, j)

            @pl.when((j >= begin + skew) & mine(1))
            def _():
                combine(pair, 1, j - skew)

            return 0

        skew = 0 if ends else SKEW
        lax.fori_loop(begin, end + skew, one_part, 0)
        if end == SUM_PIECES:
            for i in range(2):

                @pl.when(mine(i))
                def _():
                    give_credit(pair, i)

    def start_line(pair, i, begin, end):
        def one_part(j, _):
            combine(pair, i, j)
            return 0

        lax.fori_loop(begin, end, one_part, 0)

    def project_turn(turn):
        def one_turn(turn, _):
            pair, i = turn // 2, lax.rem(turn, 2)
            owner = owner_of(pair, i)
            slot = slot_of(pair, i)

            def one_wait(distance, _):
                other = lax.rem(z + distance, count)
                spot = lse_ref.at[other, owner]
                remote(spot, spot, lse_send.at[0, owner], lse_recv.at[other, owner], twin).wait_recv()
                return 0

            lax.fori_loop(1, count, one_wait, 0)

            @pl.when((pair == 0) & (i == 0))
            def _():
                for k in range(tiles):
                    load_output_tile(k).wait()

                load_residual.wait()

            for b in range(blocks):
                spot = slice(b * block_rows, (b + 1) * block_rows)
                terms = [lse_ref[k, owner, b] for k in range(count)]
                top = functools.reduce(jnp.maximum, terms)
                total = sum(jnp.exp2(term - top) for term in terms)
                share = jnp.exp2(top_ref[owner, b] - top) / total
                share = jnp.concatenate([share, jnp.zeros((128 - heads_local, block_rows), jnp.float32)], axis=0).T
                share = jnp.concatenate(
                    [
                        jnp.broadcast_to(share[:, head : head + 1], (block_rows, head_size))
                        for head in range(heads_local)
                    ],
                    axis=1,
                )
                normed_ref[spot, :] = (acc_ref[owner, spot, :].astype(jnp.float32) * share).astype(jnp.bfloat16)

            if pairs > 2:

                @pl.when(pair > 1)
                def _():
                    for k in range(tiles // 2):
                        away_copy(slot, k).wait_send()
                    pl.semaphore_wait(credit.at[slot], 1)

            per_half = tiles // 2
            for k in range(per_half):
                away_ref[slot, :, k * tile : (k + 1) * tile] = jnp.dot(
                    normed_ref[...], output_tiles[k], preferred_element_type=jnp.float32
                ).astype(jnp.bfloat16)
                away_copy(slot, k).start()
            for k in range(per_half):
                near_ref[slot, :, k * tile : (k + 1) * tile] = jnp.dot(
                    normed_ref[...], output_tiles[per_half + k], preferred_element_type=jnp.float32
                )
            for k in range(per_half):
                away_copy(slot, k).wait_recv()

            whole = (i == 0) | (pair == pairs - 1)

            @pl.when(first_of_line(owner))
            def _():
                start_line(pair, i, 0, jnp.where(whole, SUM_PIECES, EARLY_PIECES))

                @pl.when(whole)
                def _():
                    give_credit(pair, i)

            @pl.when((i == 0) & (pair > 0) & first_of_line(owner_of(pair - 1, 1)))
            def _():
                start_line(pair - 1, 1, EARLY_PIECES, SUM_PIECES)
                give_credit(pair - 1, 1)

            return 0

        lax.fori_loop(turn, turn + 1, one_turn, 0)

    def one_step(step, _):
        if tight:

            @pl.when(step < count)
            def _():
                attention_step(step)
        else:
            attention_step(step)

        def one_turn(turn, _):
            pair = turn // 2

            @pl.when((turn >= 0) & (turn < count))
            def _():
                project_turn(turn)

            @pl.when((lax.rem(turn + 2, 2) == 1) & (turn > 0) & (turn < count - 1))
            def _():
                relay_early(step, RELAYS[2], RELAYS[3])

            @pl.when((lax.rem(turn + 2, 2) == 0) & (turn > 0) & (turn < count))
            def _():
                finish_pair(pair - 1, False, served=0 if tight else RELAYS[3])

            if pairs > 2:

                @pl.when((lax.rem(turn + 2, 2) == 1) & (pair > 0) & (turn < count - 1))
                def _():
                    finish_pair(pair - 1, True)

            return 0

        begin = 2 * (step - first_pair) - 1
        end = jnp.where(step == first_pair + pairs - 1, count, begin + 2)
        lax.fori_loop(jnp.where(step >= first_pair, begin, 0), jnp.where(step >= first_pair, end, 0), one_turn, 0)

        @pl.when(step < count - 1)
        def _():
            for j in range(min(ROW_PIECES, blocks) - 1, ROW_PIECES):
                serve(step + 1, j)

        return 0

    lax.fori_loop(0, first_pair + pairs, one_step, 0)
    if pairs > 1:
        finish_pair(pairs - 2, True, 0, EARLY_PIECES)
    finish_pair(pairs - 1, False)
    if pairs > 1:
        finish_pair(pairs - 2, True, EARLY_PIECES, SUM_PIECES)
    finish_pair(pairs - 1, True)

    for pair in range(max(pairs - 2, 0), pairs):
        for i in range(2):
            for k in range(tiles // 2):
                away_copy(slot_of(pair, i), k).wait_send()

            def one_part(j, _):
                wait_sum_send(pair, i, j)
                return 0

            lax.fori_loop(0, SUM_PIECES, one_part, 0)
    for j in range(ROW_PIECES):

        @pl.when(z > 0)
        def _():
            own_copy(-1, j).wait_send()

        @pl.when(z < count - 1)
        def _():
            own_copy(1, j).wait_send()

    def one_owner(owner, _):
        if not tight:

            @pl.when(owner != z)
            def _():
                wait_row_sends(owner)

        def one_send(distance, _):
            lse_copy(owner, distance).wait_send()
            return 0

        lax.fori_loop(1, count, one_send, 0)
        return 0

    lax.fori_loop(0, count, one_owner, 0)
    for j in range(SUM_PIECES):
        out_copy(0, j).wait_recv()


def run_section(dims, hidden, norm_gain, w_query, query_gain, w_output, key_cache, value_cache, *small):
    count, sections, kv_local = dims
    rows, width = hidden.shape[1:]
    depth, columns = w_query.shape[1:]
    head_size = query_gain.shape[1]
    heads_local = columns // head_size
    all_blocks = small[0].shape[0]
    blocks = all_blocks // count
    block_rows = rows // blocks
    half_width = width // 2
    tile = min(512, half_width, columns)
    tiles = columns // tile
    bf16, f32 = jnp.bfloat16, jnp.float32
    fixed = 2 * (w_query.size + key_cache.size + value_cache.size) + 28 * rows * width
    tight = fixed + 2 * w_output.size + 5 * count * rows * width > 50 * 2**20
    anywhere = pl.BlockSpec(memory_space=pl.ANY)
    stored = pl.BlockSpec(memory_space=pltpu.HBM)
    held = pl.BlockSpec(memory_space=pltpu.VMEM)
    dma = pltpu.SemaphoreType.DMA
    scratch = [
        pltpu.VMEM((count, rows, width), bf16),
        pltpu.VMEM((tiles, depth, tile), bf16),
        pltpu.VMEM(key_cache.shape[1:], bf16),
        pltpu.VMEM(value_cache.shape[1:], bf16),
        pltpu.VMEM((rows, width), bf16),
        pltpu.VMEM((blocks, heads_local, block_rows, head_size), bf16),
        pltpu.VMEM((count, count, blocks, heads_local, block_rows), f32),
        pltpu.VMEM((count, blocks, heads_local, block_rows), f32),
        pltpu.VMEM((rows, half_width), bf16),
        pltpu.VMEM((4, rows, half_width), f32),
        pltpu.VMEM((4, rows, half_width), bf16),
        pltpu.VMEM((4, rows, half_width), bf16),
        pltpu.VMEM((count + 1, rows, half_width), bf16),
        pltpu.VMEM((4, rows, half_width), bf16),
        dma((4,)),
        dma((2, tiles)),
        dma((count, 2, ROW_PIECES)),
        dma((2, ROW_PIECES)),
        dma((count, ROW_PIECES)),
        dma((count, ROW_PIECES)),
        dma((count - 1, count)),
        dma((count, count)),
        dma((4, tiles // 2)),
        dma((4, tiles // 2)),
        dma((4, SUM_PIECES)),
        dma((count + 1, SUM_PIECES)),
        dma((SUM_PIECES,)),
        dma((SUM_PIECES,)),
        pltpu.SemaphoreType.REGULAR((4,)),
    ]
    if not tight:
        scratch += [
            pltpu.VMEM((count, rows, heads_local * head_size), bf16),
            pltpu.VMEM((tiles, heads_local * head_size, tile), bf16),
        ]
    return pl.pallas_call(
        functools.partial(section_kernel, (count, sections, kv_local, tight)),
        out_shape=jax.ShapeDtypeStruct((1, rows, half_width), bf16),
        in_specs=[
            stored,
            held,
            stored,
            held,
            stored,
            stored,
            stored,
            *[pl.BlockSpec(memory_space=pltpu.SMEM)] * len(small),
        ],
        out_specs=anywhere,
        scratch_shapes=scratch,
        compiler_params=pltpu.CompilerParams(
            collective_id=0, has_side_effects=True, vmem_limit_bytes=63 * 2**20
        ),
        name="section",
    )(hidden, norm_gain, w_query, query_gain, w_output, key_cache, value_cache, *small)


def body(
    hidden,
    norm_gain,
    w_query,
    query_gain,
    w_output,
    key_cache,
    value_cache,
    key_scale,
    value_scale,
    page_table,
    page_tokens,
    page_list,
    list_len,
):
    kv_local = key_scale.shape[2]
    count = lax.axis_size("cache")
    sections = lax.axis_size("sections")
    places = plan(page_table, page_tokens, page_list[0], list_len[0])
    return run_section(
        (count, sections, kv_local),
        hidden,
        norm_gain,
        w_query,
        query_gain,
        w_output,
        key_cache,
        value_cache,
        places,
        key_scale[0].T,
        value_scale[0].T,
    )


def solution(mesh):
    return jax.shard_map(
        body,
        mesh=mesh,
        in_specs=(
            P("sections", "cache", None),
            P("sections", None),
            P("sections", None, "heads"),
            P("sections", None),
            P("sections", "heads", None),
            P("sections", "cache", None, "heads"),
            P("sections", "cache", None, "heads"),
            P("sections", "cache", "heads"),
            P("sections", "cache", "heads"),
            P(),
            P(),
            P("sections", None, None),
            P("sections", None),
        ),
        out_specs=P("sections", "cache", "heads"),
        check_vma=False,
    )
```

```python
import functools
import math

import jax
import jax.numpy as jnp
from jax import lax
from jax.experimental import pallas as pl
from jax.experimental.pallas import tpu as pltpu
from jax.sharding import PartitionSpec as P

MOST = 8
ROW_PIECES = 2
SUM_PIECES = 16
EARLY_PIECES = 6
FIRST_PIECES = 12
SKEW = 6
RELAYS = (0, 3, 6, 11)
PACK = 1024

tiny_eps = 1e-06
masked_score = -1e30
lowest_top = -1e29
MESH = pl.DeviceIdType.MESH


def plan_kernel(table_ref, token_ref, list_ref, length_ref, place_ref):
    all_blocks, listed = list_ref.shape
    pages_dev = table_ref.shape[0] // lax.axis_size("cache")
    first = lax.axis_index("cache") * pages_dev

    def one_block(block, _):
        length = length_ref[block]
        for i in range(MOST + 1):
            place_ref[block, i] = 0

        def one_entry(entry, rank):
            page = list_ref[block, entry]
            local = table_ref[page] - first
            place_ref[block, rank] = local * PACK + token_ref[page]
            chosen = (local >= 0) & (local < pages_dev) & (entry < length)
            return rank + chosen.astype(jnp.int32)

        rank = lax.fori_loop(0, listed, one_entry, jnp.int32(0), unroll=16)
        place_ref[block, rank] = 0
        return 0

    lax.fori_loop(0, all_blocks, one_block, 0)


def plan(page_table, page_tokens, page_list, list_len):
    shape = jax.ShapeDtypeStruct((page_list.shape[0], MOST + 1), jnp.int32)
    scalars = pl.BlockSpec(memory_space=pltpu.SMEM)
    return pl.pallas_call(
        plan_kernel,
        out_shape=shape,
        in_specs=[scalars] * 4,
        out_specs=scalars,
        name="plan",
    )(page_table, page_tokens, page_list, list_len)


def section_kernel(
    dims,
    hidden_ref,
    norm_gain_ref,
    w_query_ref,
    query_gain_ref,
    w_output_ref,
    key_ref,
    value_ref,
    place_ref,
    key_scale_ref,
    value_scale_ref,
    out_ref,
    rows_ref,
    query_tiles,
    keys_ref,
    values_ref,
    normed_ref,
    queries_ref,
    lse_ref,
    top_ref,
    residual_ref,
    near_ref,
    away_ref,
    sibling_ref,
    carry_ref,
    sum_ref,
    local_sems,
    tile_sems,
    row_recv,
    own_send,
    forward_send,
    sibling_send,
    lse_send,
    lse_recv,
    away_send,
    away_recv,
    carry_send,
    carry_recv,
    out_send,
    out_recv,
    credit,
    *spare,
):
    count, sections, kv_local, tight = dims
    acc_ref, output_tiles = (rows_ref, query_tiles) if tight else spare
    z = lax.axis_index("cache")
    core = lax.axis_index("heads")
    section = lax.axis_index("sections")
    rows, width = hidden_ref.shape[1:]
    heads_local, head_size = queries_ref.shape[1], queries_ref.shape[3]
    blocks, block_rows = queries_ref.shape[0], queries_ref.shape[2]
    tiles, depth, tile = query_tiles.shape
    half_rows, half_width = rows // 2, width // 2
    piece = half_rows // ROW_PIECES
    part = rows // SUM_PIECES
    pages_dev, page_len = keys_ref.shape[:2]
    most = MOST
    group_size = heads_local // kv_local
    middle = count // 2
    first_pair = count if tight else middle
    pairs = count // 2
    twin = {"heads": 1 - core}
    following = {"sections": lax.rem(section + 1, sections)}
    previous = {"sections": lax.rem(section + sections - 1, sections)}

    def at(index):
        return {"cache": index}

    def remote(src, dst, send, recv, device):
        return pltpu.make_async_remote_copy(
            src_ref=src, dst_ref=dst, send_sem=send, recv_sem=recv, device_id=device, device_id_type=MESH
        )

    def piece_of(side, j):
        return pl.ds(pl.multiple_of(side * half_rows + j * piece, piece), piece)

    load_rows = pltpu.make_async_copy(hidden_ref.at[0], rows_ref.at[z], local_sems.at[0])
    load_keys = pltpu.make_async_copy(key_ref.at[0], keys_ref, local_sems.at[1])
    load_values = pltpu.make_async_copy(value_ref.at[0], values_ref, local_sems.at[2])
    load_residual = pltpu.make_async_copy(
        hidden_ref.at[0, :, pl.ds(pl.multiple_of(core * half_width, half_width), half_width)],
        residual_ref,
        local_sems.at[3],
    )

    def load_query_tile(i):
        return pltpu.make_async_copy(
            w_query_ref.at[0, :, pl.ds(pl.multiple_of(i * tile, tile), tile)], query_tiles.at[i], tile_sems.at[0, i]
        )

    def load_output_tile(i):
        per_half = tiles // 2
        own = jnp.where(i < per_half, 1 - core, core)
        column = own * half_width + lax.rem(i, per_half) * tile
        return pltpu.make_async_copy(
            w_output_ref.at[0, :, pl.ds(pl.multiple_of(column, tile), tile)], output_tiles.at[i], tile_sems.at[1, i]
        )

    load_rows.start()
    load_query_tile(0).start()
    barrier = pltpu.get_barrier_semaphore()
    for distance in range(1, count):
        pl.semaphore_signal(barrier, inc=1, device_id=at(lax.rem(z + distance, count)), device_id_type=MESH)
    for other in (twin, following, previous):
        pl.semaphore_signal(barrier, inc=1, device_id=other, device_id_type=MESH)
    for i in range(1, tiles):
        load_query_tile(i).start()
    load_keys.start()
    load_values.start()
    load_residual.start()
    if not tight:
        for i in range(tiles):
            load_output_tile(i).start()

    pl.semaphore_wait(barrier, count + 2)

    def own_copy(step, j):
        return remote(
            hidden_ref.at[0, piece_of(core, j)],
            rows_ref.at[z, piece_of(core, j)],
            own_send.at[(step + 1) // 2, j],
            row_recv.at[z, core, j],
            at(z + step),
        )

    def row_copy(owner, side, j, send, device):
        spot = rows_ref.at[owner, piece_of(side, j)]
        return remote(spot, spot, send, row_recv.at[owner, side, j], device)

    for j in range(ROW_PIECES):

        @pl.when(z > 0)
        def _():
            own_copy(-1, j).start()

        @pl.when(z < count - 1)
        def _():
            own_copy(1, j).start()

    def serve(distance, j):
        for step in (1, -1):
            owner = z - step * distance

            @pl.when((owner >= 0) & (owner < count))
            def _():
                row_copy(owner, core, j, forward_send.at[owner, j], twin).wait_recv()

                @pl.when((z + step >= 0) & (z + step < count))
                def _():
                    row_copy(owner, core, j, forward_send.at[owner, j], at(z + step)).start()

                row_copy(owner, core, j, sibling_send.at[owner, j], twin).start()

    def wait_row_sends(owner):
        step = jnp.where(owner < z, 1, -1)
        for j in range(ROW_PIECES):
            row_copy(owner, core, j, sibling_send.at[owner, j], twin).wait_send()

            @pl.when((z + step >= 0) & (z + step < count))
            def _():
                row_copy(owner, core, j, forward_send.at[owner, j], twin).wait_send()

    def owner_at(step):
        low = jnp.minimum(z, count - 1 - z)
        both = step <= 2 * low
        reach = jnp.where(both, (step + 1) // 2, step - low)
        right = (z < middle) == (jnp.logical_not(both) | (lax.rem(step, 2) == 1))
        return z + jnp.where(right, reach, -reach)

    def make_queries(owner, step):
        x = rows_ref[owner].astype(jnp.float32)
        inverse = lax.rsqrt(jnp.mean(x * x, axis=-1, keepdims=True) + tiny_eps)
        normed_ref[...] = (x * inverse * norm_gain_ref[...]).astype(jnp.bfloat16)

        @pl.when(step == 0)
        def _():
            for i in range(tiles):
                load_query_tile(i).wait()

        for i in range(tiles):
            projected = jnp.dot(normed_ref[...], query_tiles[i], preferred_element_type=jnp.float32)
            per_tile = tile // head_size
            for head in range(per_tile):
                own = projected[:, head * head_size : (head + 1) * head_size]
                turn = lax.rsqrt(jnp.mean(own * own, axis=-1, keepdims=True) + tiny_eps)
                scaled = (own * turn * query_gain_ref[...] / math.sqrt(head_size)).astype(jnp.bfloat16)
                for b in range(blocks):
                    queries_ref[b, i * per_tile + head] = scaled[b * block_rows : (b + 1) * block_rows]

    lanes = lax.broadcasted_iota(jnp.int32, (block_rows, 128), 1)
    together = min(4, group_size)

    def attend(owner, b):
        block = owner * blocks + b
        spot = pl.ds(pl.multiple_of(b * block_rows, block_rows), block_rows)
        places = [place_ref[block, i] for i in range(most)]
        slots = [place // PACK for place in places]
        fills = [lax.rem(place, PACK) for place in places]
        token = lax.broadcasted_iota(jnp.int32, (1, most * page_len), 1)

        def spread(values):
            row = jnp.full(token.shape, values[0])
            for i in range(1, most):
                row = jnp.where(token >= i * page_len, values[i], row)
            return row

        keeper = token < spread([i * page_len + fills[i] for i in range(most)])
        bias = jnp.where(keeper, 0.0, masked_score)
        top_tile = jnp.zeros((block_rows, 128), jnp.float32)
        total_tile = jnp.zeros((block_rows, 128), jnp.float32)
        for g in range(kv_local):
            columns = slice(g * head_size, (g + 1) * head_size)
            keys = jnp.concatenate([keys_ref[slot, :, columns] for slot in slots], axis=0)
            values = jnp.concatenate([values_ref[slot, :, columns] for slot in slots], axis=0)
            key_factor = spread([key_scale_ref[g, slot] for slot in slots]) * math.log2(math.e)
            key_factor = jnp.where(keeper, key_factor, 0.0)
            value_factor = spread([value_scale_ref[g, slot] for slot in slots])
            for j in range(0, group_size, together):
                head = g * group_size + j
                queries = queries_ref[b, head : head + together].reshape(together * block_rows, head_size)
                scores = lax.dot_general(
                    queries, keys, (((1,), (1,)), ((), ())), preferred_element_type=jnp.float32
                )
                scores = scores * key_factor + bias
                top = jnp.maximum(jnp.max(scores, axis=-1, keepdims=True), lowest_top)
                weights = jnp.exp2(scores - top)
                total = jnp.sum(weights, axis=-1, keepdims=True)
                scaled = (weights * value_factor).astype(jnp.bfloat16)
                acc = jnp.dot(scaled, values, preferred_element_type=jnp.float32)
                for k in range(together):
                    own = slice(k * block_rows, (k + 1) * block_rows)
                    place = slice((head + k) * head_size, (head + k + 1) * head_size)
                    acc_ref[owner, spot, place] = acc[own].astype(jnp.bfloat16)
                    top_tile = jnp.where(lanes == head + k, top[own], top_tile)
                    total_tile = jnp.where(lanes == head + k, total[own], total_tile)
        top = top_tile.T[:heads_local, :]
        total = total_tile.T[:heads_local, :]
        some = total > 0.0
        top_ref[owner, b] = top
        lse_ref[z, owner, b] = jnp.where(some, top + jnp.log2(jnp.where(some, total, 1.0)), masked_score)

    def lse_copy(owner, distance):
        spot = lse_ref.at[z, owner]
        other = lax.rem(z + distance, count)
        return remote(spot, spot, lse_send.at[distance - 1, owner], lse_recv.at[z, owner], at(other))

    def made_early(step):
        return (step == first_pair + 1) & (jnp.abs(owner_at(step) - z) < step)

    def prepare(step):
        owner = owner_at(step)

        @pl.when(step == 0)
        def _():
            load_rows.wait()

        @pl.when(step > 0)
        def _():
            for j in range(ROW_PIECES):
                row_copy(owner, 1 - core, j, sibling_send.at[owner, j], twin).wait_recv()
            if tight:
                wait_row_sends(owner)

        make_queries(owner, step)

    def attention_step(step):
        owner = owner_at(step)
        if tight:
            prepare(step)
        else:

            @pl.when(jnp.logical_not(made_early(step)))
            def _():
                prepare(step)

        @pl.when(step == 0)
        def _():
            load_keys.wait()
            load_values.wait()

        def one_block(b, _):
            attend(owner, b)

            @pl.when((step < count - 1) & (b < blocks - 1))
            def _():
                for j in range(ROW_PIECES - 1):

                    @pl.when(b == j)
                    def _():
                        serve(step + 1, j)

            @pl.when(b == 0)
            def _():
                relay_early(step, RELAYS[0], RELAYS[1])

            return 0

        lax.fori_loop(0, blocks, one_block, 0)

        def one_send(distance, _):
            lse_copy(owner, distance).start()
            return 0

        lax.fori_loop(1, count, one_send, 0)
        relay_early(step, RELAYS[1], RELAYS[2])
        if not tight:
            pair = step - first_pair - 1

            @pl.when((pair >= 0) & first_of_line(owner_of(pair, 0)))
            def _():
                start_line(pair, 0, FIRST_PIECES, SUM_PIECES)
                give_credit(pair, 0)

            @pl.when((step < count - 1) & made_early(step + 1))
            def _():
                prepare(step + 1)


        if tight:

            @pl.when(step == count - 1)
            def _():
                for i in range(tiles):
                    load_output_tile(i).start()

    def owner_of(pair, i):
        upper = (z < middle) == (i == 0)
        return jnp.where(upper, middle + pair, middle - 1 - pair)

    def slot_of(pair, i):
        return 2 * (pair if pairs <= 2 else lax.rem(pair, 2)) + i

    def away_copy(i, k):
        columns = pl.ds(k * tile, tile)
        return remote(
            away_ref.at[i, :, columns], sibling_ref.at[i, :, columns], away_send.at[i, k], away_recv.at[i, k], twin
        )

    def sum_rows(j):
        return pl.ds(pl.multiple_of(j * part, part), part)

    def carry_copy(owner, i, j):
        step = jnp.where(owner > z, 1, -1)
        target = jnp.where(owner == z - 1, count, owner)
        return remote(
            sum_ref.at[i, sum_rows(j)],
            carry_ref.at[target, sum_rows(j)],
            carry_send.at[i, j],
            carry_recv.at[target, j],
            at(z + step),
        )

    def out_copy(i, j):
        return remote(
            sum_ref.at[i, sum_rows(j)], out_ref.at[0, sum_rows(j)], out_send.at[j], out_recv.at[j], following
        )

    def combine(pair, i, j):
        owner = owner_of(pair, i)
        slot = slot_of(pair, i)
        spot = sum_rows(j)

        @pl.when((owner >= z) & (z > 0))
        def _():
            landed = carry_ref.at[owner, spot]
            remote(landed, landed, carry_send.at[slot, j], carry_recv.at[owner, j], twin).wait_recv()
            near_ref[slot, spot, :] += carry_ref[owner, spot, :].astype(jnp.float32)

        @pl.when((owner <= z) & (z < count - 1))
        def _():
            source = jnp.where(owner == z, count, owner)
            landed = carry_ref.at[source, spot]
            remote(landed, landed, carry_send.at[slot, j], carry_recv.at[source, j], twin).wait_recv()
            near_ref[slot, spot, :] += carry_ref[source, spot, :].astype(jnp.float32)

        value = near_ref[slot, spot, :] + sibling_ref[slot, spot, :].astype(jnp.float32)

        @pl.when(pair > 1)
        def _():
            wait_sum_send(pair - 2, i, j)

        @pl.when(owner != z)
        def _():
            sum_ref[slot, spot, :] = value.astype(jnp.bfloat16)
            carry_copy(owner, slot, j).start()

        @pl.when(owner == z)
        def _():
            sum_ref[slot, spot, :] = (value + residual_ref[spot, :].astype(jnp.float32)).astype(jnp.bfloat16)
            out_copy(slot, j).start()

    def wait_sum_send(pair, i, j):
        owner = owner_of(pair, i)
        slot = slot_of(pair, i)

        @pl.when(owner != z)
        def _():
            carry_copy(owner, slot, j).wait_send()

        @pl.when(owner == z)
        def _():
            out_copy(slot, j).wait_send()

    def first_of_line(owner):
        return ((z == 0) & (owner > z)) | ((z == count - 1) & (owner < z))

    def give_credit(pair, i):
        if pairs > 2:

            @pl.when(pair < pairs - 2)
            def _():
                pl.semaphore_signal(credit.at[slot_of(pair, i)], inc=1, device_id=twin, device_id_type=MESH)

    def relay_early(step, begin, end):
        if tight:
            return
        pair = step - first_pair - 1

        @pl.when((pair >= 0) & (z > 0) & (z < count - 1))
        def _():
            owner = owner_of(pair, 0)

            @pl.when(owner != z)
            def _():
                start_line(pair, 0, begin, end)

    def finish_pair(pair, ends, begin=0, end=SUM_PIECES, served=0):
        def mine(i):
            owner = owner_of(pair, i)
            if ends:
                return owner == z
            return (owner != z) & jnp.logical_not(first_of_line(owner))

        def one_part(j, _):
            @pl.when((j >= served) & (j < end) & mine(0))
            def _():
                combine(pair, 0, j)

            @pl.when((j >= begin + skew) & mine(1))
            def _():
                combine(pair, 1, j - skew)

            return 0

        skew = 0 if ends else SKEW
        lax.fori_loop(begin, end + skew, one_part, 0)
        if end == SUM_PIECES:
            for i in range(2):

                @pl.when(mine(i))
                def _():
                    give_credit(pair, i)

    def start_line(pair, i, begin, end):
        def one_part(j, _):
            combine(pair, i, j)
            return 0

        lax.fori_loop(begin, end, one_part, 0)

    def project_turn(turn):
        def one_turn(turn, _):
            pair, i = turn // 2, lax.rem(turn, 2)
            owner = owner_of(pair, i)
            slot = slot_of(pair, i)

            def one_wait(distance, _):
                other = lax.rem(z + distance, count)
                spot = lse_ref.at[other, owner]
                remote(spot, spot, lse_send.at[0, owner], lse_recv.at[other, owner], twin).wait_recv()
                return 0

            lax.fori_loop(1, count, one_wait, 0)

            @pl.when((pair == 0) & (i == 0))
            def _():
                for k in range(tiles):
                    load_output_tile(k).wait()

                load_residual.wait()

            for b in range(blocks):
                spot = slice(b * block_rows, (b + 1) * block_rows)
                terms = [lse_ref[k, owner, b] for k in range(count)]
                top = functools.reduce(jnp.maximum, terms)
                total = sum(jnp.exp2(term - top) for term in terms)
                share = jnp.exp2(top_ref[owner, b] - top) / total
                share = jnp.concatenate([share, jnp.zeros((128 - heads_local, block_rows), jnp.float32)], axis=0).T
                share = jnp.concatenate(
                    [
                        jnp.broadcast_to(share[:, head : head + 1], (block_rows, head_size))
                        for head in range(heads_local)
                    ],
                    axis=1,
                )
                normed_ref[spot, :] = (acc_ref[owner, spot, :].astype(jnp.float32) * share).astype(jnp.bfloat16)

            if pairs > 2:

                @pl.when(pair > 1)
                def _():
                    for k in range(tiles // 2):
                        away_copy(slot, k).wait_send()
                    pl.semaphore_wait(credit.at[slot], 1)

            per_half = tiles // 2
            for k in range(per_half):
                away_ref[slot, :, k * tile : (k + 1) * tile] = jnp.dot(
                    normed_ref[...], output_tiles[k], preferred_element_type=jnp.float32
                ).astype(jnp.bfloat16)
                away_copy(slot, k).start()
            for k in range(per_half):
                near_ref[slot, :, k * tile : (k + 1) * tile] = jnp.dot(
                    normed_ref[...], output_tiles[per_half + k], preferred_element_type=jnp.float32
                )
            for k in range(per_half):
                away_copy(slot, k).wait_recv()

            whole = (i == 0) | (pair == pairs - 1)

            parted = jnp.logical_not(tight) & (i == 0) & (pair < pairs - 1)

            @pl.when(first_of_line(owner))
            def _():
                start_line(
                    pair, i, 0, jnp.where(parted, FIRST_PIECES, jnp.where(whole, SUM_PIECES, EARLY_PIECES))
                )

                @pl.when(whole & jnp.logical_not(parted))
                def _():
                    give_credit(pair, i)

            @pl.when((i == 0) & (pair > 0) & first_of_line(owner_of(pair - 1, 1)))
            def _():
                start_line(pair - 1, 1, EARLY_PIECES, SUM_PIECES)
                give_credit(pair - 1, 1)

            return 0

        lax.fori_loop(turn, turn + 1, one_turn, 0)

    def one_step(step, _):
        if tight:

            @pl.when(step < count)
            def _():
                attention_step(step)
        else:
            attention_step(step)

        def one_turn(turn, _):
            pair = turn // 2

            @pl.when((turn >= 0) & (turn < count))
            def _():
                project_turn(turn)

            @pl.when((lax.rem(turn + 2, 2) == 1) & (turn > 0) & (turn < count - 1))
            def _():
                relay_early(step, RELAYS[2], RELAYS[3])

            @pl.when((lax.rem(turn + 2, 2) == 0) & (turn > 0) & (turn < count))
            def _():
                finish_pair(pair - 1, False, served=0 if tight else RELAYS[3])

            if pairs > 2:

                @pl.when((lax.rem(turn + 2, 2) == 1) & (pair > 0) & (turn < count - 1))
                def _():
                    finish_pair(pair - 1, True)

            return 0

        begin = 2 * (step - first_pair) - 1
        end = jnp.where(step == first_pair + pairs - 1, count, begin + 2)
        lax.fori_loop(jnp.where(step >= first_pair, begin, 0), jnp.where(step >= first_pair, end, 0), one_turn, 0)

        @pl.when(step < count - 1)
        def _():
            for j in range(min(ROW_PIECES, blocks) - 1, ROW_PIECES):
                serve(step + 1, j)

        return 0

    lax.fori_loop(0, first_pair + pairs, one_step, 0)
    if pairs > 1:
        finish_pair(pairs - 2, True, 0, EARLY_PIECES)
    finish_pair(pairs - 1, False)
    if pairs > 1:
        finish_pair(pairs - 2, True, EARLY_PIECES, SUM_PIECES)
    finish_pair(pairs - 1, True)

    for pair in range(max(pairs - 2, 0), pairs):
        for i in range(2):
            for k in range(tiles // 2):
                away_copy(slot_of(pair, i), k).wait_send()

            def one_part(j, _):
                wait_sum_send(pair, i, j)
                return 0

            lax.fori_loop(0, SUM_PIECES, one_part, 0)
    for j in range(ROW_PIECES):

        @pl.when(z > 0)
        def _():
            own_copy(-1, j).wait_send()

        @pl.when(z < count - 1)
        def _():
            own_copy(1, j).wait_send()

    def one_owner(owner, _):
        if not tight:

            @pl.when(owner != z)
            def _():
                wait_row_sends(owner)

        def one_send(distance, _):
            lse_copy(owner, distance).wait_send()
            return 0

        lax.fori_loop(1, count, one_send, 0)
        return 0

    lax.fori_loop(0, count, one_owner, 0)
    for j in range(SUM_PIECES):
        out_copy(0, j).wait_recv()


def run_section(dims, hidden, norm_gain, w_query, query_gain, w_output, key_cache, value_cache, *small):
    count, sections, kv_local = dims
    rows, width = hidden.shape[1:]
    depth, columns = w_query.shape[1:]
    head_size = query_gain.shape[1]
    heads_local = columns // head_size
    all_blocks = small[0].shape[0]
    blocks = all_blocks // count
    block_rows = rows // blocks
    half_width = width // 2
    tile = min(512, half_width, columns)
    tiles = columns // tile
    bf16, f32 = jnp.bfloat16, jnp.float32
    fixed = 2 * (w_query.size + key_cache.size + value_cache.size) + 28 * rows * width
    tight = fixed + 2 * w_output.size + 5 * count * rows * width > 50 * 2**20
    anywhere = pl.BlockSpec(memory_space=pl.ANY)
    stored = pl.BlockSpec(memory_space=pltpu.HBM)
    held = pl.BlockSpec(memory_space=pltpu.VMEM)
    dma = pltpu.SemaphoreType.DMA
    scratch = [
        pltpu.VMEM((count, rows, width), bf16),
        pltpu.VMEM((tiles, depth, tile), bf16),
        pltpu.VMEM(key_cache.shape[1:], bf16),
        pltpu.VMEM(value_cache.shape[1:], bf16),
        pltpu.VMEM((rows, width), bf16),
        pltpu.VMEM((blocks, heads_local, block_rows, head_size), bf16),
        pltpu.VMEM((count, count, blocks, heads_local, block_rows), f32),
        pltpu.VMEM((count, blocks, heads_local, block_rows), f32),
        pltpu.VMEM((rows, half_width), bf16),
        pltpu.VMEM((4, rows, half_width), f32),
        pltpu.VMEM((4, rows, half_width), bf16),
        pltpu.VMEM((4, rows, half_width), bf16),
        pltpu.VMEM((count + 1, rows, half_width), bf16),
        pltpu.VMEM((4, rows, half_width), bf16),
        dma((4,)),
        dma((2, tiles)),
        dma((count, 2, ROW_PIECES)),
        dma((2, ROW_PIECES)),
        dma((count, ROW_PIECES)),
        dma((count, ROW_PIECES)),
        dma((count - 1, count)),
        dma((count, count)),
        dma((4, tiles // 2)),
        dma((4, tiles // 2)),
        dma((4, SUM_PIECES)),
        dma((count + 1, SUM_PIECES)),
        dma((SUM_PIECES,)),
        dma((SUM_PIECES,)),
        pltpu.SemaphoreType.REGULAR((4,)),
    ]
    if not tight:
        scratch += [
            pltpu.VMEM((count, rows, heads_local * head_size), bf16),
            pltpu.VMEM((tiles, heads_local * head_size, tile), bf16),
        ]
    return pl.pallas_call(
        functools.partial(section_kernel, (count, sections, kv_local, tight)),
        out_shape=jax.ShapeDtypeStruct((1, rows, half_width), bf16),
        in_specs=[
            stored,
            held,
            stored,
            held,
            stored,
            stored,
            stored,
            *[pl.BlockSpec(memory_space=pltpu.SMEM)] * len(small),
        ],
        out_specs=anywhere,
        scratch_shapes=scratch,
        compiler_params=pltpu.CompilerParams(
            collective_id=0, has_side_effects=True, vmem_limit_bytes=63 * 2**20
        ),
        name="section",
    )(hidden, norm_gain, w_query, query_gain, w_output, key_cache, value_cache, *small)


def body(
    hidden,
    norm_gain,
    w_query,
    query_gain,
    w_output,
    key_cache,
    value_cache,
    key_scale,
    value_scale,
    page_table,
    page_tokens,
    page_list,
    list_len,
):
    kv_local = key_scale.shape[2]
    count = lax.axis_size("cache")
    sections = lax.axis_size("sections")
    places = plan(page_table, page_tokens, page_list[0], list_len[0])
    return run_section(
        (count, sections, kv_local),
        hidden,
        norm_gain,
        w_query,
        query_gain,
        w_output,
        key_cache,
        value_cache,
        places,
        key_scale[0].T,
        value_scale[0].T,
    )


def solution(mesh):
    return jax.shard_map(
        body,
        mesh=mesh,
        in_specs=(
            P("sections", "cache", None),
            P("sections", None),
            P("sections", None, "heads"),
            P("sections", None),
            P("sections", "heads", None),
            P("sections", "cache", None, "heads"),
            P("sections", "cache", None, "heads"),
            P("sections", "cache", "heads"),
            P("sections", "cache", "heads"),
            P(),
            P(),
            P("sections", None, None),
            P("sections", None),
        ),
        out_specs=P("sections", "cache", "heads"),
        check_vma=False,
    )
```

```python
import functools
import math

import jax
import jax.numpy as jnp
from jax import lax
from jax.experimental import pallas as pl
from jax.experimental.pallas import tpu as pltpu
from jax.sharding import PartitionSpec as P

MOST = 8
ROW_PIECES = 2
SUM_PIECES = 16
EARLY_PIECES = 4
FIRST_PIECES = 12
SKEW = 6
RELAYS = (0, 3, 6, 11)
PACK = 1024

tiny_eps = 1e-06
masked_score = -1e30
lowest_top = -1e29
MESH = pl.DeviceIdType.MESH


def plan_kernel(table_ref, token_ref, list_ref, length_ref, place_ref):
    all_blocks, listed = list_ref.shape
    pages_dev = table_ref.shape[0] // lax.axis_size("cache")
    first = lax.axis_index("cache") * pages_dev

    def one_block(block, _):
        length = length_ref[block]
        for i in range(MOST + 1):
            place_ref[block, i] = 0

        def one_entry(entry, rank):
            page = list_ref[block, entry]
            local = table_ref[page] - first
            place_ref[block, rank] = local * PACK + token_ref[page]
            chosen = (local >= 0) & (local < pages_dev) & (entry < length)
            return rank + chosen.astype(jnp.int32)

        rank = lax.fori_loop(0, listed, one_entry, jnp.int32(0), unroll=16)
        place_ref[block, rank] = 0
        return 0

    lax.fori_loop(0, all_blocks, one_block, 0)


def plan(page_table, page_tokens, page_list, list_len):
    shape = jax.ShapeDtypeStruct((page_list.shape[0], MOST + 1), jnp.int32)
    scalars = pl.BlockSpec(memory_space=pltpu.SMEM)
    return pl.pallas_call(
        plan_kernel,
        out_shape=shape,
        in_specs=[scalars] * 4,
        out_specs=scalars,
        name="plan",
    )(page_table, page_tokens, page_list, list_len)


def section_kernel(
    dims,
    hidden_ref,
    norm_gain_ref,
    w_query_ref,
    query_gain_ref,
    w_output_ref,
    key_ref,
    value_ref,
    place_ref,
    key_scale_ref,
    value_scale_ref,
    out_ref,
    rows_ref,
    query_tiles,
    keys_ref,
    values_ref,
    normed_ref,
    queries_ref,
    lse_ref,
    top_ref,
    residual_ref,
    near_ref,
    away_ref,
    sibling_ref,
    carry_ref,
    sum_ref,
    local_sems,
    tile_sems,
    row_recv,
    own_send,
    forward_send,
    sibling_send,
    lse_send,
    lse_recv,
    away_send,
    away_recv,
    carry_send,
    carry_recv,
    out_send,
    out_recv,
    credit,
    *spare,
):
    count, sections, kv_local, tight = dims
    acc_ref, output_tiles = (rows_ref, query_tiles) if tight else spare
    z = lax.axis_index("cache")
    core = lax.axis_index("heads")
    section = lax.axis_index("sections")
    rows, width = hidden_ref.shape[1:]
    heads_local, head_size = queries_ref.shape[1], queries_ref.shape[3]
    blocks, block_rows = queries_ref.shape[0], queries_ref.shape[2]
    tiles, depth, tile = query_tiles.shape
    half_rows, half_width = rows // 2, width // 2
    piece = half_rows // ROW_PIECES
    part = rows // SUM_PIECES
    pages_dev, page_len = keys_ref.shape[:2]
    most = MOST
    group_size = heads_local // kv_local
    middle = count // 2
    first_pair = count if tight else middle
    pairs = count // 2
    twin = {"heads": 1 - core}
    following = {"sections": lax.rem(section + 1, sections)}
    previous = {"sections": lax.rem(section + sections - 1, sections)}

    def at(index):
        return {"cache": index}

    def remote(src, dst, send, recv, device):
        return pltpu.make_async_remote_copy(
            src_ref=src, dst_ref=dst, send_sem=send, recv_sem=recv, device_id=device, device_id_type=MESH
        )

    def piece_of(side, j):
        return pl.ds(pl.multiple_of(side * half_rows + j * piece, piece), piece)

    load_rows = pltpu.make_async_copy(hidden_ref.at[0], rows_ref.at[z], local_sems.at[0])
    load_keys = pltpu.make_async_copy(key_ref.at[0], keys_ref, local_sems.at[1])
    load_values = pltpu.make_async_copy(value_ref.at[0], values_ref, local_sems.at[2])
    load_residual = pltpu.make_async_copy(
        hidden_ref.at[0, :, pl.ds(pl.multiple_of(core * half_width, half_width), half_width)],
        residual_ref,
        local_sems.at[3],
    )

    def load_query_tile(i):
        return pltpu.make_async_copy(
            w_query_ref.at[0, :, pl.ds(pl.multiple_of(i * tile, tile), tile)], query_tiles.at[i], tile_sems.at[0, i]
        )

    def load_output_tile(i):
        per_half = tiles // 2
        own = jnp.where(i < per_half, 1 - core, core)
        column = own * half_width + lax.rem(i, per_half) * tile
        return pltpu.make_async_copy(
            w_output_ref.at[0, :, pl.ds(pl.multiple_of(column, tile), tile)], output_tiles.at[i], tile_sems.at[1, i]
        )

    load_rows.start()
    load_query_tile(0).start()
    barrier = pltpu.get_barrier_semaphore()
    for distance in range(1, count):
        pl.semaphore_signal(barrier, inc=1, device_id=at(lax.rem(z + distance, count)), device_id_type=MESH)
    for other in (twin, following, previous):
        pl.semaphore_signal(barrier, inc=1, device_id=other, device_id_type=MESH)
    for i in range(1, tiles):
        load_query_tile(i).start()
    load_keys.start()
    load_values.start()
    load_residual.start()
    if not tight:
        for i in range(tiles):
            load_output_tile(i).start()

    pl.semaphore_wait(barrier, count + 2)

    def own_copy(step, j):
        return remote(
            hidden_ref.at[0, piece_of(core, j)],
            rows_ref.at[z, piece_of(core, j)],
            own_send.at[(step + 1) // 2, j],
            row_recv.at[z, core, j],
            at(z + step),
        )

    def row_copy(owner, side, j, send, device):
        spot = rows_ref.at[owner, piece_of(side, j)]
        return remote(spot, spot, send, row_recv.at[owner, side, j], device)

    for j in range(ROW_PIECES):

        @pl.when(z > 0)
        def _():
            own_copy(-1, j).start()

        @pl.when(z < count - 1)
        def _():
            own_copy(1, j).start()

    def serve(distance, j):
        for step in (1, -1):
            owner = z - step * distance

            @pl.when((owner >= 0) & (owner < count))
            def _():
                row_copy(owner, core, j, forward_send.at[owner, j], twin).wait_recv()

                @pl.when((z + step >= 0) & (z + step < count))
                def _():
                    row_copy(owner, core, j, forward_send.at[owner, j], at(z + step)).start()

                row_copy(owner, core, j, sibling_send.at[owner, j], twin).start()

    def wait_row_sends(owner):
        step = jnp.where(owner < z, 1, -1)
        for j in range(ROW_PIECES):
            row_copy(owner, core, j, sibling_send.at[owner, j], twin).wait_send()

            @pl.when((z + step >= 0) & (z + step < count))
            def _():
                row_copy(owner, core, j, forward_send.at[owner, j], twin).wait_send()

    def owner_at(step):
        low = jnp.minimum(z, count - 1 - z)
        both = step <= 2 * low
        reach = jnp.where(both, (step + 1) // 2, step - low)
        right = (z < middle) == (jnp.logical_not(both) | (lax.rem(step, 2) == 1))
        return z + jnp.where(right, reach, -reach)

    def make_queries(owner, step):
        x = rows_ref[owner].astype(jnp.float32)
        inverse = lax.rsqrt(jnp.mean(x * x, axis=-1, keepdims=True) + tiny_eps)
        normed_ref[...] = (x * inverse * norm_gain_ref[...]).astype(jnp.bfloat16)

        @pl.when(step == 0)
        def _():
            for i in range(tiles):
                load_query_tile(i).wait()

        for i in range(tiles):
            projected = jnp.dot(normed_ref[...], query_tiles[i], preferred_element_type=jnp.float32)
            per_tile = tile // head_size
            for head in range(per_tile):
                own = projected[:, head * head_size : (head + 1) * head_size]
                turn = lax.rsqrt(jnp.mean(own * own, axis=-1, keepdims=True) + tiny_eps)
                scaled = (own * turn * query_gain_ref[...] / math.sqrt(head_size)).astype(jnp.bfloat16)
                for b in range(blocks):
                    queries_ref[b, i * per_tile + head] = scaled[b * block_rows : (b + 1) * block_rows]

    lanes = lax.broadcasted_iota(jnp.int32, (block_rows, 128), 1)
    together = min(4, group_size)

    def attend(owner, b):
        block = owner * blocks + b
        spot = pl.ds(pl.multiple_of(b * block_rows, block_rows), block_rows)
        places = [place_ref[block, i] for i in range(most)]
        slots = [place // PACK for place in places]
        fills = [lax.rem(place, PACK) for place in places]
        token = lax.broadcasted_iota(jnp.int32, (1, most * page_len), 1)

        def spread(values):
            row = jnp.full(token.shape, values[0])
            for i in range(1, most):
                row = jnp.where(token >= i * page_len, values[i], row)
            return row

        keeper = token < spread([i * page_len + fills[i] for i in range(most)])
        bias = jnp.where(keeper, 0.0, masked_score)
        top_tile = jnp.zeros((block_rows, 128), jnp.float32)
        total_tile = jnp.zeros((block_rows, 128), jnp.float32)
        for g in range(kv_local):
            columns = slice(g * head_size, (g + 1) * head_size)
            keys = jnp.concatenate([keys_ref[slot, :, columns] for slot in slots], axis=0)
            values = jnp.concatenate([values_ref[slot, :, columns] for slot in slots], axis=0)
            key_factor = spread([key_scale_ref[g, slot] for slot in slots]) * math.log2(math.e)
            key_factor = jnp.where(keeper, key_factor, 0.0)
            value_factor = spread([value_scale_ref[g, slot] for slot in slots])
            for j in range(0, group_size, together):
                head = g * group_size + j
                queries = queries_ref[b, head : head + together].reshape(together * block_rows, head_size)
                scores = lax.dot_general(
                    queries, keys, (((1,), (1,)), ((), ())), preferred_element_type=jnp.float32
                )
                scores = scores * key_factor + bias
                top = jnp.maximum(jnp.max(scores, axis=-1, keepdims=True), lowest_top)
                weights = jnp.exp2(scores - top)
                total = jnp.sum(weights, axis=-1, keepdims=True)
                scaled = (weights * value_factor).astype(jnp.bfloat16)
                acc = jnp.dot(scaled, values, preferred_element_type=jnp.float32)
                for k in range(together):
                    own = slice(k * block_rows, (k + 1) * block_rows)
                    place = slice((head + k) * head_size, (head + k + 1) * head_size)
                    acc_ref[owner, spot, place] = acc[own].astype(jnp.bfloat16)
                    top_tile = jnp.where(lanes == head + k, top[own], top_tile)
                    total_tile = jnp.where(lanes == head + k, total[own], total_tile)
        top = top_tile.T[:heads_local, :]
        total = total_tile.T[:heads_local, :]
        some = total > 0.0
        top_ref[owner, b] = top
        lse_ref[z, owner, b] = jnp.where(some, top + jnp.log2(jnp.where(some, total, 1.0)), masked_score)

    def lse_copy(owner, distance):
        spot = lse_ref.at[z, owner]
        other = lax.rem(z + distance, count)
        return remote(spot, spot, lse_send.at[distance - 1, owner], lse_recv.at[z, owner], at(other))

    def made_early(step):
        return (step == first_pair + 1) & (jnp.abs(owner_at(step) - z) < step)

    def prepare(step):
        owner = owner_at(step)

        @pl.when(step == 0)
        def _():
            load_rows.wait()

        @pl.when(step > 0)
        def _():
            for j in range(ROW_PIECES):
                row_copy(owner, 1 - core, j, sibling_send.at[owner, j], twin).wait_recv()
            if tight:
                wait_row_sends(owner)

        make_queries(owner, step)

    def attention_step(step):
        owner = owner_at(step)
        if tight:
            prepare(step)
        else:

            @pl.when(jnp.logical_not(made_early(step)))
            def _():
                prepare(step)

        @pl.when(step == 0)
        def _():
            load_keys.wait()
            load_values.wait()

        def one_block(b, _):
            attend(owner, b)

            @pl.when((step < count - 1) & (b < blocks - 1))
            def _():
                for j in range(ROW_PIECES - 1):

                    @pl.when(b == j)
                    def _():
                        serve(step + 1, j)

            @pl.when(b == 0)
            def _():
                relay_early(step, RELAYS[0], RELAYS[1])

            return 0

        lax.fori_loop(0, blocks, one_block, 0)

        def one_send(distance, _):
            lse_copy(owner, distance).start()
            return 0

        lax.fori_loop(1, count, one_send, 0)
        relay_early(step, RELAYS[1], RELAYS[2])
        if not tight:
            pair = step - first_pair - 1

            @pl.when((pair >= 0) & first_of_line(owner_of(pair, 0)))
            def _():
                start_line(pair, 0, FIRST_PIECES, SUM_PIECES)
                give_credit(pair, 0)

            @pl.when((step < count - 1) & made_early(step + 1))
            def _():
                prepare(step + 1)


        if tight:

            @pl.when(step == count - 1)
            def _():
                for i in range(tiles):
                    load_output_tile(i).start()

    def owner_of(pair, i):
        upper = (z < middle) == (i == 0)
        return jnp.where(upper, middle + pair, middle - 1 - pair)

    def slot_of(pair, i):
        return 2 * (pair if pairs <= 2 else lax.rem(pair, 2)) + i

    def away_copy(i, k):
        columns = pl.ds(k * tile, tile)
        return remote(
            away_ref.at[i, :, columns], sibling_ref.at[i, :, columns], away_send.at[i, k], away_recv.at[i, k], twin
        )

    def sum_rows(j):
        return pl.ds(pl.multiple_of(j * part, part), part)

    def carry_copy(owner, i, j):
        step = jnp.where(owner > z, 1, -1)
        target = jnp.where(owner == z - 1, count, owner)
        return remote(
            sum_ref.at[i, sum_rows(j)],
            carry_ref.at[target, sum_rows(j)],
            carry_send.at[i, j],
            carry_recv.at[target, j],
            at(z + step),
        )

    def out_copy(i, j):
        return remote(
            sum_ref.at[i, sum_rows(j)], out_ref.at[0, sum_rows(j)], out_send.at[j], out_recv.at[j], following
        )

    def combine(pair, i, j):
        owner = owner_of(pair, i)
        slot = slot_of(pair, i)
        spot = sum_rows(j)

        @pl.when((owner >= z) & (z > 0))
        def _():
            landed = carry_ref.at[owner, spot]
            remote(landed, landed, carry_send.at[slot, j], carry_recv.at[owner, j], twin).wait_recv()
            near_ref[slot, spot, :] += carry_ref[owner, spot, :].astype(jnp.float32)

        @pl.when((owner <= z) & (z < count - 1))
        def _():
            source = jnp.where(owner == z, count, owner)
            landed = carry_ref.at[source, spot]
            remote(landed, landed, carry_send.at[slot, j], carry_recv.at[source, j], twin).wait_recv()
            near_ref[slot, spot, :] += carry_ref[source, spot, :].astype(jnp.float32)

        value = near_ref[slot, spot, :] + sibling_ref[slot, spot, :].astype(jnp.float32)

        @pl.when(pair > 1)
        def _():
            wait_sum_send(pair - 2, i, j)

        @pl.when(owner != z)
        def _():
            sum_ref[slot, spot, :] = value.astype(jnp.bfloat16)
            carry_copy(owner, slot, j).start()

        @pl.when(owner == z)
        def _():
            sum_ref[slot, spot, :] = (value + residual_ref[spot, :].astype(jnp.float32)).astype(jnp.bfloat16)
            out_copy(slot, j).start()

    def wait_sum_send(pair, i, j):
        owner = owner_of(pair, i)
        slot = slot_of(pair, i)

        @pl.when(owner != z)
        def _():
            carry_copy(owner, slot, j).wait_send()

        @pl.when(owner == z)
        def _():
            out_copy(slot, j).wait_send()

    def first_of_line(owner):
        return ((z == 0) & (owner > z)) | ((z == count - 1) & (owner < z))

    def give_credit(pair, i):
        if pairs > 2:

            @pl.when(pair < pairs - 2)
            def _():
                pl.semaphore_signal(credit.at[slot_of(pair, i)], inc=1, device_id=twin, device_id_type=MESH)

    def relay_early(step, begin, end):
        if tight:
            return
        pair = step - first_pair - 1

        @pl.when((pair >= 0) & (z > 0) & (z < count - 1))
        def _():
            owner = owner_of(pair, 0)

            @pl.when(owner != z)
            def _():
                start_line(pair, 0, begin, end)

    def finish_pair(pair, ends, begin=0, end=SUM_PIECES, served=0):
        def mine(i):
            owner = owner_of(pair, i)
            if ends:
                return owner == z
            return (owner != z) & jnp.logical_not(first_of_line(owner))

        def one_part(j, _):
            @pl.when((j >= served) & (j < end) & mine(0))
            def _():
                combine(pair, 0, j)

            @pl.when((j >= begin + skew) & mine(1))
            def _():
                combine(pair, 1, j - skew)

            return 0

        skew = 0 if ends else SKEW
        lax.fori_loop(begin, end + skew, one_part, 0)
        if end == SUM_PIECES:
            for i in range(2):

                @pl.when(mine(i))
                def _():
                    give_credit(pair, i)

    def start_line(pair, i, begin, end):
        def one_part(j, _):
            combine(pair, i, j)
            return 0

        lax.fori_loop(begin, end, one_part, 0)

    def project_turn(turn):
        def one_turn(turn, _):
            pair, i = turn // 2, lax.rem(turn, 2)
            owner = owner_of(pair, i)
            slot = slot_of(pair, i)

            def one_wait(distance, _):
                other = lax.rem(z + distance, count)
                spot = lse_ref.at[other, owner]
                remote(spot, spot, lse_send.at[0, owner], lse_recv.at[other, owner], twin).wait_recv()
                return 0

            lax.fori_loop(1, count, one_wait, 0)

            @pl.when((pair == 0) & (i == 0))
            def _():
                for k in range(tiles):
                    load_output_tile(k).wait()

                load_residual.wait()

            for b in range(blocks):
                spot = slice(b * block_rows, (b + 1) * block_rows)
                terms = [lse_ref[k, owner, b] for k in range(count)]
                top = functools.reduce(jnp.maximum, terms)
                total = sum(jnp.exp2(term - top) for term in terms)
                share = jnp.exp2(top_ref[owner, b] - top) / total
                share = jnp.concatenate([share, jnp.zeros((128 - heads_local, block_rows), jnp.float32)], axis=0).T
                share = jnp.concatenate(
                    [
                        jnp.broadcast_to(share[:, head : head + 1], (block_rows, head_size))
                        for head in range(heads_local)
                    ],
                    axis=1,
                )
                normed_ref[spot, :] = (acc_ref[owner, spot, :].astype(jnp.float32) * share).astype(jnp.bfloat16)

            if pairs > 2:

                @pl.when(pair > 1)
                def _():
                    for k in range(tiles // 2):
                        away_copy(slot, k).wait_send()
                    pl.semaphore_wait(credit.at[slot], 1)

            per_half = tiles // 2
            for k in range(per_half):
                away_ref[slot, :, k * tile : (k + 1) * tile] = jnp.dot(
                    normed_ref[...], output_tiles[k], preferred_element_type=jnp.float32
                ).astype(jnp.bfloat16)
                away_copy(slot, k).start()
            for k in range(per_half):
                near_ref[slot, :, k * tile : (k + 1) * tile] = jnp.dot(
                    normed_ref[...], output_tiles[per_half + k], preferred_element_type=jnp.float32
                )
            for k in range(per_half):
                away_copy(slot, k).wait_recv()

            whole = (i == 0) | (pair == pairs - 1)

            parted = jnp.logical_not(tight) & (i == 0) & (pair < pairs - 1)

            @pl.when(first_of_line(owner))
            def _():
                start_line(
                    pair, i, 0, jnp.where(parted, FIRST_PIECES, jnp.where(whole, SUM_PIECES, EARLY_PIECES))
                )

                @pl.when(whole & jnp.logical_not(parted))
                def _():
                    give_credit(pair, i)

            @pl.when((i == 0) & (pair > 0) & first_of_line(owner_of(pair - 1, 1)))
            def _():
                start_line(pair - 1, 1, EARLY_PIECES, SUM_PIECES)
                give_credit(pair - 1, 1)

            return 0

        lax.fori_loop(turn, turn + 1, one_turn, 0)

    def one_step(step, _):
        if tight:

            @pl.when(step < count)
            def _():
                attention_step(step)
        else:
            attention_step(step)

        def one_turn(turn, _):
            pair = turn // 2

            @pl.when((turn >= 0) & (turn < count))
            def _():
                project_turn(turn)

            @pl.when((lax.rem(turn + 2, 2) == 1) & (turn > 0) & (turn < count - 1))
            def _():
                relay_early(step, RELAYS[2], RELAYS[3])

            @pl.when((lax.rem(turn + 2, 2) == 0) & (turn > 0) & (turn < count))
            def _():
                finish_pair(pair - 1, False, served=0 if tight else RELAYS[3])

            if pairs > 2:

                @pl.when((lax.rem(turn + 2, 2) == 1) & (pair > 0) & (turn < count - 1))
                def _():
                    finish_pair(pair - 1, True)

            return 0

        begin = 2 * (step - first_pair) - 1
        end = jnp.where(step == first_pair + pairs - 1, count, begin + 2)
        lax.fori_loop(jnp.where(step >= first_pair, begin, 0), jnp.where(step >= first_pair, end, 0), one_turn, 0)

        @pl.when(step < count - 1)
        def _():
            for j in range(min(ROW_PIECES, blocks) - 1, ROW_PIECES):
                serve(step + 1, j)

        return 0

    lax.fori_loop(0, first_pair + pairs, one_step, 0)
    if pairs > 1:
        finish_pair(pairs - 2, True, 0, EARLY_PIECES)
    finish_pair(pairs - 1, False)
    if pairs > 1:
        finish_pair(pairs - 2, True, EARLY_PIECES, SUM_PIECES)
    finish_pair(pairs - 1, True)

    for pair in range(max(pairs - 2, 0), pairs):
        for i in range(2):
            for k in range(tiles // 2):
                away_copy(slot_of(pair, i), k).wait_send()

            def one_part(j, _):
                wait_sum_send(pair, i, j)
                return 0

            lax.fori_loop(0, SUM_PIECES, one_part, 0)
    for j in range(ROW_PIECES):

        @pl.when(z > 0)
        def _():
            own_copy(-1, j).wait_send()

        @pl.when(z < count - 1)
        def _():
            own_copy(1, j).wait_send()

    def one_owner(owner, _):
        if not tight:

            @pl.when(owner != z)
            def _():
                wait_row_sends(owner)

        def one_send(distance, _):
            lse_copy(owner, distance).wait_send()
            return 0

        lax.fori_loop(1, count, one_send, 0)
        return 0

    lax.fori_loop(0, count, one_owner, 0)
    for j in range(SUM_PIECES):
        out_copy(0, j).wait_recv()


def run_section(dims, hidden, norm_gain, w_query, query_gain, w_output, key_cache, value_cache, *small):
    count, sections, kv_local = dims
    rows, width = hidden.shape[1:]
    depth, columns = w_query.shape[1:]
    head_size = query_gain.shape[1]
    heads_local = columns // head_size
    all_blocks = small[0].shape[0]
    blocks = all_blocks // count
    block_rows = rows // blocks
    half_width = width // 2
    tile = min(512, half_width, columns)
    tiles = columns // tile
    bf16, f32 = jnp.bfloat16, jnp.float32
    fixed = 2 * (w_query.size + key_cache.size + value_cache.size) + 28 * rows * width
    tight = fixed + 2 * w_output.size + 5 * count * rows * width > 50 * 2**20
    anywhere = pl.BlockSpec(memory_space=pl.ANY)
    stored = pl.BlockSpec(memory_space=pltpu.HBM)
    held = pl.BlockSpec(memory_space=pltpu.VMEM)
    dma = pltpu.SemaphoreType.DMA
    scratch = [
        pltpu.VMEM((count, rows, width), bf16),
        pltpu.VMEM((tiles, depth, tile), bf16),
        pltpu.VMEM(key_cache.shape[1:], bf16),
        pltpu.VMEM(value_cache.shape[1:], bf16),
        pltpu.VMEM((rows, width), bf16),
        pltpu.VMEM((blocks, heads_local, block_rows, head_size), bf16),
        pltpu.VMEM((count, count, blocks, heads_local, block_rows), f32),
        pltpu.VMEM((count, blocks, heads_local, block_rows), f32),
        pltpu.VMEM((rows, half_width), bf16),
        pltpu.VMEM((4, rows, half_width), f32),
        pltpu.VMEM((4, rows, half_width), bf16),
        pltpu.VMEM((4, rows, half_width), bf16),
        pltpu.VMEM((count + 1, rows, half_width), bf16),
        pltpu.VMEM((4, rows, half_width), bf16),
        dma((4,)),
        dma((2, tiles)),
        dma((count, 2, ROW_PIECES)),
        dma((2, ROW_PIECES)),
        dma((count, ROW_PIECES)),
        dma((count, ROW_PIECES)),
        dma((count - 1, count)),
        dma((count, count)),
        dma((4, tiles // 2)),
        dma((4, tiles // 2)),
        dma((4, SUM_PIECES)),
        dma((count + 1, SUM_PIECES)),
        dma((SUM_PIECES,)),
        dma((SUM_PIECES,)),
        pltpu.SemaphoreType.REGULAR((4,)),
    ]
    if not tight:
        scratch += [
            pltpu.VMEM((count, rows, heads_local * head_size), bf16),
            pltpu.VMEM((tiles, heads_local * head_size, tile), bf16),
        ]
    return pl.pallas_call(
        functools.partial(section_kernel, (count, sections, kv_local, tight)),
        out_shape=jax.ShapeDtypeStruct((1, rows, half_width), bf16),
        in_specs=[
            stored,
            held,
            stored,
            held,
            stored,
            stored,
            stored,
            *[pl.BlockSpec(memory_space=pltpu.SMEM)] * len(small),
        ],
        out_specs=anywhere,
        scratch_shapes=scratch,
        compiler_params=pltpu.CompilerParams(
            collective_id=0, has_side_effects=True, vmem_limit_bytes=63 * 2**20
        ),
        name="section",
    )(hidden, norm_gain, w_query, query_gain, w_output, key_cache, value_cache, *small)


def body(
    hidden,
    norm_gain,
    w_query,
    query_gain,
    w_output,
    key_cache,
    value_cache,
    key_scale,
    value_scale,
    page_table,
    page_tokens,
    page_list,
    list_len,
):
    kv_local = key_scale.shape[2]
    count = lax.axis_size("cache")
    sections = lax.axis_size("sections")
    places = plan(page_table, page_tokens, page_list[0], list_len[0])
    return run_section(
        (count, sections, kv_local),
        hidden,
        norm_gain,
        w_query,
        query_gain,
        w_output,
        key_cache,
        value_cache,
        places,
        key_scale[0].T,
        value_scale[0].T,
    )


def solution(mesh):
    return jax.shard_map(
        body,
        mesh=mesh,
        in_specs=(
            P("sections", "cache", None),
            P("sections", None),
            P("sections", None, "heads"),
            P("sections", None),
            P("sections", "heads", None),
            P("sections", "cache", None, "heads"),
            P("sections", "cache", None, "heads"),
            P("sections", "cache", "heads"),
            P("sections", "cache", "heads"),
            P(),
            P(),
            P("sections", None, None),
            P("sections", None),
        ),
        out_specs=P("sections", "cache", "heads"),
        check_vma=False,
    )
```
